32 devices in a mesh: comp: 2 (over x), tile: 16 (over z, y, core).
Axes of the slice: x: 2, y: 2, z: 4, core: 2. Of those that a mesh axis runs over, the one named last changes fastest.
Arguments:
- ocean_fields: float32 [2, 6, 64, 2048], P('comp', None, None, 'tile'), may hold values from -6 to 6, as said below
- tracers: float32 [19, 64, 2048], P(None, None, 'tile'), may hold values from -6 to 6
- reaction: float32 [19, 19], replicated, may hold values from -1.25 to 1.25
- wet_levels: int32 [2048], P('tile'), may hold values from 0 to 64, as said below
- neighbours: int32 [3, 2048], P(None, 'tile'), may hold values from 0 to 383, as said below
Outputs:
- ocean_out: float32 [2, 6, 64, 2048], P('comp', None, None, 'tile')
- chl_out: float32 [2, 64, 2048], P('comp', None, 'tile')
The draws below stay inside these ranges and needn't reach their ends.
Inputs may be any that keep to these rules, and one draw needn't show every extreme that they name: `ocean_fields`: along the second dimension: temperature, salinity, eastward and northward velocity, a mixing index, and the shortwave flux, which lies between 0.2 and 2. `wet_levels`: 0 marks land; the share of land differs from tile to tile. `neighbours`: entry [k, c] gives the k-th neighbour of column c as a position in its tile's columns extended by 128 columns of each adjacent tile on both sides, the tiles closing into a loop: position p is the tile's column p - 128; no column is its own neighbour.
All inputs are finite; a program needn't handle non-finite values.
Results may differ from the reference program's by a relative error of at most 0.000061.
Values sent between devices are 32-bit elements; how exact they have to be, the bound alone decides.
No kernel may reach another device: no remote copies, remote signals or barrier semaphores. Data moves between devices by JAX's collectives and lax.ppermute only.
A program may use at most 64 MiB of HBM per device.

```python
import math
import jax
import jax.numpy as jnp
from jax import lax

NT = 19
NF = 6
LEV = 64
RIM = 128
COL_DEV = 128
COLS = 2048


def draw_ocean_fields(key, part):
    base_key = jax.random.fold_in(key, 11)
    first_key, second_key = jax.random.split(base_key, 2)
    values = jnp.clip(jax.random.normal(first_key, (2, NF - 1, LEV, COLS), jnp.float32), -6.0, 6.0)
    sunlight_input = jnp.exp(jax.random.uniform(second_key, (2, 1, LEV, COLS), jnp.float32, math.log(0.2), math.log(2.0)))
    return jnp.concatenate([values, sunlight_input], axis=1).astype(jnp.float32)


def draw_tracers(key, part):
    base_key = jax.random.fold_in(key, 53)
    first_key, second_key = jax.random.split(base_key, 2)
    chlorophyll = jax.random.uniform(second_key, (1, LEV, COLS), jnp.float32, -6.0, -3.0)
    others = jnp.clip(jax.random.normal(first_key, (NT - 1, LEV, COLS), jnp.float32), -6.0, 6.0)
    return jnp.concatenate([chlorophyll, others], axis=0).astype(jnp.float32)


def draw_wet_levels(key, part):
    base_key = jax.random.fold_in(key, 23)
    first_key, second_key, third_key = jax.random.split(base_key, 3)
    tile_count = COLS // COL_DEV
    land_share = jax.random.randint(first_key, (tile_count,), 0, 8)
    column = jnp.arange(COLS, dtype=jnp.int32)
    position = column % COL_DEV
    on_land = jax.random.randint(second_key, (COLS,), 0, 8) < land_share[column // COL_DEV]
    levels = jax.random.randint(third_key, (COLS,), 1, LEV + 1)
    levels = jnp.where(on_land, 0, levels)
    levels = jnp.where(position == 1, 0, levels)
    forced_wet = (position == 0) | (position == COL_DEV - 1) | (position == COL_DEV - RIM) | (position == RIM - 1)
    levels = jnp.where(forced_wet, LEV, levels)
    return levels.astype(jnp.int32)


def draw_neighbours(key, part):
    base_key = jax.random.fold_in(key, 37)
    first_key, second_key = jax.random.split(base_key, 2)
    reach = jax.random.randint(first_key, (3, COLS), 1, RIM + 1)
    side = jax.random.randint(second_key, (3, COLS), 0, 2) * 2 - 1
    position = jnp.arange(COLS, dtype=jnp.int32) % COL_DEV
    located = RIM + position[None, :] + side * reach
    row_index = jnp.arange(3, dtype=jnp.int32)[:, None]
    located = jnp.where((row_index == 0) & (position[None, :] == 0), 0, located)
    located = jnp.where((row_index == 1) & (position[None, :] == COL_DEV - 1), COL_DEV + 2 * RIM - 1, located)
    return located.astype(jnp.int32)


def block_scale(stream_key, dims, cuts, least, largest):
    level, own = 1.0, jax.random.fold_in(stream_key, 6)
    for axis_at, shards_of in cuts:
        heights = jnp.exp(jax.random.uniform(jax.random.fold_in(own, axis_at), (shards_of,), jnp.float32, least / len(cuts), largest / len(cuts)))
        level = level * jnp.repeat(heights, dims[axis_at] // shards_of).reshape([-1 if axis == axis_at else 1 for axis in range(len(dims))])
    return level


def centred(rng, shape, scale, most, kind=jnp.bfloat16):
    entries = jax.random.normal(rng, shape, jnp.float32) * scale
    return jnp.minimum(jnp.maximum(entries, -most), most).astype(kind)


def setup_inputs(seed: int = 0) -> dict:
    arg_keys = jax.random.split(jax.random.key(seed), 6)
    return {
        "ocean_fields": draw_ocean_fields(jax.random.fold_in(arg_keys[5], 71), 0),
        "tracers": draw_tracers(jax.random.fold_in(arg_keys[5], 71), 0),
        "reaction": centred(arg_keys[2], (NT, NT), NT ** -0.5, 1.25, jnp.float32),
        "wet_levels": draw_wet_levels(jax.random.fold_in(arg_keys[5], 71), 0),
        "neighbours": draw_neighbours(jax.random.fold_in(arg_keys[5], 71), 0),
    }


ROTATE_COS = math.cos(0.3)
ROTATE_SIN = math.sin(0.3)


def edge_weight(eastward, northward, face_index):
    angle = 2.0 * math.pi * face_index / 3.0
    return 0.05 + 0.25 * jax.nn.sigmoid(eastward * math.cos(angle) + northward * math.sin(angle))


def vertical_mix(state, mixing, active):
    diffusivity = 0.02 + 0.13 * jax.nn.sigmoid(mixing)
    link_weight = diffusivity[:-1] * active[:-1] * active[1:]
    link_flux = link_weight * (state[..., 1:, :] - state[..., :-1, :])
    zero_row = jnp.zeros_like(state[..., :1, :])
    upper_term = jnp.concatenate([link_flux, zero_row], axis=-2)
    lower_term = jnp.concatenate([zero_row, link_flux], axis=-2)
    return state + upper_term - lower_term


def transport(carried, active, places, weights):
    count = carried.shape[0]
    joined = jnp.concatenate([carried, active[None]], axis=0)
    change = jnp.zeros_like(carried)
    for face_index in range(3):
        remote = jnp.take(joined, places[face_index], axis=2)
        change = change + weights[face_index] * remote[count] * (remote[:count] - carried)
    return carried + active * change


def ocean_step(fields, chlorophyll, active, places):
    weights = []
    for face_index in range(3):
        face_weight = edge_weight(fields[2], fields[3], face_index)
        steady = jnp.full_like(face_weight, 0.15)
        weights.append(jnp.stack([face_weight, face_weight, steady, steady]))
    moved_state = transport(fields[:4], active, places, weights)
    rotated_east = ROTATE_COS * moved_state[2] + ROTATE_SIN * moved_state[3]
    rotated_north = -ROTATE_SIN * moved_state[2] + ROTATE_COS * moved_state[3]
    stacked = jnp.stack([moved_state[0], moved_state[1], rotated_east, rotated_north])
    stirred_condition = vertical_mix(stacked, fields[4], active)
    uppermost_layer = fields[5, 0]
    absorbed = 0.01 + 0.3 * jax.nn.softplus(chlorophyll)
    optical_depth = jnp.cumsum(absorbed, axis=0)
    bottom_light_flux = jnp.exp(-optical_depth)
    ceiling_light_flux = jnp.exp(-(optical_depth - absorbed))
    seawater_warmth = stirred_condition[0] + 4.0 * uppermost_layer * (ceiling_light_flux - bottom_light_flux)
    stratified_mass_profile = seawater_warmth - jnp.concatenate([seawater_warmth[1:], seawater_warmth[-1:]], axis=0)
    sunlight_input = uppermost_layer * ceiling_light_flux
    advance_outcome = jnp.stack([seawater_warmth, stirred_condition[1], stirred_condition[2], stirred_condition[3], stratified_mass_profile, sunlight_input])
    return advance_outcome * active


def bgc_step(tracer_state, lagged, reaction, active, places):
    weights = [edge_weight(lagged[2], lagged[3], face_index) for face_index in range(3)]
    moved_state = transport(tracer_state, active, places, weights)
    stirred_condition = vertical_mix(moved_state, lagged[4], active)
    growth_rate = 0.5 * lagged[5] * jax.nn.sigmoid(lagged[0] + 0.5 * lagged[1])
    flat_state = jnp.tanh(stirred_condition).reshape(stirred_condition.shape[0], -1)
    growth = jnp.dot(reaction, flat_state, precision=lax.Precision.HIGHEST,
                     preferred_element_type=jnp.float32).reshape(stirred_condition.shape)
    return (stirred_condition + growth_rate * growth) * active


def reference(ocean_fields, tracers, reaction, wet_levels, neighbours):
    level_index = jnp.arange(LEV, dtype=jnp.int32)
    active = (level_index[:, None] < wet_levels[None, :]).astype(jnp.float32)
    column = jnp.arange(COLS, dtype=jnp.int32)
    tile_start = (column // COL_DEV) * COL_DEV
    places = ((tile_start[None, :] + neighbours - RIM) % COLS).astype(jnp.int32)
    ocean_one = ocean_step(ocean_fields[0], tracers[0], active, places)
    tracer_one = bgc_step(tracers, ocean_fields[1], reaction, active, places)
    ocean_two = ocean_step(ocean_one, tracer_one[0], active, places)
    tracer_two = bgc_step(tracer_one, ocean_one, reaction, active, places)
    return jnp.stack([ocean_two, ocean_one]), jnp.stack([tracer_one[0], tracer_two[0]])
```

```python
import functools
import math

import jax
import jax.numpy as jnp
from jax import lax
from jax.experimental import pallas as pl
from jax.experimental.pallas import tpu as pltpu
from jax.sharding import PartitionSpec as P

ROTATE_COS = math.cos(0.3)
ROTATE_SIN = math.sin(0.3)
SUB = 8
AXES = ("comp", "tile")
ANGLES = [2.0 * math.pi * k / 3.0 for k in range(3)]


def edge_weight(eastward, northward, k):
    return 0.05 + 0.25 * jax.nn.sigmoid(
        eastward * math.cos(ANGLES[k]) + northward * math.sin(ANGLES[k])
    )


def take_lanes(block, index):
    return jnp.take_along_axis(block, index, axis=1, mode="promise_in_bounds")


class Stencil:
    def __init__(self, rows, odd, nb_ref, wet, wet_core, wet_cross):
        shape = (rows, nb_ref.shape[-1])
        cols = nb_ref.shape[-1]
        spread = lambda row: jnp.broadcast_to(row, shape)
        own, core, cross = spread(wet), spread(wet_core), spread(wet_cross)
        core_side = jnp.where(odd == 1, 0, 2)
        self.own_wet = own
        self.index, self.in_core, self.in_cross, self.wet = [], [], [], []
        for k in range(3):
            nb = spread(nb_ref[k : k + 1, :])
            side = nb // cols
            self.index.append(nb - side * cols)
            self.in_core.append(side == core_side)
            self.in_cross.append(side == 2 - core_side)
        for k in range(3):
            self.wet.append(self.pick(own, core, cross, k))

    def pick(self, own, core, cross, k):
        found = take_lanes(own, self.index[k])
        found = jnp.where(self.in_core[k], take_lanes(core, self.index[k]), found)
        return jnp.where(self.in_cross[k], take_lanes(cross, self.index[k]), found)

    def coefficients(self, level, weights):
        active = level < self.own_wet
        cs = [
            jnp.where(active & (level < self.wet[k]), weights[k], 0.0) for k in range(3)
        ]
        return cs, 1.0 - (cs[0] + cs[1] + cs[2])

    def move(self, own, core, cross, cs, rest):
        total = own * rest
        for k in range(3):
            total = total + cs[k] * self.pick(own, core, cross, k)
        return total


def links(level, own_wet, mixing, last_level):
    diffusivity = 0.02 + 0.13 * jax.nn.sigmoid(mixing)
    nxt = level + 1.0
    return jnp.where((nxt < own_wet) & (nxt <= last_level), diffusivity, 0.0)


def levels_of(rows, cols, start):
    return lax.broadcasted_iota(jnp.int32, (rows, cols), 0).astype(jnp.float32) + start


def ocean_kernel(place_ref, nb_ref, wets_ref, f_ref, core_ref, cross_ref, chl_ref, out_ref):
    @pl.when(place_ref[0] == 0)
    def _():
        lev, cols = f_ref.shape[1:]
        level = levels_of(lev, cols, 0.0)
        st = Stencil(lev, place_ref[1], nb_ref, wets_ref[0:1, :], wets_ref[1:2, :], wets_ref[2:3, :])
        active = (level < st.own_wet).astype(jnp.float32)
        ws = [edge_weight(f_ref[2], f_ref[3], k) for k in range(3)]
        cs, rest = st.coefficients(level, ws)
        c0, rest0 = st.coefficients(level, [jnp.full((lev, cols), 0.15, jnp.float32)] * 3)
        q = []
        for i in range(4):
            a, r = (cs, rest) if i < 2 else (c0, rest0)
            q.append(st.move(f_ref[i], core_ref[i], cross_ref[i], a, r))
        e = ROTATE_COS * q[2] + ROTATE_SIN * q[3]
        n = -ROTATE_SIN * q[2] + ROTATE_COS * q[3]
        link = links(level, st.own_wet, f_ref[4], lev - 1.0)

        def mix(v):
            flux = link * (pltpu.roll(v, lev - 1, 0) - v)
            return v + flux - pltpu.roll(flux, 1, 0)

        p = [mix(v) for v in (q[0], q[1], e, n)]
        top = f_ref[5, 0:1, :]
        x = chl_ref[...]
        absorbed = 0.01 + 0.3 * (jnp.maximum(x, 0.0) + jnp.log1p(jnp.exp(-jnp.abs(x))))
        row = lax.broadcasted_iota(jnp.int32, (lev, lev), 0)
        col = lax.broadcasted_iota(jnp.int32, (lev, lev), 1)
        above = jnp.dot(
            (col < row).astype(jnp.float32),
            absorbed,
            precision=lax.Precision.HIGHEST,
            preferred_element_type=jnp.float32,
        )
        ceiling = jnp.exp(-above)
        bottom = jnp.exp(-(above + absorbed))
        warm = p[0] + 4.0 * top * (ceiling - bottom)
        lower = jnp.where(level == lev - 1.0, warm, pltpu.roll(warm, lev - 1, 0))
        out_ref[0] = warm * active
        for i in range(1, 4):
            out_ref[i] = p[i] * active
        out_ref[4] = (warm - lower) * active
        out_ref[5] = top * ceiling * active


def bgc_kernel(
    second,
    place_ref,
    react_ref,
    nb_ref,
    wets_ref,
    g_ref,
    own_ref,
    core_ref,
    cross_ref,
    core_x_ref,
    cross_x_ref,
    *rest_refs,
):
    outs, (h_ref, l_ref) = rest_refs[:-2], rest_refs[-2:]
    nt, rows, cols = own_ref.shape
    main = rows - SUB
    low = place_ref[0] == 1
    base = place_ref[2].astype(jnp.float32)
    last = place_ref[3].astype(jnp.float32)
    st = Stencil(SUB, place_ref[1], nb_ref, wets_ref[0:1, :], wets_ref[1:2, :], wets_ref[2:3, :])
    zero = jnp.zeros((SUB, cols), jnp.float32)
    pads = (0, SUB + rows)
    for r in pads:
        l_ref[r : r + SUB, :] = zero
        for j in range(nt):
            h_ref[j, r : r + SUB, :] = zero

    def first_pass(r, core, cross):
        here = pl.ds(r, SUB)
        level = levels_of(SUB, cols, base + jnp.asarray(r, jnp.float32))
        ws = [edge_weight(g_ref[2, here, :], g_ref[3, here, :], k) for k in range(3)]
        cs, rest = st.coefficients(level, ws)
        there = pl.ds(r + SUB, SUB)
        l_ref[there, :] = links(level, st.own_wet, g_ref[4, here, :], last)
        for j in range(nt):
            h_ref[j, there, :] = st.move(own_ref[j, here, :], core(j), cross(j), cs, rest)

    def second_pass(r, put):
        here, there = pl.ds(r, SUB), pl.ds(r + SUB, SUB)
        after, before = pl.ds(r + SUB + 1, SUB), pl.ds(r + SUB - 1, SUB)
        level = levels_of(SUB, cols, base + jnp.asarray(r, jnp.float32))
        active = (level < st.own_wet).astype(jnp.float32)
        down, up = l_ref[there, :], l_ref[before, :]
        ys, ts = [], []
        for j in range(nt):
            v = h_ref[j, there, :]
            y = v + down * (h_ref[j, after, :] - v) - up * (v - h_ref[j, before, :])
            ys.append(y)
            ts.append(jnp.tanh(y))
        growth = 0.5 * g_ref[5, here, :] * jax.nn.sigmoid(g_ref[0, here, :] + 0.5 * g_ref[1, here, :])
        for i in range(1 if second else nt):
            total = react_ref[i, 0] * ts[0]
            for j in range(1, nt):
                total = total + react_ref[i, j] * ts[j]
            put(i, (ys[i] + growth * total) * active)

    def main_first(b, carry):
        r = pl.multiple_of(b * SUB, SUB)
        inner = pl.ds(pl.multiple_of(r - SUB, SUB), SUB)
        first_pass(r, lambda j: core_ref[j, inner, :], lambda j: cross_ref[j, inner, :])
        return carry

    def main_second(b, carry):
        r = pl.multiple_of(b * SUB, SUB)
        inner = pl.ds(pl.multiple_of(r - SUB, SUB), SUB)

        def put(i, value):
            if second:
                outs[0][pl.ds(r, SUB), :] = value
            else:
                outs[0][i, inner, :] = value

        second_pass(r, put)
        return carry

    @pl.when(low)
    def _():
        first_pass(0, lambda j: core_x_ref[j], lambda j: cross_x_ref[j])

    @pl.when(jnp.logical_not(low))
    def _():
        l_ref[SUB : 2 * SUB, :] = zero
        for j in range(nt):
            h_ref[j, SUB : 2 * SUB, :] = zero

    lax.fori_loop(1, rows // SUB, main_first, 0)
    lax.fori_loop(1, rows // SUB, main_second, 0)

    @pl.when(low)
    def _():
        def put(i, value):
            if second:
                outs[0][0:SUB, :] = value
            else:
                outs[1][i] = value

        second_pass(0, put)


VMEM = pl.BlockSpec(memory_space=pltpu.VMEM)
SMEM = pl.BlockSpec(memory_space=pltpu.SMEM)


def ocean_step(place, nb, wets, fields, core, cross, chl):
    return pl.pallas_call(
        ocean_kernel,
        out_shape=jax.ShapeDtypeStruct(fields.shape, jnp.float32),
        in_specs=[SMEM] + [VMEM] * 6,
        out_specs=VMEM,
        cost_estimate=pl.CostEstimate(flops=4_000_000, bytes_accessed=800_000, transcendentals=0),
    )(place, nb, wets, fields, core, cross, chl)


def bgc_step(second, place, reaction, nb, wets, g, own, core, cross, core_x, cross_x):
    nt, rows, cols = own.shape
    main = rows - SUB
    if second:
        out_shape = (jax.ShapeDtypeStruct((rows, cols), jnp.float32),)
    else:
        out_shape = (
            jax.ShapeDtypeStruct((nt, main, cols), jnp.float32),
            jax.ShapeDtypeStruct((nt, SUB, cols), jnp.float32),
        )
    return pl.pallas_call(
        functools.partial(bgc_kernel, second),
        out_shape=out_shape,
        in_specs=[SMEM, SMEM] + [VMEM] * 8,
        out_specs=tuple(VMEM for _ in out_shape),
        scratch_shapes=[
            pltpu.VMEM((nt, rows + 2 * SUB, cols), jnp.float32),
            pltpu.VMEM((rows + 2 * SUB, cols), jnp.float32),
        ],
        cost_estimate=pl.CostEstimate(flops=8_000_000, bytes_accessed=2_000_000, transcendentals=0),
    )(place, reaction, nb, wets, g, own, core, cross, core_x, cross_x)


def swaps(comps, tiles, across):
    pairs = []
    for c in comps:
        for t in range(tiles):
            other = (t + 1) % tiles if (t % 2 == 0) != across else (t - 1) % tiles
            pairs.append((c * tiles + t, c * tiles + other))
    return pairs


def over_comp(source, tiles):
    return [(source * tiles + t, (1 - source) * tiles + t) for t in range(tiles)]


def per_device(ocean_fields, tracers, reaction, wet_levels, neighbours):
    tiles = lax.axis_size("tile")
    comp, tile = lax.axis_index("comp"), lax.axis_index("tile")
    is_ocean = comp == 0
    nt, lev, cols = tracers.shape
    main = lev // 2
    fields = ocean_fields[0]
    both = (0, 1)
    exchange = lambda v, comps: [lax.ppermute(v, AXES, swaps(comps, tiles, a)) for a in (False, True)]

    wet_row = wet_levels.astype(jnp.float32)[None]
    place = jnp.stack([comp, tile % 2, jnp.where(is_ocean, -SUB, main - SUB), jnp.int32(lev - 1)]).astype(jnp.int32)
    start = jnp.where(is_ocean, 0, main)
    own_main = lax.dynamic_slice_in_dim(tracers, start, main, axis=1)
    own_extra = lax.slice_in_dim(tracers, main - SUB, main, axis=1)
    own = jnp.concatenate([own_extra, own_main], axis=1)
    flat = jnp.concatenate([own_main.reshape(nt * main, cols), jnp.broadcast_to(wet_row, (SUB, cols))], axis=0)
    flat_core, flat_cross = exchange(flat, both)
    ocean_core, ocean_cross = exchange(fields[:4], (0,))
    extra_core, extra_cross = exchange(own_extra, (1,))
    lagged_top = lax.ppermute(fields[:, :main], AXES, over_comp(1, tiles))

    part = lambda v: v[: nt * main].reshape(nt, main, cols)
    wets = jnp.concatenate([wet_row, flat_core[nt * main : nt * main + 1], flat_cross[nt * main : nt * main + 1]], axis=0)
    window = lambda mine, others: jnp.where(is_ocean, jnp.pad(mine, ((0, 0), (SUB, 0), (0, 0))), others[:, main - SUB :])
    g_one = window(lagged_top, fields)

    ocean_one = ocean_step(place, neighbours, wets, fields, ocean_core, ocean_cross, tracers[0])
    main_one, extra_one = bgc_step(
        False, place, reaction, neighbours, wets, g_one, own, part(flat_core), part(flat_cross), extra_core, extra_cross
    )

    main_core, main_cross = exchange(main_one, both)
    ocean_core, ocean_cross = exchange(ocean_one[:4], (0,))
    extra_core, extra_cross = exchange(extra_one, (1,))
    ocean_sent = lax.ppermute(ocean_one, AXES, over_comp(0, tiles))
    own_one = jnp.concatenate([extra_one, main_one], axis=1)
    chl_lower = lax.ppermute(own_one[0], AXES, over_comp(1, tiles))
    g_two = window(ocean_one[:, :main], ocean_sent)

    (chl_two,) = bgc_step(
        True, place, reaction, neighbours, wets, g_two, own_one, main_core, main_cross, extra_core, extra_cross
    )
    level = jnp.arange(lev, dtype=jnp.int32)[:, None]
    cut = main - SUB // 2
    chl_one = jnp.where(
        level < cut,
        jnp.pad(main_one[0], ((0, lev - main), (0, 0))),
        jnp.pad(chl_lower, ((lev - main - SUB, 0), (0, 0))),
    )
    chl_upper = lax.ppermute(chl_two[SUB:], AXES, over_comp(0, tiles))
    ocean_two = ocean_step(place, neighbours, wets, ocean_one, ocean_core, ocean_cross, chl_one)
    chl_last = jnp.where(
        level < cut,
        jnp.pad(chl_upper, ((0, lev - main), (0, 0))),
        jnp.pad(chl_two, ((lev - main - SUB, 0), (0, 0))),
    )
    ocean_out = jnp.where(is_ocean, ocean_two, ocean_sent)[None]
    chl_out = jnp.where(is_ocean, chl_one, chl_last)[None]
    return (ocean_out, chl_out)


def solution(mesh):
    return jax.shard_map(
        per_device,
        mesh=mesh,
        in_specs=(
            P("comp", None, None, "tile"),
            P(None, None, "tile"),
            P(),
            P("tile"),
            P(None, "tile"),
        ),
        out_specs=(P("comp", None, None, "tile"), P("comp", None, "tile")),
        check_vma=False,
    )
```

```python
import functools
import math

import jax
import jax.numpy as jnp
from jax import lax
from jax.experimental import pallas as pl
from jax.experimental.pallas import tpu as pltpu
from jax.sharding import PartitionSpec as P

ROTATE_COS = math.cos(0.3)
ROTATE_SIN = math.sin(0.3)
SUB = 8
AXES = ("comp", "tile")
ANGLES = [2.0 * math.pi * k / 3.0 for k in range(3)]
F32 = jnp.float32
BF16 = jnp.bfloat16


VMEM = pl.BlockSpec(memory_space=pltpu.VMEM)
SMEM = pl.BlockSpec(memory_space=pltpu.SMEM)
ANY = pl.BlockSpec(memory_space=pl.ANY)


class Plan:
    def __init__(self, nt, lev):
        self.nt, self.lev = nt, lev
        self.blocks = lev // SUB
        self.main = self.blocks // 2
        self.window = self.main + 1
        self.extra = nt * self.main
        self.wet = self.extra + max(4 * self.blocks, nt)
        self.total = self.wet + 1

    def slot(self, j, r):
        return jnp.where(r == 0, self.extra + j, j * self.main + r - 1)


def edge_weights(eastward, northward):
    return [
        0.05 + 0.25 * jax.nn.sigmoid(eastward * math.cos(a) + northward * math.sin(a)) for a in ANGLES
    ]


def take_lanes(block, index):
    return jnp.take_along_axis(block, index, axis=1, mode="promise_in_bounds")


def shape_of(*dims):
    return jax.ShapeDtypeStruct(dims, F32)


def neighbours_of(nb_ref, odd):
    cols = nb_ref.shape[-1]
    core_side = jnp.where(odd == 1, 0, 2)
    index, in_core, in_cross = [], [], []
    for k in range(3):
        nb = jnp.broadcast_to(nb_ref[k : k + 1, :], (SUB, cols))
        side = nb // cols
        index.append(nb - side * cols)
        in_core.append(side == core_side)
        in_cross.append(side == 2 - core_side)
    return index, in_core, in_cross


def level_block(block, cols):
    first = (block * SUB).astype(F32) if not isinstance(block, int) else float(block * SUB)
    return lax.broadcasted_iota(jnp.int32, (SUB, cols), 0).astype(F32) + first


def link_weight(level, wet, mixing, last):
    nxt = level + 1.0
    return jnp.where((nxt < wet) & (nxt <= last), 0.02 + 0.13 * jax.nn.sigmoid(mixing), 0.0)


def pack_kernel(plan, wet_ref, f_ref, t_ref, out_ref, chl_ref, sems):
    comp = lax.axis_index("comp")
    first = comp * plan.main
    copies = [
        (t_ref.at[j, pl.ds(first, plan.main)], out_ref.at[pl.ds(j * plan.main, plan.main)])
        for j in range(plan.nt)
    ]
    copies.append((t_ref.at[0], chl_ref))
    copies = [pltpu.make_async_copy(s, d, sems.at[i]) for i, (s, d) in enumerate(copies)]
    for c in copies:
        c.start()
    base = len(copies)
    ocean = [
        pltpu.make_async_copy(
            f_ref.at[i], out_ref.at[pl.ds(plan.extra + i * plan.blocks, plan.blocks)], sems.at[base + i]
        )
        for i in range(4)
    ]
    above = pltpu.make_async_copy(
        t_ref.at[:, plan.main - 1], out_ref.at[pl.ds(plan.extra, plan.nt)], sems.at[base + 4]
    )

    @pl.when(comp == 0)
    def _():
        for c in ocean:
            c.start()

    @pl.when(comp != 0)
    def _():
        above.start()

    out_ref[plan.wet] = jnp.broadcast_to(wet_ref[...].astype(F32), out_ref.shape[1:])
    for c in copies:
        c.wait()

    @pl.when(comp == 0)
    def _():
        for c in ocean:
            c.wait()

    @pl.when(comp != 0)
    def _():
        above.wait()


def matrix_kernel(r_ref, out_ref):
    nt = r_ref.shape[0]
    rows, n = out_ref.shape
    p = lax.broadcasted_iota(jnp.int32, (n, nt), 0)
    spread = (p // SUB == lax.broadcasted_iota(jnp.int32, (n, nt), 1)).astype(F32)
    exact = functools.partial(
        lax.dot_general, precision=lax.Precision.HIGHEST, preferred_element_type=F32
    )
    tall = exact(spread, r_ref[...], (((1,), (0,)), ((), ())))
    full = exact(tall, spread, (((1,), (1,)), ((), ())))
    a = lax.broadcasted_iota(jnp.int32, (n, n), 0)
    b = lax.broadcasted_iota(jnp.int32, (n, n), 1)
    full = jnp.where(a % SUB == b % SUB, full, 0.0)
    high = full.astype(BF16)
    out_ref[0:n, :] = high
    out_ref[n:rows, :] = (full - high.astype(F32)).astype(BF16)


def near_kernel(plan, second, nb_ref, f_ref, ga_ref, gb_ref, own_ref, core_ref, chl_ref, *refs):
    if second:
        chl_low_ref, *refs = refs
    part_ref, far_ref, aux_ref, opart_ref, ofar_ref, oaux_ref = refs[:6]
    refs = refs[6:]
    if second:
        chl_out_ref, g_ref, s_ref = refs
    else:
        g_ref, s_ref = refs
    comp, odd = lax.axis_index("comp"), lax.axis_index("tile") % 2
    cols = nb_ref.shape[-1]
    low = comp != 0
    index, in_core, in_cross = neighbours_of(nb_ref, odd)
    wet, wet_core = own_ref[plan.wet], core_ref[plan.wet]
    near_wet = []
    for k in range(3):
        found = jnp.where(in_core[k], take_lanes(wet_core, index[k]), take_lanes(wet, index[k]))
        near_wet.append(jnp.where(in_cross[k], 0.0, found))
    last = float(plan.lev - 1)

    @pl.when(low)
    def _():
        g_ref[...] = gb_ref[:, plan.main - 1 :]

    @pl.when(jnp.logical_not(low))
    def _():
        g_ref[:, 1:] = ga_ref[:, : plan.main]

    def split(level, ws):
        active = level < wet
        near = [jnp.where(active & (level < near_wet[k]), ws[k], 0.0) for k in range(3)]
        far = [jnp.where(active & in_cross[k], ws[k], 0.0) for k in range(3)]
        return near, far

    def moves(own, core, near, rest):
        totals = [o * r for o, r in zip(own, rest)]
        for k in range(3):
            for j in range(len(own)):
                v = jnp.where(in_core[k], take_lanes(core[j], index[k]), take_lanes(own[j], index[k]))
                totals[j] = totals[j] + near[j][k] * v
        return totals

    first = jnp.where(low, 0, 1)
    shift = jnp.where(low, plan.main - 1, -1)

    def body(r, carry):
        level = level_block(r + shift, cols)
        near, far = split(level, edge_weights(g_ref[2, r], g_ref[3, r]))
        rest = 1.0 - (near[0] + near[1] + near[2])
        for k in range(3):
            far_ref[k, r] = far[k]
        aux_ref[0, r] = link_weight(level, wet, g_ref[4, r], last)
        aux_ref[1, r] = 0.5 * g_ref[5, r] * jax.nn.sigmoid(g_ref[0, r] + 0.5 * g_ref[1, r])
        slots = [plan.slot(j, r) for j in range(plan.nt)]
        own = [own_ref[s] for s in slots]
        core = [core_ref[s] for s in slots]
        n = plan.nt
        for j, v in enumerate(moves(own, core, [near] * n, [rest] * n)):
            part_ref[j, r] = v
        return carry

    lax.fori_loop(first, plan.window, body, 0)

    @pl.when(jnp.logical_not(low))
    def _():
        top = f_ref[5, 0, 0:1, :]

        def chl_block(b):
            v = chl_ref[b]
            if second:
                v = jnp.where(level_block(b, cols) < float(plan.main * SUB - SUB // 2), v, chl_low_ref[0, b])
                chl_out_ref[b] = v
            return v

        run = jnp.zeros((1, cols), F32)
        for b in range(plan.blocks):
            x = chl_block(b) if not second or b >= plan.main - 1 else chl_ref[b]
            if second and b < plan.main - 1:
                chl_out_ref[b] = x
            absorbed = 0.01 + 0.3 * (jnp.maximum(x, 0.0) + jnp.log1p(jnp.exp(-jnp.abs(x))))
            s_ref[b] = absorbed
            level = level_block(b, cols)
            sub = level - float(b * SUB)
            cum = absorbed
            for d in (1, 2, 4):
                cum = cum + jnp.where(sub >= float(d), pltpu.roll(cum, d, 0), 0.0)
            depth = cum + run
            ceiling = jnp.exp(-(depth - absorbed))
            oaux_ref[1, b] = 4.0 * top * (ceiling - jnp.exp(-depth))
            oaux_ref[2, b] = jnp.where(level < wet, top * ceiling, 0.0)
            run = depth[SUB - 1 : SUB, :]

        def ocean(b, carry):
            level = level_block(b, cols)
            near, far = split(level, edge_weights(f_ref[2, b], f_ref[3, b]))
            rest = 1.0 - (near[0] + near[1] + near[2])
            flat = [jnp.where(v > 0.0, 0.15, 0.0) for v in near]
            rest_flat = 1.0 - (flat[0] + flat[1] + flat[2])
            for k in range(3):
                ofar_ref[k, b] = far[k]
            oaux_ref[0, b] = link_weight(level, wet, f_ref[4, b], last)
            own = [f_ref[i, b] for i in range(4)]
            core = [core_ref[plan.extra + i * plan.blocks + b] for i in range(4)]
            out = moves(own, core, [near, near, flat, flat], [rest, rest, rest_flat, rest_flat])
            for i in range(4):
                opart_ref[i, b] = out[i]
            return carry

        lax.fori_loop(0, plan.blocks, ocean, 0)


def far_wet(index, in_cross, wet_cross):
    return [jnp.where(in_cross[k], take_lanes(wet_cross, index[k]), 0.0) for k in range(3)]


def far_moves(parts, own, cross, far, index):
    totals = [p - o * (f[0] + f[1] + f[2]) for p, o, f in zip(parts, own, far)]
    for k in range(3):
        for j in range(len(own)):
            totals[j] = totals[j] + far[j][k] * take_lanes(cross[j], index[k])
    return totals


def bgc_far(plan, second, react_ref, nb_ref, own_ref, cross_ref, part_ref, far_ref, aux_ref, h_ref, l_ref, put):
    comp, odd = lax.axis_index("comp"), lax.axis_index("tile") % 2
    low = comp != 0
    nt, cols = plan.nt, nb_ref.shape[-1]
    index, _, in_cross = neighbours_of(nb_ref, odd)
    wet = own_ref[plan.wet]
    wets = far_wet(index, in_cross, cross_ref[plan.wet])
    first = jnp.where(low, 0, 1)
    shift = jnp.where(low, plan.main - 1, -1)
    zero = jnp.zeros((SUB, cols), F32)
    end = (plan.window + 1) * SUB
    above = pl.ds(pl.multiple_of(first * SUB, SUB), SUB)
    l_ref[above, :] = zero
    for j in range(nt):
        h_ref[j, above, :] = zero
        h_ref[j, end : end + SUB, :] = zero

    def move(r, carry):
        level = level_block(r + shift, cols)
        far = [jnp.where(level < wets[k], far_ref[k, r], 0.0) for k in range(3)]
        there = pl.ds(pl.multiple_of((r + 1) * SUB, SUB), SUB)
        l_ref[there, :] = aux_ref[0, r]
        slots = [plan.slot(j, r) for j in range(nt)]
        parts = [part_ref[j, r] for j in range(nt)]
        own = [own_ref[s] for s in slots]
        cross = [cross_ref[s] for s in slots]
        for j, v in enumerate(far_moves(parts, own, cross, [far] * nt, index)):
            h_ref[j, there, :] = v
        return carry

    def react(r, carry):
        active = (level_block(r + shift, cols) < wet).astype(F32)
        at = (r + 1) * SUB
        there, after, before = pl.ds(pl.multiple_of(at, SUB), SUB), pl.ds(at + 1, SUB), pl.ds(at - 1, SUB)
        down, up = l_ref[there, :], l_ref[before, :]
        ys, ts = [], []
        for j in range(nt):
            v = h_ref[j, there, :]
            y = v + down * (h_ref[j, after, :] - v) - up * (v - h_ref[j, before, :])
            ys.append(y)
            ts.append(jnp.tanh(y))
        growth = aux_ref[1, r]
        if second:
            total = react_ref[0, 0] * ts[0]
            for j in range(1, nt):
                total = total + react_ref[0, j] * ts[j]
            put(0, r, (ys[0] + growth * total) * active)
        else:
            n = react_ref.shape[1]
            ts += [zero] * (n // SUB - nt)
            stack = jnp.concatenate(ts, axis=0)
            high = stack.astype(BF16)
            rest = (stack - high.astype(F32)).astype(BF16)
            both = jnp.dot(react_ref[...], high, preferred_element_type=F32)
            total = both[:n] + both[n:] + jnp.dot(react_ref[0:n, :], rest, preferred_element_type=F32)
            for i in range(nt):
                put(i, r, (ys[i] + growth * total[i * SUB : (i + 1) * SUB]) * active)
        return carry

    lax.fori_loop(first, plan.window, move, 0)
    lax.fori_loop(first, plan.window, react, 0)


def ocean_far(plan, nb_ref, f_ref, own_ref, cross_ref, opart_ref, ofar_ref, oaux_ref, q_ref, l_ref, put):
    odd = lax.axis_index("tile") % 2
    cols = nb_ref.shape[-1]
    index, _, in_cross = neighbours_of(nb_ref, odd)
    wet = own_ref[plan.wet]
    wets = far_wet(index, in_cross, cross_ref[plan.wet])
    zero = jnp.zeros((SUB, cols), F32)
    end = (plan.blocks + 1) * SUB
    l_ref[0:SUB, :] = zero
    for i in range(4):
        q_ref[i, 0:SUB, :] = zero
        q_ref[i, end : end + SUB, :] = zero

    def move(b, carry):
        level = level_block(b, cols)
        far = [jnp.where(level < wets[k], ofar_ref[k, b], 0.0) for k in range(3)]
        flat = [jnp.where(v > 0.0, 0.15, 0.0) for v in far]
        there = pl.ds(pl.multiple_of((b + 1) * SUB, SUB), SUB)
        l_ref[there, :] = oaux_ref[0, b]
        parts = [opart_ref[i, b] for i in range(4)]
        own = [f_ref[i, b] for i in range(4)]
        cross = [cross_ref[plan.extra + i * plan.blocks + b] for i in range(4)]
        q = far_moves(parts, own, cross, [far, far, flat, flat], index)
        q_ref[0, there, :] = q[0]
        q_ref[1, there, :] = q[1]
        q_ref[2, there, :] = ROTATE_COS * q[2] + ROTATE_SIN * q[3]
        q_ref[3, there, :] = -ROTATE_SIN * q[2] + ROTATE_COS * q[3]
        return carry

    lax.fori_loop(0, plan.blocks, move, 0)
    warm = [None] * plan.blocks
    for b in range(plan.blocks):
        at = (b + 1) * SUB
        active = (level_block(b, cols) < wet).astype(F32)
        down, up = l_ref[at : at + SUB, :], l_ref[at - 1 : at - 1 + SUB, :]
        for i in range(4):
            v = q_ref[i, at : at + SUB, :]
            y = v + down * (q_ref[i, at + 1 : at + 1 + SUB, :] - v) - up * (v - q_ref[i, at - 1 : at - 1 + SUB, :])
            if i == 0:
                warm[b] = y + oaux_ref[1, b]
                put(0, b, warm[b] * active)
            else:
                put(i, b, y * active)
        put(5, b, oaux_ref[2, b])
    sub = lax.broadcasted_iota(jnp.int32, (SUB, cols), 0)
    for b in range(plan.blocks):
        active = (level_block(b, cols) < wet).astype(F32)
        nxt = warm[b + 1] if b + 1 < plan.blocks else None
        lower = pltpu.roll(warm[b], SUB - 1, 0)
        if nxt is None:
            lower = jnp.where(sub == SUB - 1, warm[b], lower)
        else:
            lower = jnp.where(sub == SUB - 1, pltpu.roll(nxt, SUB - 1, 0), lower)
        put(4, b, (warm[b] - lower) * active)


def first_far_kernel(
    plan, react_ref, nb_ref, f_ref, own_ref, cross_ref, part_ref, far_ref, aux_ref, opart_ref, ofar_ref, oaux_ref,
    out_ref, over_ref, h_ref, l_ref, q_ref, ql_ref,
):
    comp = lax.axis_index("comp")
    out_ref[plan.wet] = own_ref[plan.wet]

    @pl.when(comp == 0)
    def _():
        def put(i, b, value):
            over_ref[i, b] = value
            if i < 4:
                out_ref[plan.extra + i * plan.blocks + b] = value

        ocean_far(plan, nb_ref, f_ref, own_ref, cross_ref, opart_ref, ofar_ref, oaux_ref, q_ref, ql_ref, put)

    def put(i, r, value):
        out_ref[plan.slot(i, r)] = value

    bgc_far(plan, False, react_ref, nb_ref, own_ref, cross_ref, part_ref, far_ref, aux_ref, h_ref, l_ref, put)

    @pl.when(comp != 0)
    def _():
        over_ref[0, plan.main - 1] = out_ref[plan.extra]
        over_ref[0, plan.main :] = out_ref[0 : plan.main]


def second_bgc_kernel(
    plan, react_ref, nb_ref, own_ref, cross_ref, part_ref, far_ref, aux_ref, out_ref, h_ref, l_ref
):
    def put(i, r, value):
        out_ref[r] = value

    bgc_far(plan, True, react_ref, nb_ref, own_ref, cross_ref, part_ref, far_ref, aux_ref, h_ref, l_ref, put)


def second_ocean_kernel(
    plan, nb_ref, f_ref, over_ref, own_ref, cross_ref, opart_ref, ofar_ref, oaux_ref, out_ref, q_ref, ql_ref
):
    comp = lax.axis_index("comp")

    @pl.when(comp == 0)
    def _():
        def put(i, b, value):
            out_ref[i, b] = value

        ocean_far(plan, nb_ref, f_ref, own_ref, cross_ref, opart_ref, ofar_ref, oaux_ref, q_ref, ql_ref, put)

    @pl.when(comp != 0)
    def _():
        out_ref[...] = over_ref[...]


def last_kernel(plan, chl_ref, mine_ref, upper_ref, out_ref):
    comp = lax.axis_index("comp")
    cut = SUB // 2

    @pl.when(comp == 0)
    def _():
        out_ref[...] = chl_ref[...]

    @pl.when(comp != 0)
    def _():
        out_ref[: plan.main - 1] = upper_ref[1 : plan.main]
        sub = lax.broadcasted_iota(jnp.int32, mine_ref.shape[1:], 0)
        out_ref[plan.main - 1] = jnp.where(sub < cut, upper_ref[plan.main], mine_ref[0])
        out_ref[plan.main :] = mine_ref[1:]


def call(kernel, outs, ins, specs=None, scratch=(), cost=1_000_000):
    return pl.pallas_call(
        kernel,
        out_shape=outs,
        in_specs=specs or [VMEM] * len(ins),
        out_specs=jax.tree.map(lambda _: VMEM, outs),
        scratch_shapes=list(scratch),
        cost_estimate=pl.CostEstimate(flops=cost, bytes_accessed=1_000_000, transcendentals=0),
    )(*ins)


def swaps(tiles, across):
    pairs = []
    for c in (0, 1):
        for t in range(tiles):
            other = (t + 1) % tiles if (t % 2 == 0) != across else (t - 1) % tiles
            pairs.append((c * tiles + t, c * tiles + other))
    return pairs


def over_comp(sources, tiles):
    return [(c * tiles + t, (1 - c) * tiles + t) for c in sources for t in range(tiles)]


def per_device(ocean_fields, tracers, reaction, wet_levels, neighbours):
    tiles = lax.axis_size("tile")
    nt, lev, cols = tracers.shape
    plan = Plan(nt, lev)
    blocks, window = plan.blocks, plan.window
    fields = ocean_fields.reshape(-1, blocks, SUB, cols)
    nf = fields.shape[0]
    sent = lambda v, pairs: lax.ppermute(v, AXES, pairs)

    near_shapes = (
        shape_of(nt, window, SUB, cols),
        shape_of(3, window, SUB, cols),
        shape_of(2, window, SUB, cols),
        shape_of(4, blocks, SUB, cols),
        shape_of(3, blocks, SUB, cols),
        shape_of(3, blocks, SUB, cols),
    )
    near_scratch = (pltpu.VMEM((nf, window, SUB, cols), F32), pltpu.VMEM((blocks, SUB, cols), F32))
    h_scratch = (pltpu.VMEM((nt, (window + 2) * SUB, cols), F32), pltpu.VMEM(((window + 2) * SUB, cols), F32))
    q_scratch = (pltpu.VMEM((4, (blocks + 2) * SUB, cols), F32), pltpu.VMEM(((blocks + 2) * SUB, cols), F32))

    out_zero, chl_zero = call(
        functools.partial(pack_kernel, plan),
        (shape_of(plan.total, SUB, cols), shape_of(blocks, SUB, cols)),
        (wet_levels.reshape(1, cols), fields, tracers.reshape(nt, blocks, SUB, cols)),
        specs=[VMEM, ANY, ANY],
        scratch=[pltpu.SemaphoreType.DMA((nt + 6,))],
    )
    cross = sent(out_zero, swaps(tiles, True))
    core = sent(out_zero, swaps(tiles, False))
    lagged = sent(fields, over_comp((1,), tiles))
    n = -(-nt // 2) * 2 * SUB
    matrix = call(matrix_kernel, jax.ShapeDtypeStruct((2 * n, n), BF16), (reaction,))

    near = call(
        functools.partial(near_kernel, plan, False),
        near_shapes,
        (neighbours, fields, lagged, fields, out_zero, core, chl_zero),
        scratch=near_scratch,
        cost=8_000_000,
    )
    out_one, over_one = call(
        functools.partial(first_far_kernel, plan),
        (shape_of(plan.total, SUB, cols), shape_of(nf, blocks, SUB, cols)),
        (matrix, neighbours, fields, out_zero, cross, *near),
        scratch=h_scratch + q_scratch,
        cost=8_000_000,
    )

    cross = sent(out_one, swaps(tiles, True))
    core = sent(out_one, swaps(tiles, False))
    over = sent(over_one, over_comp((0, 1), tiles))
    *near, chl_one = call(
        functools.partial(near_kernel, plan, True),
        near_shapes + (shape_of(blocks, SUB, cols),),
        (neighbours, over_one, over_one, over, out_one, core, out_one, over),
        scratch=near_scratch,
        cost=8_000_000,
    )
    chl_two = call(
        functools.partial(second_bgc_kernel, plan),
        shape_of(window, SUB, cols),
        (reaction, neighbours, out_one, cross, *near[:3]),
        specs=[SMEM] + [VMEM] * 6,
        scratch=h_scratch,
        cost=8_000_000,
    )
    upper = sent(chl_two, over_comp((0,), tiles))
    ocean_out = call(
        functools.partial(second_ocean_kernel, plan),
        shape_of(nf, blocks, SUB, cols),
        (neighbours, over_one, over, out_one, cross, *near[3:]),
        scratch=q_scratch,
        cost=4_000_000,
    )
    chl_out = call(
        functools.partial(last_kernel, plan), shape_of(blocks, SUB, cols), (chl_one, chl_two, upper)
    )
    return (ocean_out.reshape(1, nf, lev, cols), chl_out.reshape(1, lev, cols))


def solution(mesh):
    return jax.shard_map(
        per_device,
        mesh=mesh,
        in_specs=(
            P("comp", None, None, "tile"),
            P(None, None, "tile"),
            P(),
            P("tile"),
            P(None, "tile"),
        ),
        out_specs=(P("comp", None, None, "tile"), P("comp", None, "tile")),
        check_vma=False,
    )
```

```python
import functools
import math

import jax
import jax.numpy as jnp
from jax import lax
from jax.experimental import pallas as pl
from jax.experimental.pallas import tpu as pltpu
from jax.sharding import PartitionSpec as P

ROTATE_COS = math.cos(0.3)
ROTATE_SIN = math.sin(0.3)
SUB = 8
AXES = ("comp", "tile")
ANGLES = [2.0 * math.pi * k / 3.0 for k in range(3)]
F32 = jnp.float32
BF16 = jnp.bfloat16
GRANT = 8 << 20


VMEM = pl.BlockSpec(memory_space=pltpu.VMEM)
SMEM = pl.BlockSpec(memory_space=pltpu.SMEM)
HBM = pl.BlockSpec(memory_space=pltpu.HBM)


class Plan:
    def __init__(self, nt, lev):
        self.nt, self.lev = nt, lev
        self.blocks = lev // SUB
        self.main = self.blocks // 2
        self.window = self.main + 1
        self.extra = nt * self.main
        self.wet = self.extra + max(4 * self.blocks, nt)
        self.total = self.wet + 1

    def slot(self, j, r):
        return jnp.where(r == 0, self.extra + j, j * self.main + r - 1)


def edge_weights(eastward, northward):
    return [
        0.05 + 0.25 * jax.nn.sigmoid(eastward * math.cos(a) + northward * math.sin(a)) for a in ANGLES
    ]


def take_lanes(block, index):
    return jnp.take_along_axis(block, index, axis=1, mode="promise_in_bounds")


def shape_of(*dims):
    return jax.ShapeDtypeStruct(dims, F32)


def neighbours_of(nb_ref, odd):
    cols = nb_ref.shape[-1]
    core_side = jnp.where(odd == 1, 0, 2)
    index, in_core, in_cross = [], [], []
    for k in range(3):
        nb = jnp.broadcast_to(nb_ref[k : k + 1, :], (SUB, cols))
        side = nb // cols
        index.append(nb - side * cols)
        in_core.append(side == core_side)
        in_cross.append(side == 2 - core_side)
    return index, in_core, in_cross


def level_block(block, cols):
    first = (block * SUB).astype(F32) if not isinstance(block, int) else float(block * SUB)
    return lax.broadcasted_iota(jnp.int32, (SUB, cols), 0).astype(F32) + first


def link_weight(level, wet, mixing, last):
    nxt = level + 1.0
    return jnp.where((nxt < wet) & (nxt <= last), 0.02 + 0.13 * jax.nn.sigmoid(mixing), 0.0)


def pack_kernel(plan, wet_ref, f_ref, t_ref, out_ref, top_ref, chl_ref, wet_buf, sems):
    comp = lax.axis_index("comp")
    first = comp * plan.main
    copies = [(wet_ref, wet_buf)]
    copies += [
        (t_ref.at[j, pl.ds(first, plan.main)], out_ref.at[pl.ds(j * plan.main, plan.main)])
        for j in range(plan.nt)
    ]
    copies.append((t_ref.at[0], chl_ref))
    copies.append((f_ref.at[:, pl.ds(0, plan.main)], top_ref))
    copies = [pltpu.make_async_copy(s, d, sems.at[i]) for i, (s, d) in enumerate(copies)]
    for c in copies:
        c.start()
    base = len(copies)
    ocean = [
        pltpu.make_async_copy(
            f_ref.at[i], out_ref.at[pl.ds(plan.extra + i * plan.blocks, plan.blocks)], sems.at[base + i]
        )
        for i in range(4)
    ]
    above = pltpu.make_async_copy(
        t_ref.at[:, plan.main - 1], out_ref.at[pl.ds(plan.extra, plan.nt)], sems.at[base + 4]
    )

    @pl.when(comp == 0)
    def _():
        for c in ocean:
            c.start()

    @pl.when(comp != 0)
    def _():
        above.start()

    copies[0].wait()
    out_ref[plan.wet] = jnp.broadcast_to(wet_buf[...].astype(F32), out_ref.shape[1:])
    for c in copies[1:]:
        c.wait()

    @pl.when(comp == 0)
    def _():
        for c in ocean:
            c.wait()

    @pl.when(comp != 0)
    def _():
        above.wait()


def matrix_kernel(r_ref, out_ref):
    nt = r_ref.shape[0]
    rows, n = out_ref.shape
    p = lax.broadcasted_iota(jnp.int32, (n, nt), 0)
    spread = (p // SUB == lax.broadcasted_iota(jnp.int32, (n, nt), 1)).astype(F32)
    exact = functools.partial(
        lax.dot_general, precision=lax.Precision.HIGHEST, preferred_element_type=F32
    )
    tall = exact(spread, r_ref[...], (((1,), (0,)), ((), ())))
    full = exact(tall, spread, (((1,), (1,)), ((), ())))
    a = lax.broadcasted_iota(jnp.int32, (n, n), 0)
    b = lax.broadcasted_iota(jnp.int32, (n, n), 1)
    full = jnp.where(a % SUB == b % SUB, full, 0.0)
    high = full.astype(BF16)
    out_ref[0:n, :] = high
    out_ref[n:rows, :] = (full - high.astype(F32)).astype(BF16)


def near_kernel(plan, second, nb_ref, f_ref, ga_ref, gb_ref, own_ref, core_ref, chl_ref, *refs):
    if second:
        chl_low_ref, *refs = refs
    part_ref, far_ref, aux_ref, opart_ref, ofar_ref, oaux_ref = refs[:6]
    refs = refs[6:]
    if second:
        chl_out_ref, g_ref, s_ref = refs
    else:
        g_ref, s_ref = refs
    comp, odd = lax.axis_index("comp"), lax.axis_index("tile") % 2
    cols = nb_ref.shape[-1]
    low = comp != 0
    index, in_core, in_cross = neighbours_of(nb_ref, odd)
    wet, wet_core = own_ref[plan.wet], core_ref[plan.wet]
    near_wet = []
    for k in range(3):
        found = jnp.where(in_core[k], take_lanes(wet_core, index[k]), take_lanes(wet, index[k]))
        near_wet.append(jnp.where(in_cross[k], 0.0, found))
    last = float(plan.lev - 1)

    @pl.when(low)
    def _():
        g_ref[...] = gb_ref[:, plan.main - 1 :]

    @pl.when(jnp.logical_not(low))
    def _():
        g_ref[:, 1:] = ga_ref[:, : plan.main]

    def split(level, ws):
        active = level < wet
        near = [jnp.where(active & (level < near_wet[k]), ws[k], 0.0) for k in range(3)]
        far = [jnp.where(active & in_cross[k], ws[k], 0.0) for k in range(3)]
        return near, far

    def moves(own, core, near, rest):
        totals = [o * r for o, r in zip(own, rest)]
        for k in range(3):
            for j in range(len(own)):
                v = jnp.where(in_core[k], take_lanes(core[j], index[k]), take_lanes(own[j], index[k]))
                totals[j] = totals[j] + near[j][k] * v
        return totals

    first = jnp.where(low, 0, 1)
    shift = jnp.where(low, plan.main - 1, -1)

    def body(r, carry):
        level = level_block(r + shift, cols)
        near, far = split(level, edge_weights(g_ref[2, r], g_ref[3, r]))
        rest = 1.0 - (near[0] + near[1] + near[2])
        for k in range(3):
            far_ref[k, r] = far[k]
        aux_ref[0, r] = link_weight(level, wet, g_ref[4, r], last)
        aux_ref[1, r] = 0.5 * g_ref[5, r] * jax.nn.sigmoid(g_ref[0, r] + 0.5 * g_ref[1, r])
        slots = [plan.slot(j, r) for j in range(plan.nt)]
        own = [own_ref[s] for s in slots]
        core = [core_ref[s] for s in slots]
        n = plan.nt
        for j, v in enumerate(moves(own, core, [near] * n, [rest] * n)):
            part_ref[j, r] = v
        return carry

    lax.fori_loop(first, plan.window, body, 0)

    @pl.when(jnp.logical_not(low))
    def _():
        top = f_ref[5, 0, 0:1, :]

        def chl_block(b):
            v = chl_ref[b]
            if second:
                v = jnp.where(level_block(b, cols) < float(plan.main * SUB - SUB // 2), v, chl_low_ref[0, b])
                chl_out_ref[b] = v
            return v

        run = jnp.zeros((1, cols), F32)
        for b in range(plan.blocks):
            x = chl_block(b) if not second or b >= plan.main - 1 else chl_ref[b]
            if second and b < plan.main - 1:
                chl_out_ref[b] = x
            absorbed = 0.01 + 0.3 * (jnp.maximum(x, 0.0) + jnp.log1p(jnp.exp(-jnp.abs(x))))
            s_ref[b] = absorbed
            level = level_block(b, cols)
            sub = level - float(b * SUB)
            cum = absorbed
            for d in (1, 2, 4):
                cum = cum + jnp.where(sub >= float(d), pltpu.roll(cum, d, 0), 0.0)
            depth = cum + run
            ceiling = jnp.exp(-(depth - absorbed))
            oaux_ref[1, b] = 4.0 * top * (ceiling - jnp.exp(-depth))
            oaux_ref[2, b] = jnp.where(level < wet, top * ceiling, 0.0)
            run = depth[SUB - 1 : SUB, :]

        def ocean(b, carry):
            level = level_block(b, cols)
            near, far = split(level, edge_weights(f_ref[2, b], f_ref[3, b]))
            rest = 1.0 - (near[0] + near[1] + near[2])
            flat = [jnp.where(v > 0.0, 0.15, 0.0) for v in near]
            rest_flat = 1.0 - (flat[0] + flat[1] + flat[2])
            for k in range(3):
                ofar_ref[k, b] = far[k]
            oaux_ref[0, b] = link_weight(level, wet, f_ref[4, b], last)
            own = [f_ref[i, b] for i in range(4)]
            core = [core_ref[plan.extra + i * plan.blocks + b] for i in range(4)]
            out = moves(own, core, [near, near, flat, flat], [rest, rest, rest_flat, rest_flat])
            for i in range(4):
                opart_ref[i, b] = out[i]
            return carry

        lax.fori_loop(0, plan.blocks, ocean, 0)


def far_wet(index, in_cross, wet_cross):
    return [jnp.where(in_cross[k], take_lanes(wet_cross, index[k]), 0.0) for k in range(3)]


def far_moves(parts, own, cross, far, index):
    totals = [p - o * (f[0] + f[1] + f[2]) for p, o, f in zip(parts, own, far)]
    for k in range(3):
        for j in range(len(own)):
            totals[j] = totals[j] + far[j][k] * take_lanes(cross[j], index[k])
    return totals


def bgc_far(plan, second, react_ref, nb_ref, own_ref, cross_ref, part_ref, far_ref, aux_ref, h_ref, l_ref, put):
    comp, odd = lax.axis_index("comp"), lax.axis_index("tile") % 2
    low = comp != 0
    nt, cols = plan.nt, nb_ref.shape[-1]
    index, _, in_cross = neighbours_of(nb_ref, odd)
    wet = own_ref[plan.wet]
    wets = far_wet(index, in_cross, cross_ref[plan.wet])
    first = jnp.where(low, 0, 1)
    shift = jnp.where(low, plan.main - 1, -1)
    zero = jnp.zeros((SUB, cols), F32)
    end = (plan.window + 1) * SUB
    above = pl.ds(pl.multiple_of(first * SUB, SUB), SUB)
    l_ref[above, :] = zero
    for j in range(nt):
        h_ref[j, above, :] = zero
        h_ref[j, end : end + SUB, :] = zero

    def move(r, carry):
        level = level_block(r + shift, cols)
        far = [jnp.where(level < wets[k], far_ref[k, r], 0.0) for k in range(3)]
        there = pl.ds(pl.multiple_of((r + 1) * SUB, SUB), SUB)
        l_ref[there, :] = aux_ref[0, r]
        slots = [plan.slot(j, r) for j in range(nt)]
        parts = [part_ref[j, r] for j in range(nt)]
        own = [own_ref[s] for s in slots]
        cross = [cross_ref[s] for s in slots]
        for j, v in enumerate(far_moves(parts, own, cross, [far] * nt, index)):
            h_ref[j, there, :] = v
        return carry

    def react(r, carry):
        active = (level_block(r + shift, cols) < wet).astype(F32)
        at = (r + 1) * SUB
        there, after, before = pl.ds(pl.multiple_of(at, SUB), SUB), pl.ds(at + 1, SUB), pl.ds(at - 1, SUB)
        down, up = l_ref[there, :], l_ref[before, :]
        ys, ts = [], []
        for j in range(nt):
            v = h_ref[j, there, :]
            y = v + down * (h_ref[j, after, :] - v) - up * (v - h_ref[j, before, :])
            ys.append(y)
            ts.append(jnp.tanh(y))
        growth = aux_ref[1, r]
        if second:
            total = react_ref[0, 0] * ts[0]
            for j in range(1, nt):
                total = total + react_ref[0, j] * ts[j]
            put(0, r, (ys[0] + growth * total) * active)
        else:
            n = react_ref.shape[1]
            ts += [zero] * (n // SUB - nt)
            stack = jnp.concatenate(ts, axis=0)
            high = stack.astype(BF16)
            rest = (stack - high.astype(F32)).astype(BF16)
            both = jnp.dot(react_ref[...], high, preferred_element_type=F32)
            total = both[:n] + both[n:] + jnp.dot(react_ref[0:n, :], rest, preferred_element_type=F32)
            for i in range(nt):
                put(i, r, (ys[i] + growth * total[i * SUB : (i + 1) * SUB]) * active)
        return carry

    lax.fori_loop(first, plan.window, move, 0)
    lax.fori_loop(first, plan.window, react, 0)


def ocean_far(plan, nb_ref, f_ref, own_ref, cross_ref, opart_ref, ofar_ref, oaux_ref, q_ref, l_ref, put):
    odd = lax.axis_index("tile") % 2
    cols = nb_ref.shape[-1]
    index, _, in_cross = neighbours_of(nb_ref, odd)
    wet = own_ref[plan.wet]
    wets = far_wet(index, in_cross, cross_ref[plan.wet])
    zero = jnp.zeros((SUB, cols), F32)
    end = (plan.blocks + 1) * SUB
    l_ref[0:SUB, :] = zero
    for i in range(4):
        q_ref[i, 0:SUB, :] = zero
        q_ref[i, end : end + SUB, :] = zero

    def move(b, carry):
        level = level_block(b, cols)
        far = [jnp.where(level < wets[k], ofar_ref[k, b], 0.0) for k in range(3)]
        flat = [jnp.where(v > 0.0, 0.15, 0.0) for v in far]
        there = pl.ds(pl.multiple_of((b + 1) * SUB, SUB), SUB)
        l_ref[there, :] = oaux_ref[0, b]
        parts = [opart_ref[i, b] for i in range(4)]
        own = [f_ref[i, b] for i in range(4)]
        cross = [cross_ref[plan.extra + i * plan.blocks + b] for i in range(4)]
        q = far_moves(parts, own, cross, [far, far, flat, flat], index)
        q_ref[0, there, :] = q[0]
        q_ref[1, there, :] = q[1]
        q_ref[2, there, :] = ROTATE_COS * q[2] + ROTATE_SIN * q[3]
        q_ref[3, there, :] = -ROTATE_SIN * q[2] + ROTATE_COS * q[3]
        return carry

    lax.fori_loop(0, plan.blocks, move, 0)
    warm = [None] * plan.blocks
    for b in range(plan.blocks):
        at = (b + 1) * SUB
        active = (level_block(b, cols) < wet).astype(F32)
        down, up = l_ref[at : at + SUB, :], l_ref[at - 1 : at - 1 + SUB, :]
        for i in range(4):
            v = q_ref[i, at : at + SUB, :]
            y = v + down * (q_ref[i, at + 1 : at + 1 + SUB, :] - v) - up * (v - q_ref[i, at - 1 : at - 1 + SUB, :])
            if i == 0:
                warm[b] = y + oaux_ref[1, b]
                put(0, b, warm[b] * active)
            else:
                put(i, b, y * active)
        put(5, b, oaux_ref[2, b])
    sub = lax.broadcasted_iota(jnp.int32, (SUB, cols), 0)
    for b in range(plan.blocks):
        active = (level_block(b, cols) < wet).astype(F32)
        nxt = warm[b + 1] if b + 1 < plan.blocks else None
        lower = pltpu.roll(warm[b], SUB - 1, 0)
        if nxt is None:
            lower = jnp.where(sub == SUB - 1, warm[b], lower)
        else:
            lower = jnp.where(sub == SUB - 1, pltpu.roll(nxt, SUB - 1, 0), lower)
        put(4, b, (warm[b] - lower) * active)


def first_far_kernel(
    plan, react_ref, nb_ref, f_ref, own_ref, cross_ref, part_ref, far_ref, aux_ref, opart_ref, ofar_ref, oaux_ref,
    out_ref, over_ref, h_ref, l_ref, q_ref, ql_ref,
):
    comp = lax.axis_index("comp")
    out_ref[plan.wet] = own_ref[plan.wet]

    @pl.when(comp == 0)
    def _():
        def put(i, b, value):
            over_ref[i, b] = value
            if i < 4:
                out_ref[plan.extra + i * plan.blocks + b] = value

        ocean_far(plan, nb_ref, f_ref, own_ref, cross_ref, opart_ref, ofar_ref, oaux_ref, q_ref, ql_ref, put)

    def put(i, r, value):
        out_ref[plan.slot(i, r)] = value

    bgc_far(plan, False, react_ref, nb_ref, own_ref, cross_ref, part_ref, far_ref, aux_ref, h_ref, l_ref, put)

    @pl.when(comp != 0)
    def _():
        over_ref[0, plan.main - 1] = out_ref[plan.extra]
        over_ref[0, plan.main :] = out_ref[0 : plan.main]


def second_bgc_kernel(
    plan, react_ref, nb_ref, own_ref, cross_ref, part_ref, far_ref, aux_ref, out_ref, h_ref, l_ref
):
    def put(i, r, value):
        out_ref[r] = value

    bgc_far(plan, True, react_ref, nb_ref, own_ref, cross_ref, part_ref, far_ref, aux_ref, h_ref, l_ref, put)


def second_ocean_kernel(
    plan, nb_ref, f_ref, over_ref, own_ref, cross_ref, opart_ref, ofar_ref, oaux_ref, out_ref, q_ref, ql_ref
):
    comp = lax.axis_index("comp")

    @pl.when(comp == 0)
    def _():
        def put(i, b, value):
            out_ref[i, b] = value

        ocean_far(plan, nb_ref, f_ref, own_ref, cross_ref, opart_ref, ofar_ref, oaux_ref, q_ref, ql_ref, put)

    @pl.when(comp != 0)
    def _():
        out_ref[...] = over_ref[...]


def last_kernel(plan, chl_ref, mine_ref, upper_ref, out_ref):
    comp = lax.axis_index("comp")
    cut = SUB // 2

    @pl.when(comp == 0)
    def _():
        out_ref[...] = chl_ref[...]

    @pl.when(comp != 0)
    def _():
        out_ref[: plan.main - 1] = upper_ref[1 : plan.main]
        sub = lax.broadcasted_iota(jnp.int32, mine_ref.shape[1:], 0)
        out_ref[plan.main - 1] = jnp.where(sub < cut, upper_ref[plan.main], mine_ref[0])
        out_ref[plan.main :] = mine_ref[1:]


def call(kernel, outs, ins, specs=None, scratch=(), cost=1_000_000):
    inner = kernel.func if isinstance(kernel, functools.partial) else kernel
    return pl.pallas_call(
        kernel,
        name=inner.__name__,
        out_shape=outs,
        in_specs=specs or [VMEM] * len(ins),
        out_specs=jax.tree.map(lambda _: VMEM, outs),
        scratch_shapes=list(scratch),
        compiler_params=pltpu.CompilerParams(vmem_limit_bytes=GRANT),
        cost_estimate=pl.CostEstimate(flops=cost, bytes_accessed=1_000_000, transcendentals=0),
    )(*ins)


def swaps(tiles, across):
    pairs = []
    for c in (0, 1):
        for t in range(tiles):
            other = (t + 1) % tiles if (t % 2 == 0) != across else (t - 1) % tiles
            pairs.append((c * tiles + t, c * tiles + other))
    return pairs


def over_comp(sources, tiles):
    return [(c * tiles + t, (1 - c) * tiles + t) for c in sources for t in range(tiles)]


def per_device(ocean_fields, tracers, reaction, wet_levels, neighbours):
    tiles = lax.axis_size("tile")
    nt, lev, cols = tracers.shape
    plan = Plan(nt, lev)
    blocks, window = plan.blocks, plan.window
    fields = ocean_fields.reshape(-1, blocks, SUB, cols)
    nf = fields.shape[0]
    sent = lambda v, pairs: lax.ppermute(v, AXES, pairs)

    near_shapes = (
        shape_of(nt, window, SUB, cols),
        shape_of(3, window, SUB, cols),
        shape_of(2, window, SUB, cols),
        shape_of(4, blocks, SUB, cols),
        shape_of(3, blocks, SUB, cols),
        shape_of(3, blocks, SUB, cols),
    )
    near_scratch = (pltpu.VMEM((nf, window, SUB, cols), F32), pltpu.VMEM((blocks, SUB, cols), F32))
    h_scratch = (pltpu.VMEM((nt, (window + 2) * SUB, cols), F32), pltpu.VMEM(((window + 2) * SUB, cols), F32))
    q_scratch = (pltpu.VMEM((4, (blocks + 2) * SUB, cols), F32), pltpu.VMEM(((blocks + 2) * SUB, cols), F32))

    out_zero, top_zero, chl_zero = call(
        functools.partial(pack_kernel, plan),
        (shape_of(plan.total, SUB, cols), shape_of(nf, plan.main, SUB, cols), shape_of(blocks, SUB, cols)),
        tuple(
            pltpu.with_memory_space_constraint(v, pltpu.HBM)
            for v in (wet_levels.reshape(1, cols), fields, tracers.reshape(nt, blocks, SUB, cols))
        ),
        specs=[HBM, HBM, HBM],
        scratch=[pltpu.VMEM((1, cols), jnp.int32), pltpu.SemaphoreType.DMA((nt + 8,))],
    )
    cross = sent(out_zero, swaps(tiles, True))
    core = sent(out_zero, swaps(tiles, False))
    lagged = sent(top_zero, over_comp((1,), tiles))
    n = -(-nt // 2) * 2 * SUB
    matrix = call(matrix_kernel, jax.ShapeDtypeStruct((2 * n, n), BF16), (reaction,))

    near = call(
        functools.partial(near_kernel, plan, False),
        near_shapes,
        (neighbours, fields, lagged, fields, out_zero, core, chl_zero),
        scratch=near_scratch,
        cost=8_000_000,
    )
    out_one, over_one = call(
        functools.partial(first_far_kernel, plan),
        (shape_of(plan.total, SUB, cols), shape_of(nf, blocks, SUB, cols)),
        (matrix, neighbours, fields, out_zero, cross, *near),
        scratch=h_scratch + q_scratch,
        cost=8_000_000,
    )

    cross = sent(out_one, swaps(tiles, True))
    core = sent(out_one, swaps(tiles, False))
    over = sent(over_one, over_comp((0, 1), tiles))
    *near, chl_one = call(
        functools.partial(near_kernel, plan, True),
        near_shapes + (shape_of(blocks, SUB, cols),),
        (neighbours, over_one, over_one, over, out_one, core, out_one, over),
        scratch=near_scratch,
        cost=8_000_000,
    )
    chl_two = call(
        functools.partial(second_bgc_kernel, plan),
        shape_of(window, SUB, cols),
        (reaction, neighbours, out_one, cross, *near[:3]),
        specs=[SMEM] + [VMEM] * 6,
        scratch=h_scratch,
        cost=8_000_000,
    )
    upper = sent(chl_two, over_comp((0,), tiles))
    ocean_out = call(
        functools.partial(second_ocean_kernel, plan),
        shape_of(nf, blocks, SUB, cols),
        (neighbours, over_one, over, out_one, cross, *near[3:]),
        scratch=q_scratch,
        cost=4_000_000,
    )
    chl_out = call(
        functools.partial(last_kernel, plan), shape_of(blocks, SUB, cols), (chl_one, chl_two, upper)
    )
    return (ocean_out.reshape(1, nf, lev, cols), chl_out.reshape(1, lev, cols))


def solution(mesh):
    return jax.shard_map(
        per_device,
        mesh=mesh,
        in_specs=(
            P("comp", None, None, "tile"),
            P(None, None, "tile"),
            P(),
            P("tile"),
            P(None, "tile"),
        ),
        out_specs=(P("comp", None, None, "tile"), P("comp", None, "tile")),
        check_vma=False,
    )
```

```python
import functools
import math

import jax
import jax.numpy as jnp
from jax import lax
from jax.experimental import pallas as pl
from jax.experimental.pallas import tpu as pltpu
from jax.sharding import PartitionSpec as P


ROTATE_COS = math.cos(0.3)
ROTATE_SIN = math.sin(0.3)
SUB = 8
AXES = ("comp", "tile")
ANGLES = [2.0 * math.pi * k / 3.0 for k in range(3)]
F32 = jnp.float32
BF16 = jnp.bfloat16
GRANT = 8 << 20


VMEM = pl.BlockSpec(memory_space=pltpu.VMEM)
SMEM = pl.BlockSpec(memory_space=pltpu.SMEM)
HBM = pl.BlockSpec(memory_space=pltpu.HBM)


class Plan:
    def __init__(self, nt, lev):
        self.nt, self.lev = nt, lev
        self.blocks = lev // SUB
        self.full = self.blocks // 2 - 1
        self.window = self.full + 2
        self.half = SUB // 2
        self.halves = SUB * nt * self.full
        self.wet = self.halves + self.half * nt
        self.p_rows = -(-(self.wet + self.half) // SUB) * SUB
        self.q_rows = (
            max(4 * lev, -(-(SUB + self.half) * nt // SUB) * SUB),
            max(4 * lev, 2 * SUB * nt),
        )

    def rs(self, comp):
        return list(range(1 - comp, self.window))

    def level(self, comp, r):
        return SUB * (r - 1) if comp == 0 else SUB * (self.full + r)

    def block(self, comp, second, p, q, j, r):
        if comp == 0:
            return p(SUB * (self.full * j + r - 1)) if r <= self.full else p(self.halves + self.half * j)
        if r < self.full:
            return p(SUB * (self.full * j + r))
        if second:
            return q(SUB * (2 * j + r - self.full))
        if r > self.full:
            return q(SUB * j)
        upper = p(self.halves + self.half * j)
        lower = q(SUB * self.nt + self.half * (j - 1))
        sub = lax.broadcasted_iota(jnp.int32, upper.shape, 0)
        return jnp.where(sub < self.half, upper, lower)


def rows_at(ref, base=0):
    return lambda offset: ref[base + offset : base + offset + SUB, :]


def edge_weights(eastward, northward):
    return [
        0.05 + 0.25 * jax.nn.sigmoid(eastward * math.cos(a) + northward * math.sin(a)) for a in ANGLES
    ]


def take_lanes(block, index):
    return jnp.take_along_axis(block, index, axis=1, mode="promise_in_bounds")


def shape_of(*dims):
    return jax.ShapeDtypeStruct(dims, F32)


def neighbours_of(nb_ref, odd):
    cols = nb_ref.shape[-1]
    core_side = jnp.where(odd == 1, 0, 2)
    index, in_core, in_cross = [], [], []
    for k in range(3):
        nb = jnp.broadcast_to(nb_ref[k : k + 1, :], (SUB, cols))
        side = nb // cols
        index.append(nb - side * cols)
        in_core.append(side == core_side)
        in_cross.append(side == 2 - core_side)
    return index, in_core, in_cross


def level_block(first, cols):
    return lax.broadcasted_iota(jnp.int32, (SUB, cols), 0).astype(F32) + float(first)


def link_weight(level, wet, mixing, last):
    nxt = level + 1.0
    return jnp.where((nxt < wet) & (nxt <= last), 0.02 + 0.13 * jax.nn.sigmoid(mixing), 0.0)


def wet_of(plan, ref):
    return jnp.broadcast_to(ref[plan.wet : plan.wet + 1, :], (SUB, ref.shape[1]))


def on_side(comp):
    return pl.when(lax.axis_index("comp") == comp)


def pack_kernel(plan, wet_ref, f_ref, t_ref, p_ref, q_ref, pq_ref, top_ref, chl_ref, wet_buf, half_buf, sems):
    nt, full, half, lev = plan.nt, plan.full, plan.half, plan.lev
    tall = SUB * full
    first = pl.multiple_of(lax.axis_index("comp") * tall, SUB)
    copies = [(wet_ref, wet_buf), (t_ref.at[:, pl.ds(pl.multiple_of(first + tall, SUB), SUB)], half_buf)]
    copies += [(t_ref.at[j, pl.ds(first, tall)], p_ref.at[pl.ds(tall * j, tall)]) for j in range(nt)]
    copies.append((t_ref.at[0], chl_ref))
    copies.append((f_ref.at[:, pl.ds(0, top_ref.shape[1])], top_ref))
    copies = [pltpu.make_async_copy(s, d, sems.at[i]) for i, (s, d) in enumerate(copies)]
    for c in copies:
        c.start()
    base = len(copies)
    ocean = [
        pltpu.make_async_copy(f_ref.at[i], q_ref.at[pl.ds(i * lev, lev)], sems.at[base + i]) for i in range(4)
    ]
    deep = [
        pltpu.make_async_copy(t_ref.at[j, pl.ds(lev - SUB, SUB)], q_ref.at[pl.ds(SUB * j, SUB)], sems.at[base + j])
        for j in range(nt)
    ]

    @on_side(0)
    def _():
        for c in ocean:
            c.start()

    @on_side(1)
    def _():
        for c in deep:
            c.start()

    for c in copies:
        c.wait()
    p_ref[plan.wet : plan.wet + half, :] = jnp.broadcast_to(wet_buf[...].astype(F32), (half, wet_buf.shape[1]))
    for j in range(nt):
        p_ref[plan.halves + half * j : plan.halves + half * (j + 1), :] = half_buf[j, 0:half, :]

    @on_side(0)
    def _():
        for c in ocean:
            c.wait()

    @on_side(1)
    def _():
        for c in deep:
            c.wait()
        for j in range(nt):
            at = SUB * nt + half * j
            q_ref[at : at + half, :] = half_buf[j, half:SUB, :]

    pq_ref[0 : plan.p_rows, :] = p_ref[...]
    pq_ref[plan.p_rows :, :] = q_ref[...]


def matrix_kernel(r_ref, out_ref):
    nt = r_ref.shape[0]
    rows, n = out_ref.shape
    p = lax.broadcasted_iota(jnp.int32, (n, nt), 0)
    spread = (p // SUB == lax.broadcasted_iota(jnp.int32, (n, nt), 1)).astype(F32)
    exact = functools.partial(
        lax.dot_general, precision=lax.Precision.HIGHEST, preferred_element_type=F32
    )
    tall = exact(spread, r_ref[...], (((1,), (0,)), ((), ())))
    full = exact(tall, spread, (((1,), (1,)), ((), ())))
    a = lax.broadcasted_iota(jnp.int32, (n, n), 0)
    b = lax.broadcasted_iota(jnp.int32, (n, n), 1)
    full = jnp.where(a % SUB == b % SUB, full, 0.0)
    high = full.astype(BF16)
    out_ref[0:n, :] = high
    out_ref[n:rows, :] = (full - high.astype(F32)).astype(BF16)


def near_kernel(plan, second, nb_ref, f_ref, ga_ref, gb_ref, pq_ref, core_ref, chl_ref, *refs):
    if second:
        chl_low_ref, *refs = refs
    part_ref, far_ref, aux_ref, opart_ref, ofar_ref, oaux_ref = refs[:6]
    chl_out_ref = refs[6] if second else None
    odd = lax.axis_index("tile") % 2
    cols = nb_ref.shape[-1]
    nt, p_rows = plan.nt, plan.p_rows
    index, in_core, in_cross = neighbours_of(nb_ref, odd)
    wet, wet_core = wet_of(plan, pq_ref), wet_of(plan, core_ref)
    near_wet = []
    for k in range(3):
        found = jnp.where(in_core[k], take_lanes(wet_core, index[k]), take_lanes(wet, index[k]))
        near_wet.append(jnp.where(in_cross[k], 0.0, found))
    last = float(plan.lev - 1)

    def split(level, ws):
        active = level < wet
        near = [jnp.where(active & (level < near_wet[k]), ws[k], 0.0) for k in range(3)]
        far = [jnp.where(active & in_cross[k], ws[k], 0.0) for k in range(3)]
        return near, far

    def moves(own, core, near, rest):
        totals = [o * r for o, r in zip(own, rest)]
        for k in range(3):
            for j in range(len(own)):
                v = jnp.where(in_core[k], take_lanes(core[j], index[k]), take_lanes(own[j], index[k]))
                totals[j] = totals[j] + near[j][k] * v
        return totals

    def tracers(comp):
        for r in plan.rs(comp):
            first = plan.level(comp, r)
            level = level_block(first, cols)
            g = [(gb_ref if comp else ga_ref)[i, first : first + SUB, :] for i in range(6)]
            near, far = split(level, edge_weights(g[2], g[3]))
            rest = 1.0 - (near[0] + near[1] + near[2])
            for k in range(3):
                far_ref[k, r] = far[k]
            aux_ref[0, r] = link_weight(level, wet, g[4], last)
            aux_ref[1, r] = 0.5 * g[5] * jax.nn.sigmoid(g[0] + 0.5 * g[1])
            own = [plan.block(comp, second, rows_at(pq_ref), rows_at(pq_ref, p_rows), j, r) for j in range(nt)]
            core = [plan.block(comp, second, rows_at(core_ref), rows_at(core_ref, p_rows), j, r) for j in range(nt)]
            for j, v in enumerate(moves(own, core, [near] * nt, [rest] * nt)):
                part_ref[j, r] = v

    @on_side(1)
    def _():
        tracers(1)

    @on_side(0)
    def _():
        tracers(0)
        top = f_ref[5, 0:1, :]
        cut = SUB * (plan.full + 1) - SUB + 2

        def chl_block(b):
            at = SUB * b
            if not second:
                return chl_ref[at : at + SUB, :]
            if b < plan.full:
                return chl_ref[at : at + SUB, :]
            v = chl_low_ref[0, at : at + SUB, :]
            if b > plan.full:
                return v
            return jnp.where(level_block(at, cols) < float(cut), chl_ref[plan.halves : plan.halves + SUB, :], v)

        run = jnp.zeros((1, cols), F32)
        for b in range(plan.blocks):
            x = chl_block(b)
            if second:
                chl_out_ref[SUB * b : SUB * (b + 1), :] = x
            absorbed = 0.01 + 0.3 * (jnp.maximum(x, 0.0) + jnp.log1p(jnp.exp(-jnp.abs(x))))
            level = level_block(SUB * b, cols)
            sub = lax.broadcasted_iota(jnp.int32, (SUB, cols), 0)
            cum = absorbed
            for d in (1, 2, 4):
                cum = cum + jnp.where(sub >= d, pltpu.roll(cum, d, 0), 0.0)
            depth = cum + run
            ceiling = jnp.exp(-(depth - absorbed))
            oaux_ref[1, b] = 4.0 * top * (ceiling - jnp.exp(-depth))
            oaux_ref[2, b] = jnp.where(level < wet, top * ceiling, 0.0)
            run = depth[SUB - 1 : SUB, :]

        for b in range(plan.blocks):
            at = SUB * b
            level = level_block(at, cols)
            f = [f_ref[i, at : at + SUB, :] for i in range(5)]
            near, far = split(level, edge_weights(f[2], f[3]))
            rest = 1.0 - (near[0] + near[1] + near[2])
            flat = [jnp.where(v > 0.0, 0.15, 0.0) for v in near]
            rest_flat = 1.0 - (flat[0] + flat[1] + flat[2])
            for k in range(3):
                ofar_ref[k, b] = far[k]
            oaux_ref[0, b] = link_weight(level, wet, f[4], last)
            core = [rows_at(core_ref, p_rows)(plan.lev * i + at) for i in range(4)]
            out = moves(f[:4], core, [near, near, flat, flat], [rest, rest, rest_flat, rest_flat])
            for i in range(4):
                opart_ref[i, b] = out[i]


def far_wet(index, in_cross, wet_cross):
    return [jnp.where(in_cross[k], take_lanes(wet_cross, index[k]), 0.0) for k in range(3)]


def far_moves(parts, own, cross, far, index):
    totals = [p - o * (f[0] + f[1] + f[2]) for p, o, f in zip(parts, own, far)]
    for k in range(3):
        for j in range(len(own)):
            totals[j] = totals[j] + far[j][k] * take_lanes(cross[j], index[k])
    return totals


class Far:
    def __init__(self, plan, comp, second, nb_ref, pq_ref, cross_p_ref, part_ref, far_ref, aux_ref, h_ref, l_ref):
        self.plan, self.comp, self.second = plan, comp, second
        self.cols = nb_ref.shape[-1]
        self.own_p, self.own_q = rows_at(pq_ref), rows_at(pq_ref, plan.p_rows)
        self.part, self.far, self.aux, self.h, self.l = part_ref, far_ref, aux_ref, h_ref, l_ref
        self.index, _, in_cross = neighbours_of(nb_ref, lax.axis_index("tile") % 2)
        self.wet = wet_of(plan, pq_ref)
        self.wets = far_wet(self.index, in_cross, wet_of(plan, cross_p_ref))

    def at(self, r):
        return SUB * (r + 1)

    def clear(self, before, after):
        zero = jnp.zeros((SUB, self.cols), F32)
        if before is not None:
            self.l[self.at(before) : self.at(before) + SUB, :] = zero
        for j in range(self.plan.nt):
            for r in (before, after):
                if r is not None:
                    self.h[j, self.at(r) : self.at(r) + SUB, :] = zero

    def move(self, r, p, q):
        plan, at = self.plan, self.at(r)
        level = level_block(plan.level(self.comp, r), self.cols)
        far = [jnp.where(level < self.wets[k], self.far[k, r], 0.0) for k in range(3)]
        self.l[at : at + SUB, :] = self.aux[0, r]
        js = range(plan.nt)
        parts = [self.part[j, r] for j in js]
        own = [plan.block(self.comp, self.second, self.own_p, self.own_q, j, r) for j in js]
        cross = [plan.block(self.comp, self.second, p, q, j, r) for j in js]
        for j, v in enumerate(far_moves(parts, own, cross, [far] * plan.nt, self.index)):
            self.h[j, at : at + SUB, :] = v

    def react(self, r, react_ref, put):
        plan, at = self.plan, self.at(r)
        active = (level_block(plan.level(self.comp, r), self.cols) < self.wet).astype(F32)
        down, up = self.l[at : at + SUB, :], self.l[at - 1 : at - 1 + SUB, :]
        ys, ts = [], []
        for j in range(plan.nt):
            v = self.h[j, at : at + SUB, :]
            y = v + down * (self.h[j, at + 1 : at + 1 + SUB, :] - v) - up * (v - self.h[j, at - 1 : at - 1 + SUB, :])
            ys.append(y)
            ts.append(jnp.tanh(y))
        growth = self.aux[1, r]
        if self.second:
            total = react_ref[0, 0] * ts[0]
            for j in range(1, plan.nt):
                total = total + react_ref[0, j] * ts[j]
            put(0, r, (ys[0] + growth * total) * active)
            return
        n = react_ref.shape[1]
        ts += [jnp.zeros_like(ts[0])] * (n // SUB - plan.nt)
        stack = jnp.concatenate(ts, axis=0)
        high = stack.astype(BF16)
        rest = (stack - high.astype(F32)).astype(BF16)
        both = jnp.dot(react_ref[...], high, preferred_element_type=F32)
        total = both[:n] + both[n:] + jnp.dot(react_ref[0:n, :], rest, preferred_element_type=F32)
        for i in range(plan.nt):
            put(i, r, (ys[i] + growth * total[i * SUB : (i + 1) * SUB]) * active)


def nothing(offset):
    raise ValueError("not there")


def upper_kernel(plan, react_ref, nb_ref, pq_ref, p_ref, part_ref, far_ref, aux_ref, out_ref, edge_ref, h_ref, l_ref):
    out_ref[plan.wet : plan.wet + plan.half, :] = pq_ref[plan.wet : plan.wet + plan.half, :]
    refs = (nb_ref, pq_ref, p_ref, part_ref, far_ref, aux_ref, h_ref, l_ref)
    p = rows_at(p_ref)

    @on_side(0)
    def _():
        work = Far(plan, 0, False, *refs)
        work.clear(0, plan.window)
        for r in plan.rs(0):
            work.move(r, p, nothing)

        def put(i, r, value):
            if r <= plan.full:
                at = SUB * (plan.full * i + r - 1)
                out_ref[at : at + SUB, :] = value
            else:
                at = plan.halves + plan.half * i
                out_ref[at : at + plan.half, :] = value[0 : plan.half]

        for r in plan.rs(0):
            work.react(r, react_ref, put)

    @on_side(1)
    def _():
        work = Far(plan, 1, False, *refs)
        work.clear(-1, None)
        lower = lambda offset: jnp.zeros((SUB, work.cols), F32)
        for r in range(plan.full + 1):
            work.move(r, p, lower)
        at = work.at(plan.full - 1)
        for j in range(plan.nt):
            edge_ref[j] = h_ref[j, at : at + SUB, :]

        def put(i, r, value):
            at = SUB * (plan.full * i + r)
            out_ref[at : at + SUB, :] = value

        for r in range(plan.full):
            work.react(r, react_ref, put)


def ocean_far(plan, nb_ref, f_ref, pq_ref, p_ref, q_ref, opart_ref, ofar_ref, oaux_ref, w_ref, l_ref, put):
    cols = nb_ref.shape[-1]
    index, _, in_cross = neighbours_of(nb_ref, lax.axis_index("tile") % 2)
    wet = wet_of(plan, pq_ref)
    wets = far_wet(index, in_cross, wet_of(plan, p_ref))
    zero = jnp.zeros((SUB, cols), F32)
    end = SUB * (plan.blocks + 1)
    l_ref[0:SUB, :] = zero
    for i in range(4):
        w_ref[i, 0:SUB, :] = zero
        w_ref[i, end : end + SUB, :] = zero
    for b in range(plan.blocks):
        at = SUB * b
        level = level_block(at, cols)
        far = [jnp.where(level < wets[k], ofar_ref[k, b], 0.0) for k in range(3)]
        flat = [jnp.where(v > 0.0, 0.15, 0.0) for v in far]
        there = slice(at + SUB, at + 2 * SUB)
        l_ref[there, :] = oaux_ref[0, b]
        parts = [opart_ref[i, b] for i in range(4)]
        own = [f_ref[i, at : at + SUB, :] for i in range(4)]
        cross = [rows_at(q_ref)(plan.lev * i + at) for i in range(4)]
        q = far_moves(parts, own, cross, [far, far, flat, flat], index)
        w_ref[0, there, :] = q[0]
        w_ref[1, there, :] = q[1]
        w_ref[2, there, :] = ROTATE_COS * q[2] + ROTATE_SIN * q[3]
        w_ref[3, there, :] = -ROTATE_SIN * q[2] + ROTATE_COS * q[3]
    warm = [None] * plan.blocks
    for b in range(plan.blocks):
        at = SUB * (b + 1)
        active = (level_block(SUB * b, cols) < wet).astype(F32)
        down, up = l_ref[at : at + SUB, :], l_ref[at - 1 : at - 1 + SUB, :]
        for i in range(4):
            v = w_ref[i, at : at + SUB, :]
            y = v + down * (w_ref[i, at + 1 : at + 1 + SUB, :] - v) - up * (v - w_ref[i, at - 1 : at - 1 + SUB, :])
            if i == 0:
                warm[b] = y + oaux_ref[1, b]
                put(0, b, warm[b] * active)
            else:
                put(i, b, y * active)
        put(5, b, oaux_ref[2, b])
    sub = lax.broadcasted_iota(jnp.int32, (SUB, cols), 0)
    for b in range(plan.blocks):
        active = (level_block(SUB * b, cols) < wet).astype(F32)
        lower = pltpu.roll(warm[b], SUB - 1, 0)
        if b + 1 < plan.blocks:
            lower = jnp.where(sub == SUB - 1, pltpu.roll(warm[b + 1], SUB - 1, 0), lower)
        else:
            lower = jnp.where(sub == SUB - 1, warm[b], lower)
        put(4, b, (warm[b] - lower) * active)


def lower_kernel(
    plan, react_ref, nb_ref, f_ref, pq_ref, p_ref, q_ref, part_ref, far_ref, aux_ref, opart_ref, ofar_ref, oaux_ref,
    done_ref, edge_ref, out_ref, both_ref, over_ref, h_ref, l_ref, w_ref, wl_ref,
):
    both_ref[0 : plan.p_rows, :] = done_ref[...]

    @on_side(0)
    def _():
        def put(i, b, value):
            at = SUB * b
            over_ref[i, at : at + SUB, :] = value
            if i < 4:
                for ref, base in ((out_ref, 0), (both_ref, plan.p_rows)):
                    ref[base + plan.lev * i + at : base + plan.lev * i + at + SUB, :] = value

        ocean_far(plan, nb_ref, f_ref, pq_ref, p_ref, q_ref, opart_ref, ofar_ref, oaux_ref, w_ref, wl_ref, put)

    @on_side(1)
    def _():
        work = Far(plan, 1, False, nb_ref, pq_ref, p_ref, part_ref, far_ref, aux_ref, h_ref, l_ref)
        work.clear(None, plan.window)
        before = work.at(plan.full - 1)
        l_ref[before : before + SUB, :] = aux_ref[0, plan.full - 1]
        for j in range(plan.nt):
            h_ref[j, before : before + SUB, :] = edge_ref[j]
        rs = (plan.full, plan.full + 1)
        for r in rs:
            work.move(r, rows_at(p_ref), rows_at(q_ref))

        def put(i, r, value):
            at = SUB * (2 * i + r - plan.full)
            out_ref[at : at + SUB, :] = value
            both_ref[plan.p_rows + at : plan.p_rows + at + SUB, :] = value
            if i == 0:
                over_ref[0, SUB * (plan.full + r) : SUB * (plan.full + r + 1), :] = value

        for r in rs:
            work.react(r, react_ref, put)
        for r in range(plan.full):
            over_ref[0, SUB * (plan.full + r) : SUB * (plan.full + r + 1), :] = done_ref[SUB * r : SUB * (r + 1), :]


def chl_kernel(plan, react_ref, nb_ref, pq_ref, p_ref, part_ref, far_ref, aux_ref, out_ref, h_ref, l_ref):
    @on_side(0)
    def _():
        work = Far(plan, 0, True, nb_ref, pq_ref, p_ref, part_ref, far_ref, aux_ref, h_ref, l_ref)
        work.clear(0, plan.window)
        for r in plan.rs(0):
            work.move(r, rows_at(p_ref), nothing)

        def put(i, r, value):
            out_ref[SUB * (r - 1) : SUB * r, :] = value

        for r in plan.rs(0):
            work.react(r, react_ref, put)


def last_kernel(
    plan, react_ref, nb_ref, f_ref, over_ref, pq_ref, p_ref, q_ref, part_ref, far_ref, aux_ref, opart_ref, ofar_ref,
    oaux_ref, chl_ref, upper_ref, out_ref, chl_out_ref, h_ref, l_ref, w_ref, wl_ref,
):
    @on_side(0)
    def _():
        def put(i, b, value):
            out_ref[i, SUB * b : SUB * (b + 1), :] = value

        chl_out_ref[...] = chl_ref[...]
        ocean_far(plan, nb_ref, f_ref, pq_ref, p_ref, q_ref, opart_ref, ofar_ref, oaux_ref, w_ref, wl_ref, put)

    @on_side(1)
    def _():
        out_ref[...] = over_ref[...]
        work = Far(plan, 1, True, nb_ref, pq_ref, p_ref, part_ref, far_ref, aux_ref, h_ref, l_ref)
        work.clear(-1, plan.window)
        for r in plan.rs(1):
            work.move(r, rows_at(p_ref), rows_at(q_ref))
        tall = SUB * plan.full
        chl_out_ref[0:tall, :] = upper_ref[0:tall, :]

        def put(i, r, value):
            at = tall + SUB * r
            if r == 0:
                sub = lax.broadcasted_iota(jnp.int32, value.shape, 0)
                value = jnp.where(sub < 2, upper_ref[at : at + SUB, :], value)
            chl_out_ref[at : at + SUB, :] = value

        for r in plan.rs(1):
            work.react(r, react_ref, put)


def call(kernel, outs, ins, specs=None, scratch=(), cost=1_000_000):
    return pl.pallas_call(
        kernel,
        out_shape=outs,
        in_specs=specs or [VMEM] * len(ins),
        out_specs=jax.tree.map(lambda _: VMEM, outs),
        scratch_shapes=list(scratch),
        compiler_params=pltpu.CompilerParams(vmem_limit_bytes=GRANT),
        cost_estimate=pl.CostEstimate(flops=cost, bytes_accessed=1_000_000, transcendentals=0),
    )(*ins)


def swaps(tiles, across):
    pairs = []
    for c in (0, 1):
        for t in range(tiles):
            other = (t + 1) % tiles if (t % 2 == 0) != across else (t - 1) % tiles
            pairs.append((c * tiles + t, c * tiles + other))
    return pairs


def over_comp(sources, tiles):
    return [(c * tiles + t, (1 - c) * tiles + t) for c in sources for t in range(tiles)]


def sent(v, pairs):
    return lax.ppermute(v, AXES, pairs)


def per_device(ocean_fields, tracers, reaction, wet_levels, neighbours):
    tiles = lax.axis_size("tile")
    nt, lev, cols = tracers.shape
    plan = Plan(nt, lev)
    blocks, window, p_rows = plan.blocks, plan.window, plan.p_rows
    fields = ocean_fields.reshape(-1, lev, cols)
    nf = fields.shape[0]
    top = SUB * (plan.full + 1)
    across, within = swaps(tiles, True), swaps(tiles, False)

    near_shapes = (
        shape_of(nt, window, SUB, cols),
        shape_of(3, window, SUB, cols),
        shape_of(2, window, SUB, cols),
        shape_of(4, blocks, SUB, cols),
        shape_of(3, blocks, SUB, cols),
        shape_of(3, blocks, SUB, cols),
    )
    h_scratch = (pltpu.VMEM((nt, (window + 2) * SUB, cols), F32), pltpu.VMEM(((window + 2) * SUB, cols), F32))
    w_scratch = (pltpu.VMEM((4, (blocks + 2) * SUB, cols), F32), pltpu.VMEM(((blocks + 2) * SUB, cols), F32))
    kernel = lambda f, *more: functools.partial(f, plan, *more)

    p, q, pq, top_fields, chl = call(
        kernel(pack_kernel),
        (
            shape_of(p_rows, cols),
            shape_of(plan.q_rows[0], cols),
            shape_of(p_rows + plan.q_rows[0], cols),
            shape_of(nf, top, cols),
            shape_of(lev, cols),
        ),
        tuple(
            pltpu.with_memory_space_constraint(v, pltpu.HBM) for v in (wet_levels.reshape(1, cols), fields, tracers)
        ),
        specs=[HBM] * 3,
        scratch=[
            pltpu.VMEM((1, cols), jnp.int32),
            pltpu.VMEM((nt, SUB, cols), F32),
            pltpu.SemaphoreType.DMA((2 * nt + 8,)),
        ],
    )
    cross_p = sent(p, across)
    lagged = sent(top_fields, over_comp((1,), tiles))
    core = sent(pq, within)
    cross_q = sent(q, across)
    n = -(-nt // 2) * 2 * SUB
    matrix = call(matrix_kernel, jax.ShapeDtypeStruct((2 * n, n), BF16), (reaction,))

    near = call(
        kernel(near_kernel, False),
        near_shapes,
        (neighbours, fields, lagged, fields, pq, core, chl),
        cost=8_000_000,
    )
    p_one, edge = call(
        kernel(upper_kernel),
        (shape_of(p_rows, cols), shape_of(nt, SUB, cols)),
        (matrix, neighbours, pq, cross_p, *near[:3]),
        scratch=h_scratch,
        cost=8_000_000,
    )
    cross_p_one = sent(p_one, across)
    q_one, pq_one, over_one = call(
        kernel(lower_kernel),
        (shape_of(plan.q_rows[1], cols), shape_of(p_rows + plan.q_rows[1], cols), shape_of(nf, lev, cols)),
        (matrix, neighbours, fields, pq, cross_p, cross_q, *near, p_one, edge),
        scratch=h_scratch + w_scratch,
        cost=8_000_000,
    )
    over = sent(over_one, over_comp((0, 1), tiles))
    core_one = sent(pq_one, within)
    cross_q_one = sent(q_one, across)

    *near, chl_one = call(
        kernel(near_kernel, True),
        near_shapes + (shape_of(lev, cols),),
        (neighbours, over_one, over_one, over, pq_one, core_one, p_one, over),
        cost=8_000_000,
    )
    upper = call(
        kernel(chl_kernel),
        shape_of(top, cols),
        (reaction, neighbours, pq_one, cross_p_one, *near[:3]),
        specs=[SMEM] + [VMEM] * 6,
        scratch=h_scratch,
        cost=8_000_000,
    )
    upper = sent(upper, over_comp((0,), tiles))
    ocean_out, chl_out = call(
        kernel(last_kernel),
        (shape_of(nf, lev, cols), shape_of(lev, cols)),
        (reaction, neighbours, over_one, over, pq_one, cross_p_one, cross_q_one, *near, chl_one, upper),
        specs=[SMEM] + [VMEM] * 14,
        scratch=h_scratch + w_scratch,
        cost=8_000_000,
    )
    return (ocean_out[None], chl_out[None])


def solution(mesh):
    return jax.shard_map(
        per_device,
        mesh=mesh,
        in_specs=(
            P("comp", None, None, "tile"),
            P(None, None, "tile"),
            P(),
            P("tile"),
            P(None, "tile"),
        ),
        out_specs=(P("comp", None, None, "tile"), P("comp", None, "tile")),
        check_vma=False,
    )
```

```python
import functools
import math

import jax
import jax.numpy as jnp
from jax import lax
from jax.experimental import pallas as pl
from jax.experimental.pallas import tpu as pltpu
from jax.sharding import PartitionSpec as P


ROTATE_COS = math.cos(0.3)
ROTATE_SIN = math.sin(0.3)
SUB = 8
AXES = ("comp", "tile")
ANGLES = [2.0 * math.pi * k / 3.0 for k in range(3)]
F32 = jnp.float32
BF16 = jnp.bfloat16
GRANT = 8 << 20


VMEM = pl.BlockSpec(memory_space=pltpu.VMEM)
SMEM = pl.BlockSpec(memory_space=pltpu.SMEM)
HBM = pl.BlockSpec(memory_space=pltpu.HBM)


class Plan:
    def __init__(self, nt, lev):
        self.nt, self.lev = nt, lev
        self.blocks = lev // SUB
        self.full = self.blocks // 2 - 1
        self.window = self.full + 2
        self.half = SUB // 2
        self.halves = SUB * nt * self.full
        self.wet = self.halves + self.half * nt
        self.p_rows = -(-(self.wet + self.half) // SUB) * SUB
        self.q_rows = (
            max(4 * lev, -(-(SUB + self.half) * nt // SUB) * SUB),
            max(4 * lev, 2 * SUB * nt),
        )

    def rs(self, comp):
        return list(range(1 - comp, self.window))

    def level(self, comp, r):
        return SUB * (r - 1) if comp == 0 else SUB * (self.full + r)

    def block(self, comp, second, p, q, j, r):
        if comp == 0:
            return p(SUB * (self.full * j + r - 1)) if r <= self.full else p(self.halves + self.half * j)
        if r < self.full:
            return p(SUB * (self.full * j + r))
        if second:
            return q(SUB * (2 * j + r - self.full))
        if r > self.full:
            return q(SUB * j)
        upper = p(self.halves + self.half * j)
        lower = q(SUB * self.nt + self.half * (j - 1))
        sub = lax.broadcasted_iota(jnp.int32, upper.shape, 0)
        return jnp.where(sub < self.half, upper, lower)


def rows_at(ref, base=0):
    return lambda offset: ref[base + offset : base + offset + SUB, :]


def edge_weights(eastward, northward):
    return [
        0.05 + 0.25 * jax.nn.sigmoid(eastward * math.cos(a) + northward * math.sin(a)) for a in ANGLES
    ]


def take_lanes(block, index):
    return jnp.take_along_axis(block, index, axis=1, mode="promise_in_bounds")


def shape_of(*dims):
    return jax.ShapeDtypeStruct(dims, F32)


def neighbours_of(nb_ref, odd):
    cols = nb_ref.shape[-1]
    core_side = jnp.where(odd == 1, 0, 2)
    index, in_core, in_cross = [], [], []
    for k in range(3):
        nb = jnp.broadcast_to(nb_ref[k : k + 1, :], (SUB, cols))
        side = nb // cols
        index.append(nb - side * cols)
        in_core.append(side == core_side)
        in_cross.append(side == 2 - core_side)
    return index, in_core, in_cross


def level_block(first, cols):
    return lax.broadcasted_iota(jnp.int32, (SUB, cols), 0).astype(F32) + float(first)


def link_weight(level, wet, mixing, last):
    nxt = level + 1.0
    return jnp.where((nxt < wet) & (nxt <= last), 0.02 + 0.13 * jax.nn.sigmoid(mixing), 0.0)


def wet_of(plan, ref):
    return jnp.broadcast_to(ref[plan.wet : plan.wet + 1, :], (SUB, ref.shape[1]))


def on_side(comp):
    return pl.when(lax.axis_index("comp") == comp)


def pack_kernel(plan, wet_ref, f_ref, t_ref, p_ref, q_ref, pq_ref, top_ref, chl_ref, wet_buf, half_buf, sems):
    nt, full, half, lev = plan.nt, plan.full, plan.half, plan.lev
    tall = SUB * full
    first = pl.multiple_of(lax.axis_index("comp") * tall, SUB)
    copies = [
        (t_ref.at[:, pl.ds(first, tall)], p_ref.at[pl.ds(0, plan.halves)].reshape(nt, tall, p_ref.shape[1])),
        (t_ref.at[:, pl.ds(pl.multiple_of(first + tall, SUB), SUB)], half_buf),
        (wet_ref, wet_buf),
        (f_ref.at[:, pl.ds(0, top_ref.shape[1])], top_ref),
        (t_ref.at[0], chl_ref),
    ]
    copies = [pltpu.make_async_copy(s, d, sems.at[i]) for i, (s, d) in enumerate(copies)]
    for c in copies:
        c.start()
    base = len(copies)
    slab = lambda n, rows: q_ref.at[pl.ds(0, n * rows)].reshape(n, rows, q_ref.shape[1])
    ocean = [pltpu.make_async_copy(f_ref.at[pl.ds(0, 4)], slab(4, lev), sems.at[base])]
    deep = [pltpu.make_async_copy(t_ref.at[:, pl.ds(lev - SUB, SUB)], slab(nt, SUB), sems.at[base])]

    @on_side(0)
    def _():
        for c in ocean:
            c.start()

    @on_side(1)
    def _():
        for c in deep:
            c.start()

    for c in copies:
        c.wait()
    p_ref[plan.wet : plan.wet + half, :] = jnp.broadcast_to(wet_buf[...].astype(F32), (half, wet_buf.shape[1]))
    for j in range(nt):
        p_ref[plan.halves + half * j : plan.halves + half * (j + 1), :] = half_buf[j, 0:half, :]

    @on_side(0)
    def _():
        for c in ocean:
            c.wait()

    @on_side(1)
    def _():
        for c in deep:
            c.wait()
        for j in range(nt):
            at = SUB * nt + half * j
            q_ref[at : at + half, :] = half_buf[j, half:SUB, :]

    pq_ref[0 : plan.p_rows, :] = p_ref[...]
    pq_ref[plan.p_rows :, :] = q_ref[...]


def matrix_kernel(r_ref, out_ref, first_ref):
    nt = r_ref.shape[0]
    rows, n = out_ref.shape
    p = lax.broadcasted_iota(jnp.int32, (n, nt), 0)
    spread = (p // SUB == lax.broadcasted_iota(jnp.int32, (n, nt), 1)).astype(F32)
    exact = functools.partial(
        lax.dot_general, precision=lax.Precision.HIGHEST, preferred_element_type=F32
    )
    tall = exact(spread, r_ref[...], (((1,), (0,)), ((), ())))
    full = exact(tall, spread, (((1,), (1,)), ((), ())))
    a = lax.broadcasted_iota(jnp.int32, (n, n), 0)
    b = lax.broadcasted_iota(jnp.int32, (n, n), 1)
    full = jnp.where(a % SUB == b % SUB, full, 0.0)
    high = full.astype(BF16)
    out_ref[0:n, :] = high
    out_ref[n:rows, :] = (full - high.astype(F32)).astype(BF16)
    ones = jnp.ones((1, first_ref.shape[1]), F32)
    first_ref[...] = exact(r_ref[0:1, :], ones, (((0,), (0,)), ((), ())))


def near_kernel(plan, second, nb_ref, f_ref, ga_ref, gb_ref, pq_ref, core_ref, chl_ref, *refs):
    if second:
        chl_low_ref, *refs = refs
    part_ref, far_ref, aux_ref, opart_ref, ofar_ref, oaux_ref = refs[:6]
    chl_out_ref = refs[6] if second else None
    odd = lax.axis_index("tile") % 2
    cols = nb_ref.shape[-1]
    nt, p_rows = plan.nt, plan.p_rows
    index, in_core, in_cross = neighbours_of(nb_ref, odd)
    wet, wet_core = wet_of(plan, pq_ref), wet_of(plan, core_ref)
    near_wet = []
    for k in range(3):
        found = jnp.where(in_core[k], take_lanes(wet_core, index[k]), take_lanes(wet, index[k]))
        near_wet.append(jnp.where(in_cross[k], 0.0, found))
    last = float(plan.lev - 1)

    def split(level, ws):
        active = level < wet
        near = [jnp.where(active & (level < near_wet[k]), ws[k], 0.0) for k in range(3)]
        far = [jnp.where(active & in_cross[k], ws[k], 0.0) for k in range(3)]
        return near, far

    def moves(own, core, near, rest):
        totals = [o * r for o, r in zip(own, rest)]
        for k in range(3):
            for j in range(len(own)):
                v = jnp.where(in_core[k], take_lanes(core[j], index[k]), take_lanes(own[j], index[k]))
                totals[j] = totals[j] + near[j][k] * v
        return totals

    def tracers(comp):
        for r in plan.rs(comp):
            first = plan.level(comp, r)
            level = level_block(first, cols)
            g_first = first - SUB * plan.full if comp and second else first
            g = [(gb_ref if comp else ga_ref)[i, g_first : g_first + SUB, :] for i in range(6)]
            near, far = split(level, edge_weights(g[2], g[3]))
            rest = 1.0 - (near[0] + near[1] + near[2])
            for k in range(3):
                far_ref[k, r] = far[k]
            aux_ref[0, r] = link_weight(level, wet, g[4], last)
            aux_ref[1, r] = 0.5 * g[5] * jax.nn.sigmoid(g[0] + 0.5 * g[1])
            own = [plan.block(comp, second, rows_at(pq_ref), rows_at(pq_ref, p_rows), j, r) for j in range(nt)]
            core = [plan.block(comp, second, rows_at(core_ref), rows_at(core_ref, p_rows), j, r) for j in range(nt)]
            for j, v in enumerate(moves(own, core, [near] * nt, [rest] * nt)):
                part_ref[j, r] = v

    @on_side(1)
    def _():
        tracers(1)

    @on_side(0)
    def _():
        tracers(0)
        top = f_ref[5, 0:1, :]
        cut = SUB * (plan.full + 1) - SUB + 2

        def chl_block(b):
            at = SUB * b
            if not second:
                return chl_ref[at : at + SUB, :]
            if b < plan.full:
                return chl_ref[at : at + SUB, :]
            v = chl_low_ref[0, at - SUB * plan.full : at - SUB * plan.full + SUB, :]
            if b > plan.full:
                return v
            return jnp.where(level_block(at, cols) < float(cut), chl_ref[plan.halves : plan.halves + SUB, :], v)

        run = jnp.zeros((1, cols), F32)
        for b in range(plan.blocks):
            x = chl_block(b)
            if second:
                chl_out_ref[SUB * b : SUB * (b + 1), :] = x
            absorbed = 0.01 + 0.3 * (jnp.maximum(x, 0.0) + jnp.log1p(jnp.exp(-jnp.abs(x))))
            level = level_block(SUB * b, cols)
            sub = lax.broadcasted_iota(jnp.int32, (SUB, cols), 0)
            cum = absorbed
            for d in (1, 2, 4):
                cum = cum + jnp.where(sub >= d, pltpu.roll(cum, d, 0), 0.0)
            depth = cum + run
            ceiling = jnp.exp(-(depth - absorbed))
            oaux_ref[1, b] = 4.0 * top * (ceiling - jnp.exp(-depth))
            oaux_ref[2, b] = jnp.where(level < wet, top * ceiling, 0.0)
            run = depth[SUB - 1 : SUB, :]

        for b in range(plan.blocks):
            at = SUB * b
            level = level_block(at, cols)
            f = [f_ref[i, at : at + SUB, :] for i in range(5)]
            near, far = split(level, edge_weights(f[2], f[3]))
            rest = 1.0 - (near[0] + near[1] + near[2])
            flat = [jnp.where(v > 0.0, 0.15, 0.0) for v in near]
            rest_flat = 1.0 - (flat[0] + flat[1] + flat[2])
            for k in range(3):
                ofar_ref[k, b] = far[k]
            oaux_ref[0, b] = link_weight(level, wet, f[4], last)
            core = [rows_at(core_ref, p_rows)(plan.lev * i + at) for i in range(4)]
            out = moves(f[:4], core, [near, near, flat, flat], [rest, rest, rest_flat, rest_flat])
            for i in range(4):
                opart_ref[i, b] = out[i]


def far_wet(index, in_cross, wet_cross):
    return [jnp.where(in_cross[k], take_lanes(wet_cross, index[k]), 0.0) for k in range(3)]


def far_moves(parts, own, cross, far, index):
    totals = [p - o * (f[0] + f[1] + f[2]) for p, o, f in zip(parts, own, far)]
    for k in range(3):
        for j in range(len(own)):
            totals[j] = totals[j] + far[j][k] * take_lanes(cross[j], index[k])
    return totals


class Far:
    def __init__(self, plan, comp, second, nb_ref, pq_ref, cross_p_ref, part_ref, far_ref, aux_ref, h_ref, l_ref):
        self.plan, self.comp, self.second = plan, comp, second
        self.cols = nb_ref.shape[-1]
        self.own_p, self.own_q = rows_at(pq_ref), rows_at(pq_ref, plan.p_rows)
        self.part, self.far, self.aux, self.h, self.l = part_ref, far_ref, aux_ref, h_ref, l_ref
        self.index, _, in_cross = neighbours_of(nb_ref, lax.axis_index("tile") % 2)
        self.wet = wet_of(plan, pq_ref)
        self.wets = far_wet(self.index, in_cross, wet_of(plan, cross_p_ref))

    def at(self, r):
        return SUB * (r + 1)

    def clear(self, before, after):
        zero = jnp.zeros((SUB, self.cols), F32)
        if before is not None:
            self.l[self.at(before) : self.at(before) + SUB, :] = zero
        for j in range(self.plan.nt):
            for r in (before, after):
                if r is not None:
                    self.h[j, self.at(r) : self.at(r) + SUB, :] = zero

    def move(self, r, p, q):
        plan, at = self.plan, self.at(r)
        level = level_block(plan.level(self.comp, r), self.cols)
        far = [jnp.where(level < self.wets[k], self.far[k, r], 0.0) for k in range(3)]
        self.l[at : at + SUB, :] = self.aux[0, r]
        js = range(plan.nt)
        parts = [self.part[j, r] for j in js]
        own = [plan.block(self.comp, self.second, self.own_p, self.own_q, j, r) for j in js]
        cross = [plan.block(self.comp, self.second, p, q, j, r) for j in js]
        for j, v in enumerate(far_moves(parts, own, cross, [far] * plan.nt, self.index)):
            self.h[j, at : at + SUB, :] = v

    def react(self, r, react_ref, put):
        plan, at = self.plan, self.at(r)
        active = (level_block(plan.level(self.comp, r), self.cols) < self.wet).astype(F32)
        down, up = self.l[at : at + SUB, :], self.l[at - 1 : at - 1 + SUB, :]
        ys, ts = [], []
        for j in range(plan.nt):
            v = self.h[j, at : at + SUB, :]
            y = v + down * (self.h[j, at + 1 : at + 1 + SUB, :] - v) - up * (v - self.h[j, at - 1 : at - 1 + SUB, :])
            ys.append(y)
            ts.append(jnp.tanh(y))
        growth = self.aux[1, r]
        if self.second:
            total = react_ref[0:1, :] * ts[0]
            for j in range(1, plan.nt):
                total = total + react_ref[j : j + 1, :] * ts[j]
            put(0, r, (ys[0] + growth * total) * active)
            return
        n = react_ref.shape[1]
        ts += [jnp.zeros_like(ts[0])] * (n // SUB - plan.nt)
        stack = jnp.concatenate(ts, axis=0)
        high = stack.astype(BF16)
        rest = (stack - high.astype(F32)).astype(BF16)
        both = jnp.dot(react_ref[...], high, preferred_element_type=F32)
        total = both[:n] + both[n:] + jnp.dot(react_ref[0:n, :], rest, preferred_element_type=F32)
        for i in range(plan.nt):
            put(i, r, (ys[i] + growth * total[i * SUB : (i + 1) * SUB]) * active)


def nothing(offset):
    raise ValueError("not there")


def upper_kernel(plan, react_ref, nb_ref, pq_ref, p_ref, part_ref, far_ref, aux_ref, out_ref, edge_ref, h_ref, l_ref):
    out_ref[plan.wet : plan.wet + plan.half, :] = pq_ref[plan.wet : plan.wet + plan.half, :]
    refs = (nb_ref, pq_ref, p_ref, part_ref, far_ref, aux_ref, h_ref, l_ref)
    p = rows_at(p_ref)

    @on_side(0)
    def _():
        work = Far(plan, 0, False, *refs)
        work.clear(0, plan.window)
        for r in plan.rs(0):
            work.move(r, p, nothing)

        def put(i, r, value):
            if r <= plan.full:
                at = SUB * (plan.full * i + r - 1)
                out_ref[at : at + SUB, :] = value
            else:
                at = plan.halves + plan.half * i
                out_ref[at : at + plan.half, :] = value[0 : plan.half]

        for r in plan.rs(0):
            work.react(r, react_ref, put)

    @on_side(1)
    def _():
        work = Far(plan, 1, False, *refs)
        work.clear(-1, None)
        lower = lambda offset: jnp.zeros((SUB, work.cols), F32)
        for r in range(plan.full + 1):
            work.move(r, p, lower)
        at = work.at(plan.full - 1)
        for j in range(plan.nt):
            edge_ref[j] = h_ref[j, at : at + SUB, :]

        def put(i, r, value):
            at = SUB * (plan.full * i + r)
            out_ref[at : at + SUB, :] = value

        for r in range(plan.full):
            work.react(r, react_ref, put)


def ocean_far(plan, nb_ref, f_ref, pq_ref, p_ref, q_ref, opart_ref, ofar_ref, oaux_ref, w_ref, l_ref, put):
    cols = nb_ref.shape[-1]
    index, _, in_cross = neighbours_of(nb_ref, lax.axis_index("tile") % 2)
    wet = wet_of(plan, pq_ref)
    wets = far_wet(index, in_cross, wet_of(plan, p_ref))
    zero = jnp.zeros((SUB, cols), F32)
    end = SUB * (plan.blocks + 1)
    l_ref[0:SUB, :] = zero
    for i in range(4):
        w_ref[i, 0:SUB, :] = zero
        w_ref[i, end : end + SUB, :] = zero
    for b in range(plan.blocks):
        at = SUB * b
        level = level_block(at, cols)
        far = [jnp.where(level < wets[k], ofar_ref[k, b], 0.0) for k in range(3)]
        flat = [jnp.where(v > 0.0, 0.15, 0.0) for v in far]
        there = slice(at + SUB, at + 2 * SUB)
        l_ref[there, :] = oaux_ref[0, b]
        parts = [opart_ref[i, b] for i in range(4)]
        own = [f_ref[i, at : at + SUB, :] for i in range(4)]
        cross = [rows_at(q_ref)(plan.lev * i + at) for i in range(4)]
        q = far_moves(parts, own, cross, [far, far, flat, flat], index)
        w_ref[0, there, :] = q[0]
        w_ref[1, there, :] = q[1]
        w_ref[2, there, :] = ROTATE_COS * q[2] + ROTATE_SIN * q[3]
        w_ref[3, there, :] = -ROTATE_SIN * q[2] + ROTATE_COS * q[3]
    warm = [None] * plan.blocks
    for b in range(plan.blocks):
        at = SUB * (b + 1)
        active = (level_block(SUB * b, cols) < wet).astype(F32)
        down, up = l_ref[at : at + SUB, :], l_ref[at - 1 : at - 1 + SUB, :]
        for i in range(4):
            v = w_ref[i, at : at + SUB, :]
            y = v + down * (w_ref[i, at + 1 : at + 1 + SUB, :] - v) - up * (v - w_ref[i, at - 1 : at - 1 + SUB, :])
            if i == 0:
                warm[b] = y + oaux_ref[1, b]
                put(0, b, warm[b] * active)
            else:
                put(i, b, y * active)
        put(5, b, oaux_ref[2, b])
    sub = lax.broadcasted_iota(jnp.int32, (SUB, cols), 0)
    for b in range(plan.blocks):
        active = (level_block(SUB * b, cols) < wet).astype(F32)
        lower = pltpu.roll(warm[b], SUB - 1, 0)
        if b + 1 < plan.blocks:
            lower = jnp.where(sub == SUB - 1, pltpu.roll(warm[b + 1], SUB - 1, 0), lower)
        else:
            lower = jnp.where(sub == SUB - 1, warm[b], lower)
        put(4, b, (warm[b] - lower) * active)


def lower_kernel(
    plan, react_ref, nb_ref, f_ref, pq_ref, p_ref, q_ref, part_ref, far_ref, aux_ref, opart_ref, ofar_ref, oaux_ref,
    done_ref, edge_ref, out_ref, both_ref, ocean_ref, over_ref, rest_ref, h_ref, l_ref, w_ref, wl_ref,
):
    both_ref[0 : plan.p_rows, :] = done_ref[...]

    @on_side(0)
    def _():
        def put(i, b, value):
            at = SUB * b
            ocean_ref[i, at : at + SUB, :] = value
            if b < plan.full:
                rest_ref[i, at : at + SUB, :] = value
            else:
                over_ref[i, at - SUB * plan.full : at - SUB * plan.full + SUB, :] = value
            if i < 4:
                for ref, base in ((out_ref, 0), (both_ref, plan.p_rows)):
                    ref[base + plan.lev * i + at : base + plan.lev * i + at + SUB, :] = value

        ocean_far(plan, nb_ref, f_ref, pq_ref, p_ref, q_ref, opart_ref, ofar_ref, oaux_ref, w_ref, wl_ref, put)

    @on_side(1)
    def _():
        work = Far(plan, 1, False, nb_ref, pq_ref, p_ref, part_ref, far_ref, aux_ref, h_ref, l_ref)
        work.clear(None, plan.window)
        before = work.at(plan.full - 1)
        l_ref[before : before + SUB, :] = aux_ref[0, plan.full - 1]
        for j in range(plan.nt):
            h_ref[j, before : before + SUB, :] = edge_ref[j]
        rs = (plan.full, plan.full + 1)
        for r in rs:
            work.move(r, rows_at(p_ref), rows_at(q_ref))

        def put(i, r, value):
            at = SUB * (2 * i + r - plan.full)
            out_ref[at : at + SUB, :] = value
            both_ref[plan.p_rows + at : plan.p_rows + at + SUB, :] = value
            if i == 0:
                over_ref[0, SUB * r : SUB * (r + 1), :] = value

        for r in rs:
            work.react(r, react_ref, put)
        for r in range(plan.full):
            over_ref[0, SUB * r : SUB * (r + 1), :] = done_ref[SUB * r : SUB * (r + 1), :]


def chl_kernel(plan, react_ref, nb_ref, pq_ref, p_ref, part_ref, far_ref, aux_ref, out_ref, h_ref, l_ref):
    @on_side(0)
    def _():
        work = Far(plan, 0, True, nb_ref, pq_ref, p_ref, part_ref, far_ref, aux_ref, h_ref, l_ref)
        work.clear(0, plan.window)
        for r in plan.rs(0):
            work.move(r, rows_at(p_ref), nothing)

        def put(i, r, value):
            out_ref[SUB * (r - 1) : SUB * r, :] = value

        for r in plan.rs(0):
            work.react(r, react_ref, put)


def second_kernel(
    plan, react_ref, nb_ref, f_ref, over_ref, rest_ref, pq_ref, p_ref, q_ref, part_ref, far_ref, aux_ref, opart_ref,
    ofar_ref, oaux_ref, out_ref, mine_ref, h_ref, l_ref, w_ref, wl_ref,
):
    @on_side(0)
    def _():
        def put(i, b, value):
            out_ref[i, SUB * b : SUB * (b + 1), :] = value

        ocean_far(plan, nb_ref, f_ref, pq_ref, p_ref, q_ref, opart_ref, ofar_ref, oaux_ref, w_ref, wl_ref, put)

    @on_side(1)
    def _():
        tall = SUB * plan.full
        out_ref[:, 0:tall, :] = rest_ref[...]
        out_ref[:, tall:, :] = over_ref[...]
        work = Far(plan, 1, True, nb_ref, pq_ref, p_ref, part_ref, far_ref, aux_ref, h_ref, l_ref)
        work.clear(-1, plan.window)
        for r in plan.rs(1):
            work.move(r, rows_at(p_ref), rows_at(q_ref))

        def put(i, r, value):
            mine_ref[SUB * r : SUB * (r + 1), :] = value

        for r in plan.rs(1):
            work.react(r, react_ref, put)


def merge_kernel(plan, chl_ref, mine_ref, upper_ref, out_ref):
    @on_side(0)
    def _():
        out_ref[...] = chl_ref[...]

    @on_side(1)
    def _():
        tall = SUB * plan.full
        sub = lax.broadcasted_iota(jnp.int32, (SUB, out_ref.shape[1]), 0)
        out_ref[0:tall, :] = upper_ref[0:tall, :]
        out_ref[tall : tall + SUB, :] = jnp.where(sub < 2, upper_ref[tall : tall + SUB, :], mine_ref[0:SUB, :])
        out_ref[tall + SUB :, :] = mine_ref[SUB:, :]


def call(kernel, outs, ins, specs=None, scratch=(), cost=1_000_000):
    return pl.pallas_call(
        kernel,
        out_shape=outs,
        in_specs=specs or [VMEM] * len(ins),
        out_specs=jax.tree.map(lambda _: VMEM, outs),
        scratch_shapes=list(scratch),
        compiler_params=pltpu.CompilerParams(vmem_limit_bytes=GRANT),
        cost_estimate=pl.CostEstimate(flops=cost, bytes_accessed=1_000_000, transcendentals=0),
    )(*ins)


def swaps(tiles, across):
    pairs = []
    for c in (0, 1):
        for t in range(tiles):
            other = (t + 1) % tiles if (t % 2 == 0) != across else (t - 1) % tiles
            pairs.append((c * tiles + t, c * tiles + other))
    return pairs


def over_comp(sources, tiles):
    return [(c * tiles + t, (1 - c) * tiles + t) for c in sources for t in range(tiles)]


def sent(v, pairs):
    return lax.ppermute(v, AXES, pairs)


def per_device(ocean_fields, tracers, reaction, wet_levels, neighbours):
    tiles = lax.axis_size("tile")
    nt, lev, cols = tracers.shape
    plan = Plan(nt, lev)
    blocks, window, p_rows = plan.blocks, plan.window, plan.p_rows
    fields = ocean_fields.reshape(-1, lev, cols)
    nf = fields.shape[0]
    top, tall = SUB * (plan.full + 1), SUB * plan.full
    across, within = swaps(tiles, True), swaps(tiles, False)

    near_shapes = (
        shape_of(nt, window, SUB, cols),
        shape_of(3, window, SUB, cols),
        shape_of(2, window, SUB, cols),
        shape_of(4, blocks, SUB, cols),
        shape_of(3, blocks, SUB, cols),
        shape_of(3, blocks, SUB, cols),
    )
    h_scratch = (pltpu.VMEM((nt, (window + 2) * SUB, cols), F32), pltpu.VMEM(((window + 2) * SUB, cols), F32))
    w_scratch = (pltpu.VMEM((4, (blocks + 2) * SUB, cols), F32), pltpu.VMEM(((blocks + 2) * SUB, cols), F32))
    kernel = lambda f, *more: functools.partial(f, plan, *more)

    p, q, pq, top_fields, chl = call(
        kernel(pack_kernel),
        (
            shape_of(p_rows, cols),
            shape_of(plan.q_rows[0], cols),
            shape_of(p_rows + plan.q_rows[0], cols),
            shape_of(nf, top, cols),
            shape_of(lev, cols),
        ),
        tuple(
            pltpu.with_memory_space_constraint(v, pltpu.HBM) for v in (wet_levels.reshape(1, cols), fields, tracers)
        ),
        specs=[HBM] * 3,
        scratch=[
            pltpu.VMEM((1, cols), jnp.int32),
            pltpu.VMEM((nt, SUB, cols), F32),
            pltpu.SemaphoreType.DMA((6,)),
        ],
    )
    cross_p = sent(p, across)
    lagged = sent(top_fields, over_comp((1,), tiles))
    core = sent(pq, within)
    cross_q = sent(q, across)
    n = -(-nt // 2) * 2 * SUB
    matrix, rates = call(
        matrix_kernel, (jax.ShapeDtypeStruct((2 * n, n), BF16), shape_of(nt, cols)), (reaction,)
    )

    near = call(
        kernel(near_kernel, False),
        near_shapes,
        (neighbours, fields, lagged, fields, pq, core, chl),
        cost=8_000_000,
    )
    p_one, edge = call(
        kernel(upper_kernel),
        (shape_of(p_rows, cols), shape_of(nt, SUB, cols)),
        (matrix, neighbours, pq, cross_p, *near[:3]),
        scratch=h_scratch,
        cost=8_000_000,
    )
    cross_p_one = sent(p_one, across)
    q_one, pq_one, ocean_one, over_one, rest_one = call(
        kernel(lower_kernel),
        (
            shape_of(plan.q_rows[1], cols),
            shape_of(p_rows + plan.q_rows[1], cols),
            shape_of(nf, lev, cols),
            shape_of(nf, lev - tall, cols),
            shape_of(nf, tall, cols),
        ),
        (matrix, neighbours, fields, pq, cross_p, cross_q, *near, p_one, edge),
        scratch=h_scratch + w_scratch,
        cost=8_000_000,
    )
    over = sent(over_one, over_comp((0, 1), tiles))
    core_one = sent(pq_one, within)
    cross_q_one = sent(q_one, across)
    rest = sent(rest_one, over_comp((0,), tiles))

    *near, chl_one = call(
        kernel(near_kernel, True),
        near_shapes + (shape_of(lev, cols),),
        (neighbours, ocean_one, ocean_one, over, pq_one, core_one, p_one, over),
        cost=8_000_000,
    )
    upper = call(
        kernel(chl_kernel),
        shape_of(top, cols),
        (rates, neighbours, pq_one, cross_p_one, *near[:3]),
        scratch=h_scratch,
        cost=8_000_000,
    )
    upper = sent(upper, over_comp((0,), tiles))
    ocean_out, mine = call(
        kernel(second_kernel),
        (shape_of(nf, lev, cols), shape_of(lev - tall, cols)),
        (rates, neighbours, ocean_one, over, rest, pq_one, cross_p_one, cross_q_one, *near),
        scratch=h_scratch + w_scratch,
        cost=8_000_000,
    )
    chl_out = call(kernel(merge_kernel), shape_of(lev, cols), (chl_one, mine, upper))
    return (ocean_out[None], chl_out[None])


def solution(mesh):
    return jax.shard_map(
        per_device,
        mesh=mesh,
        in_specs=(
            P("comp", None, None, "tile"),
            P(None, None, "tile"),
            P(),
            P("tile"),
            P(None, "tile"),
        ),
        out_specs=(P("comp", None, None, "tile"), P("comp", None, "tile")),
        check_vma=False,
    )
```

```python
import functools
import math

import jax
import jax.numpy as jnp
from jax import lax
from jax.experimental import pallas as pl
from jax.experimental.pallas import tpu as pltpu
from jax.sharding import PartitionSpec as P


ROTATE_COS = math.cos(0.3)
ROTATE_SIN = math.sin(0.3)
SUB = 8
AXES = ("comp", "tile")
ANGLES = [2.0 * math.pi * k / 3.0 for k in range(3)]
F32 = jnp.float32
BF16 = jnp.bfloat16
GRANT = 8 << 20


VMEM = pl.BlockSpec(memory_space=pltpu.VMEM)
SMEM = pl.BlockSpec(memory_space=pltpu.SMEM)
HBM = pl.BlockSpec(memory_space=pltpu.HBM)


class Plan:
    def __init__(self, nt, lev):
        self.nt, self.lev = nt, lev
        self.blocks = lev // SUB
        self.full = self.blocks // 2 - 1
        self.window = self.full + 2
        self.half = SUB // 2
        self.halves = SUB * nt * self.full
        self.wet = self.halves + self.half * nt
        self.p_rows = -(-(self.wet + self.half) // SUB) * SUB
        self.q_rows = (
            max(4 * lev, -(-(SUB + self.half) * nt // SUB) * SUB),
            max(4 * lev, 2 * SUB * nt),
        )

    def rs(self, comp):
        return list(range(1 - comp, self.window))

    def level(self, comp, r):
        return SUB * (r - 1) if comp == 0 else SUB * (self.full + r)

    def block(self, comp, second, p, q, j, r):
        if comp == 0:
            return p(SUB * (self.full * j + r - 1)) if r <= self.full else p(self.halves + self.half * j)
        if r < self.full:
            return p(SUB * (self.full * j + r))
        if second:
            return q(SUB * (2 * j + r - self.full))
        if r > self.full:
            return q(SUB * j)
        upper = p(self.halves + self.half * j)
        lower = q(SUB * self.nt + self.half * (j - 1))
        sub = lax.broadcasted_iota(jnp.int32, upper.shape, 0)
        return jnp.where(sub < self.half, upper, lower)


def rows_at(ref, base=0):
    return lambda offset: ref[base + offset : base + offset + SUB, :]


def edge_weights(eastward, northward):
    return [
        0.05 + 0.25 * jax.nn.sigmoid(eastward * math.cos(a) + northward * math.sin(a)) for a in ANGLES
    ]


def take_lanes(block, index):
    return jnp.take_along_axis(block, index, axis=1, mode="promise_in_bounds")


def shape_of(*dims):
    return jax.ShapeDtypeStruct(dims, F32)


def neighbours_of(nb_ref, odd):
    cols = nb_ref.shape[-1]
    core_side = jnp.where(odd == 1, 0, 2)
    index, in_core, in_cross = [], [], []
    for k in range(3):
        nb = jnp.broadcast_to(nb_ref[k : k + 1, :], (SUB, cols))
        side = nb // cols
        index.append(nb - side * cols)
        in_core.append(side == core_side)
        in_cross.append(side == 2 - core_side)
    return index, in_core, in_cross


def level_block(first, cols):
    return lax.broadcasted_iota(jnp.int32, (SUB, cols), 0).astype(F32) + float(first)


def link_weight(level, wet, mixing, last):
    nxt = level + 1.0
    return jnp.where((nxt < wet) & (nxt <= last), 0.02 + 0.13 * jax.nn.sigmoid(mixing), 0.0)


def growth_rate(temperature, salinity, light):
    return 0.5 * light * jax.nn.sigmoid(temperature + 0.5 * salinity)


def wet_of(plan, ref):
    return jnp.broadcast_to(ref[plan.wet : plan.wet + 1, :], (SUB, ref.shape[1]))


def on_side(comp):
    return pl.when(lax.axis_index("comp") == comp)


def pack_kernel(plan, wet_ref, f_ref, t_ref, p_ref, q_ref, pq_ref, top_ref, chl_ref, wet_buf, half_buf, top_buf, sems):
    nt, full, half, lev = plan.nt, plan.full, plan.half, plan.lev
    tall = SUB * full
    first = pl.multiple_of(lax.axis_index("comp") * tall, SUB)
    copies = [
        (t_ref.at[:, pl.ds(first, tall)], p_ref.at[pl.ds(0, plan.halves)].reshape(nt, tall, p_ref.shape[1])),
        (t_ref.at[:, pl.ds(pl.multiple_of(first + tall, SUB), SUB)], half_buf),
        (wet_ref, wet_buf),
        (f_ref.at[:, pl.ds(0, top_ref.shape[1])], top_buf),
        (t_ref.at[0], chl_ref),
    ]
    copies = [pltpu.make_async_copy(s, d, sems.at[i]) for i, (s, d) in enumerate(copies)]
    for c in copies:
        c.start()
    base = len(copies)
    slab = lambda n, rows: q_ref.at[pl.ds(0, n * rows)].reshape(n, rows, q_ref.shape[1])
    ocean = [pltpu.make_async_copy(f_ref.at[pl.ds(0, 4)], slab(4, lev), sems.at[base])]
    deep = [pltpu.make_async_copy(t_ref.at[:, pl.ds(lev - SUB, SUB)], slab(nt, SUB), sems.at[base])]

    @on_side(0)
    def _():
        for c in ocean:
            c.start()

    @on_side(1)
    def _():
        for c in deep:
            c.start()

    for c in copies:
        c.wait()
    p_ref[plan.wet : plan.wet + half, :] = jnp.broadcast_to(wet_buf[...].astype(F32), (half, wet_buf.shape[1]))
    for j in range(nt):
        p_ref[plan.halves + half * j : plan.halves + half * (j + 1), :] = half_buf[j, 0:half, :]

    @on_side(0)
    def _():
        for c in ocean:
            c.wait()

    @on_side(1)
    def _():
        for c in deep:
            c.wait()
        top_ref[0] = growth_rate(top_buf[0], top_buf[1], top_buf[5])
        top_ref[1:4] = top_buf[2:5]
        for j in range(nt):
            at = SUB * nt + half * j
            q_ref[at : at + half, :] = half_buf[j, half:SUB, :]

    pq_ref[0 : plan.p_rows, :] = p_ref[...]
    pq_ref[plan.p_rows :, :] = q_ref[...]


def matrix_kernel(r_ref, out_ref, first_ref):
    nt = r_ref.shape[0]
    rows, n = out_ref.shape
    p = lax.broadcasted_iota(jnp.int32, (n, nt), 0)
    spread = (p // SUB == lax.broadcasted_iota(jnp.int32, (n, nt), 1)).astype(F32)
    exact = functools.partial(
        lax.dot_general, precision=lax.Precision.HIGHEST, preferred_element_type=F32
    )
    tall = exact(spread, r_ref[...], (((1,), (0,)), ((), ())))
    full = exact(tall, spread, (((1,), (1,)), ((), ())))
    a = lax.broadcasted_iota(jnp.int32, (n, n), 0)
    b = lax.broadcasted_iota(jnp.int32, (n, n), 1)
    full = jnp.where(a % SUB == b % SUB, full, 0.0)
    high = full.astype(BF16)
    out_ref[0:n, :] = high
    out_ref[n:rows, :] = (full - high.astype(F32)).astype(BF16)
    ones = jnp.ones((1, first_ref.shape[1]), F32)
    first_ref[...] = exact(r_ref[0:1, :], ones, (((0,), (0,)), ((), ())))


def near_kernel(plan, second, nb_ref, f_ref, ga_ref, gb_ref, pq_ref, core_ref, chl_ref, *refs):
    if second:
        chl_low_ref, *refs = refs
    part_ref, far_ref, aux_ref, opart_ref, ofar_ref, oaux_ref = refs[:6]
    chl_out_ref = refs[6] if second else None
    odd = lax.axis_index("tile") % 2
    cols = nb_ref.shape[-1]
    nt, p_rows = plan.nt, plan.p_rows
    index, in_core, in_cross = neighbours_of(nb_ref, odd)
    wet, wet_core = wet_of(plan, pq_ref), wet_of(plan, core_ref)
    near_wet = []
    for k in range(3):
        found = jnp.where(in_core[k], take_lanes(wet_core, index[k]), take_lanes(wet, index[k]))
        near_wet.append(jnp.where(in_cross[k], 0.0, found))
    last = float(plan.lev - 1)

    def split(level, ws):
        active = level < wet
        near = [jnp.where(active & (level < near_wet[k]), ws[k], 0.0) for k in range(3)]
        far = [jnp.where(active & in_cross[k], ws[k], 0.0) for k in range(3)]
        return near, far

    def moves(own, core, near, rest):
        totals = [o * r for o, r in zip(own, rest)]
        for k in range(3):
            for j in range(len(own)):
                v = jnp.where(in_core[k], take_lanes(core[j], index[k]), take_lanes(own[j], index[k]))
                totals[j] = totals[j] + near[j][k] * v
        return totals

    def tracers(comp):
        for r in plan.rs(comp):
            first = plan.level(comp, r)
            level = level_block(first, cols)
            passed = comp == int(second)
            ref, at = (gb_ref if comp else ga_ref), first - SUB * plan.full * int(passed and comp)
            g = [ref[i, at : at + SUB, :] for i in range(4 if passed else 6)]
            if not passed:
                g = [growth_rate(g[0], g[1], g[5])] + g[2:5]
            near, far = split(level, edge_weights(g[1], g[2]))
            rest = 1.0 - (near[0] + near[1] + near[2])
            for k in range(3):
                far_ref[k, r] = far[k]
            aux_ref[0, r] = link_weight(level, wet, g[3], last)
            aux_ref[1, r] = g[0]
            own = [plan.block(comp, second, rows_at(pq_ref), rows_at(pq_ref, p_rows), j, r) for j in range(nt)]
            core = [plan.block(comp, second, rows_at(core_ref), rows_at(core_ref, p_rows), j, r) for j in range(nt)]
            for j, v in enumerate(moves(own, core, [near] * nt, [rest] * nt)):
                part_ref[j, r] = v

    @on_side(1)
    def _():
        tracers(1)

    @on_side(0)
    def _():
        tracers(0)
        top = f_ref[5, 0:1, :]
        cut = SUB * (plan.full + 1) - SUB + 2

        def chl_block(b):
            at = SUB * b
            if not second:
                return chl_ref[at : at + SUB, :]
            if b < plan.full:
                return chl_ref[at : at + SUB, :]
            v = chl_low_ref[0, at - SUB * plan.full : at - SUB * plan.full + SUB, :]
            if b > plan.full:
                return v
            return jnp.where(level_block(at, cols) < float(cut), chl_ref[plan.halves : plan.halves + SUB, :], v)

        run = jnp.zeros((1, cols), F32)
        for b in range(plan.blocks):
            x = chl_block(b)
            if second:
                chl_out_ref[SUB * b : SUB * (b + 1), :] = x
            absorbed = 0.01 + 0.3 * (jnp.maximum(x, 0.0) + jnp.log1p(jnp.exp(-jnp.abs(x))))
            level = level_block(SUB * b, cols)
            sub = lax.broadcasted_iota(jnp.int32, (SUB, cols), 0)
            cum = absorbed
            for d in (1, 2, 4):
                cum = cum + jnp.where(sub >= d, pltpu.roll(cum, d, 0), 0.0)
            depth = cum + run
            ceiling = jnp.exp(-(depth - absorbed))
            oaux_ref[1, b] = 4.0 * top * (ceiling - jnp.exp(-depth))
            oaux_ref[2, b] = jnp.where(level < wet, top * ceiling, 0.0)
            run = depth[SUB - 1 : SUB, :]

        for b in range(plan.blocks):
            at = SUB * b
            level = level_block(at, cols)
            f = [f_ref[i, at : at + SUB, :] for i in range(5)]
            near, far = split(level, edge_weights(f[2], f[3]))
            rest = 1.0 - (near[0] + near[1] + near[2])
            flat = [jnp.where(v > 0.0, 0.15, 0.0) for v in near]
            rest_flat = 1.0 - (flat[0] + flat[1] + flat[2])
            for k in range(3):
                ofar_ref[k, b] = far[k]
            oaux_ref[0, b] = link_weight(level, wet, f[4], last)
            core = [rows_at(core_ref, p_rows)(plan.lev * i + at) for i in range(4)]
            out = moves(f[:4], core, [near, near, flat, flat], [rest, rest, rest_flat, rest_flat])
            for i in range(4):
                opart_ref[i, b] = out[i]


def far_wet(index, in_cross, wet_cross):
    return [jnp.where(in_cross[k], take_lanes(wet_cross, index[k]), 0.0) for k in range(3)]


def far_moves(parts, own, cross, far, index):
    totals = [p - o * (f[0] + f[1] + f[2]) for p, o, f in zip(parts, own, far)]
    for k in range(3):
        for j in range(len(own)):
            totals[j] = totals[j] + far[j][k] * take_lanes(cross[j], index[k])
    return totals


class Far:
    def __init__(self, plan, comp, second, nb_ref, pq_ref, cross_p_ref, part_ref, far_ref, aux_ref, h_ref, l_ref):
        self.plan, self.comp, self.second = plan, comp, second
        self.cols = nb_ref.shape[-1]
        self.own_p, self.own_q = rows_at(pq_ref), rows_at(pq_ref, plan.p_rows)
        self.part, self.far, self.aux, self.h, self.l = part_ref, far_ref, aux_ref, h_ref, l_ref
        self.index, _, in_cross = neighbours_of(nb_ref, lax.axis_index("tile") % 2)
        self.wet = wet_of(plan, pq_ref)
        self.wets = far_wet(self.index, in_cross, wet_of(plan, cross_p_ref))

    def at(self, r):
        return SUB * (r + 1)

    def clear(self, before, after):
        zero = jnp.zeros((SUB, self.cols), F32)
        if before is not None:
            self.l[self.at(before) : self.at(before) + SUB, :] = zero
        for j in range(self.plan.nt):
            for r in (before, after):
                if r is not None:
                    self.h[j, self.at(r) : self.at(r) + SUB, :] = zero

    def move(self, r, p, q):
        plan, at = self.plan, self.at(r)
        level = level_block(plan.level(self.comp, r), self.cols)
        far = [jnp.where(level < self.wets[k], self.far[k, r], 0.0) for k in range(3)]
        self.l[at : at + SUB, :] = self.aux[0, r]
        js = range(plan.nt)
        parts = [self.part[j, r] for j in js]
        own = [plan.block(self.comp, self.second, self.own_p, self.own_q, j, r) for j in js]
        cross = [plan.block(self.comp, self.second, p, q, j, r) for j in js]
        for j, v in enumerate(far_moves(parts, own, cross, [far] * plan.nt, self.index)):
            self.h[j, at : at + SUB, :] = v

    def react(self, r, react_ref, put):
        plan, at = self.plan, self.at(r)
        active = (level_block(plan.level(self.comp, r), self.cols) < self.wet).astype(F32)
        down, up = self.l[at : at + SUB, :], self.l[at - 1 : at - 1 + SUB, :]
        ys, ts = [], []
        for j in range(plan.nt):
            v = self.h[j, at : at + SUB, :]
            y = v + down * (self.h[j, at + 1 : at + 1 + SUB, :] - v) - up * (v - self.h[j, at - 1 : at - 1 + SUB, :])
            ys.append(y)
            ts.append(jnp.tanh(y))
        growth = self.aux[1, r]
        if self.second:
            total = react_ref[0:1, :] * ts[0]
            for j in range(1, plan.nt):
                total = total + react_ref[j : j + 1, :] * ts[j]
            put(0, r, (ys[0] + growth * total) * active)
            return
        n = react_ref.shape[1]
        ts += [jnp.zeros_like(ts[0])] * (n // SUB - plan.nt)
        stack = jnp.concatenate(ts, axis=0)
        high = stack.astype(BF16)
        rest = (stack - high.astype(F32)).astype(BF16)
        both = jnp.dot(react_ref[...], high, preferred_element_type=F32)
        total = both[:n] + both[n:] + jnp.dot(react_ref[0:n, :], rest, preferred_element_type=F32)
        for i in range(plan.nt):
            put(i, r, (ys[i] + growth * total[i * SUB : (i + 1) * SUB]) * active)


def nothing(offset):
    raise ValueError("not there")


def upper_kernel(plan, react_ref, nb_ref, pq_ref, p_ref, part_ref, far_ref, aux_ref, out_ref, edge_ref, h_ref, l_ref):
    out_ref[plan.wet : plan.wet + plan.half, :] = pq_ref[plan.wet : plan.wet + plan.half, :]
    refs = (nb_ref, pq_ref, p_ref, part_ref, far_ref, aux_ref, h_ref, l_ref)
    p = rows_at(p_ref)

    @on_side(0)
    def _():
        work = Far(plan, 0, False, *refs)
        work.clear(0, plan.window)
        for r in plan.rs(0):
            work.move(r, p, nothing)

        def put(i, r, value):
            if r <= plan.full:
                at = SUB * (plan.full * i + r - 1)
                out_ref[at : at + SUB, :] = value
            else:
                at = plan.halves + plan.half * i
                out_ref[at : at + plan.half, :] = value[0 : plan.half]

        for r in plan.rs(0):
            work.react(r, react_ref, put)

    @on_side(1)
    def _():
        work = Far(plan, 1, False, *refs)
        work.clear(-1, None)
        lower = lambda offset: jnp.zeros((SUB, work.cols), F32)
        for r in range(plan.full + 1):
            work.move(r, p, lower)
        at = work.at(plan.full - 1)
        for j in range(plan.nt):
            edge_ref[j] = h_ref[j, at : at + SUB, :]

        def put(i, r, value):
            at = SUB * (plan.full * i + r)
            out_ref[at : at + SUB, :] = value

        for r in range(plan.full):
            work.react(r, react_ref, put)


def ocean_far(plan, nb_ref, f_ref, pq_ref, p_ref, q_ref, opart_ref, ofar_ref, oaux_ref, w_ref, l_ref, put):
    cols = nb_ref.shape[-1]
    index, _, in_cross = neighbours_of(nb_ref, lax.axis_index("tile") % 2)
    wet = wet_of(plan, pq_ref)
    wets = far_wet(index, in_cross, wet_of(plan, p_ref))
    zero = jnp.zeros((SUB, cols), F32)
    end = SUB * (plan.blocks + 1)
    l_ref[0:SUB, :] = zero
    for i in range(4):
        w_ref[i, 0:SUB, :] = zero
        w_ref[i, end : end + SUB, :] = zero
    for b in range(plan.blocks):
        at = SUB * b
        level = level_block(at, cols)
        far = [jnp.where(level < wets[k], ofar_ref[k, b], 0.0) for k in range(3)]
        flat = [jnp.where(v > 0.0, 0.15, 0.0) for v in far]
        there = slice(at + SUB, at + 2 * SUB)
        l_ref[there, :] = oaux_ref[0, b]
        parts = [opart_ref[i, b] for i in range(4)]
        own = [f_ref[i, at : at + SUB, :] for i in range(4)]
        cross = [rows_at(q_ref)(plan.lev * i + at) for i in range(4)]
        q = far_moves(parts, own, cross, [far, far, flat, flat], index)
        w_ref[0, there, :] = q[0]
        w_ref[1, there, :] = q[1]
        w_ref[2, there, :] = ROTATE_COS * q[2] + ROTATE_SIN * q[3]
        w_ref[3, there, :] = -ROTATE_SIN * q[2] + ROTATE_COS * q[3]
    warm = [None] * plan.blocks
    for b in range(plan.blocks):
        at = SUB * (b + 1)
        active = (level_block(SUB * b, cols) < wet).astype(F32)
        down, up = l_ref[at : at + SUB, :], l_ref[at - 1 : at - 1 + SUB, :]
        for i in range(4):
            v = w_ref[i, at : at + SUB, :]
            y = v + down * (w_ref[i, at + 1 : at + 1 + SUB, :] - v) - up * (v - w_ref[i, at - 1 : at - 1 + SUB, :])
            if i == 0:
                warm[b] = y + oaux_ref[1, b]
                put(0, b, warm[b] * active)
            else:
                put(i, b, y * active)
        put(5, b, oaux_ref[2, b])
    sub = lax.broadcasted_iota(jnp.int32, (SUB, cols), 0)
    for b in range(plan.blocks):
        active = (level_block(SUB * b, cols) < wet).astype(F32)
        lower = pltpu.roll(warm[b], SUB - 1, 0)
        if b + 1 < plan.blocks:
            lower = jnp.where(sub == SUB - 1, pltpu.roll(warm[b + 1], SUB - 1, 0), lower)
        else:
            lower = jnp.where(sub == SUB - 1, warm[b], lower)
        put(4, b, (warm[b] - lower) * active)


def lower_kernel(
    plan, react_ref, nb_ref, f_ref, pq_ref, p_ref, q_ref, part_ref, far_ref, aux_ref, opart_ref, ofar_ref, oaux_ref,
    done_ref, edge_ref, out_ref, both_ref, ocean_ref, over_ref, h_ref, l_ref, w_ref, wl_ref,
):
    both_ref[0 : plan.p_rows, :] = done_ref[...]

    @on_side(0)
    def _():
        def put(i, b, value):
            at = SUB * b
            ocean_ref[i, at : at + SUB, :] = value
            if 2 <= i < 5 and b >= plan.full:
                over_ref[i - 1, at - SUB * plan.full : at - SUB * plan.full + SUB, :] = value
            if i < 4:
                for ref, base in ((out_ref, 0), (both_ref, plan.p_rows)):
                    ref[base + plan.lev * i + at : base + plan.lev * i + at + SUB, :] = value

        ocean_far(plan, nb_ref, f_ref, pq_ref, p_ref, q_ref, opart_ref, ofar_ref, oaux_ref, w_ref, wl_ref, put)
        tall = SUB * plan.full
        over_ref[0] = growth_rate(ocean_ref[0, tall:, :], ocean_ref[1, tall:, :], ocean_ref[5, tall:, :])

    @on_side(1)
    def _():
        work = Far(plan, 1, False, nb_ref, pq_ref, p_ref, part_ref, far_ref, aux_ref, h_ref, l_ref)
        work.clear(None, plan.window)
        before = work.at(plan.full - 1)
        l_ref[before : before + SUB, :] = aux_ref[0, plan.full - 1]
        for j in range(plan.nt):
            h_ref[j, before : before + SUB, :] = edge_ref[j]
        rs = (plan.full, plan.full + 1)
        for r in rs:
            work.move(r, rows_at(p_ref), rows_at(q_ref))

        def put(i, r, value):
            at = SUB * (2 * i + r - plan.full)
            out_ref[at : at + SUB, :] = value
            both_ref[plan.p_rows + at : plan.p_rows + at + SUB, :] = value
            if i == 0:
                over_ref[0, SUB * r : SUB * (r + 1), :] = value

        for r in rs:
            work.react(r, react_ref, put)
        for r in range(plan.full):
            over_ref[0, SUB * r : SUB * (r + 1), :] = done_ref[SUB * r : SUB * (r + 1), :]


def chl_kernel(plan, react_ref, nb_ref, pq_ref, p_ref, part_ref, far_ref, aux_ref, out_ref, h_ref, l_ref):
    @on_side(0)
    def _():
        work = Far(plan, 0, True, nb_ref, pq_ref, p_ref, part_ref, far_ref, aux_ref, h_ref, l_ref)
        work.clear(0, plan.window)
        for r in plan.rs(0):
            work.move(r, rows_at(p_ref), nothing)

        def put(i, r, value):
            out_ref[SUB * (r - 1) : SUB * r, :] = value

        for r in plan.rs(0):
            work.react(r, react_ref, put)


def second_kernel(
    plan, react_ref, nb_ref, f_ref, rest_ref, pq_ref, p_ref, q_ref, part_ref, far_ref, aux_ref, opart_ref,
    ofar_ref, oaux_ref, out_ref, mine_ref, h_ref, l_ref, w_ref, wl_ref,
):
    @on_side(0)
    def _():
        def put(i, b, value):
            out_ref[i, SUB * b : SUB * (b + 1), :] = value

        ocean_far(plan, nb_ref, f_ref, pq_ref, p_ref, q_ref, opart_ref, ofar_ref, oaux_ref, w_ref, wl_ref, put)

    @on_side(1)
    def _():
        out_ref[...] = rest_ref[...]
        work = Far(plan, 1, True, nb_ref, pq_ref, p_ref, part_ref, far_ref, aux_ref, h_ref, l_ref)
        work.clear(-1, plan.window)
        for r in plan.rs(1):
            work.move(r, rows_at(p_ref), rows_at(q_ref))

        def put(i, r, value):
            mine_ref[SUB * r : SUB * (r + 1), :] = value

        for r in plan.rs(1):
            work.react(r, react_ref, put)


def merge_kernel(plan, chl_ref, mine_ref, upper_ref, out_ref):
    @on_side(0)
    def _():
        out_ref[...] = chl_ref[...]

    @on_side(1)
    def _():
        tall = SUB * plan.full
        sub = lax.broadcasted_iota(jnp.int32, (SUB, out_ref.shape[1]), 0)
        out_ref[0:tall, :] = upper_ref[0:tall, :]
        out_ref[tall : tall + SUB, :] = jnp.where(sub < 2, upper_ref[tall : tall + SUB, :], mine_ref[0:SUB, :])
        out_ref[tall + SUB :, :] = mine_ref[SUB:, :]


def call(kernel, outs, ins, specs=None, scratch=(), cost=1_000_000):
    return pl.pallas_call(
        kernel,
        out_shape=outs,
        in_specs=specs or [VMEM] * len(ins),
        out_specs=jax.tree.map(lambda _: VMEM, outs),
        scratch_shapes=list(scratch),
        compiler_params=pltpu.CompilerParams(vmem_limit_bytes=GRANT),
        cost_estimate=pl.CostEstimate(flops=cost, bytes_accessed=1_000_000, transcendentals=0),
    )(*ins)


def swaps(tiles, across):
    pairs = []
    for c in (0, 1):
        for t in range(tiles):
            other = (t + 1) % tiles if (t % 2 == 0) != across else (t - 1) % tiles
            pairs.append((c * tiles + t, c * tiles + other))
    return pairs


def over_comp(sources, tiles):
    return [(c * tiles + t, (1 - c) * tiles + t) for c in sources for t in range(tiles)]


def sent(v, pairs):
    return lax.ppermute(v, AXES, pairs)


def per_device(ocean_fields, tracers, reaction, wet_levels, neighbours):
    tiles = lax.axis_size("tile")
    nt, lev, cols = tracers.shape
    plan = Plan(nt, lev)
    blocks, window, p_rows = plan.blocks, plan.window, plan.p_rows
    fields = ocean_fields.reshape(-1, lev, cols)
    nf = fields.shape[0]
    top, tall = SUB * (plan.full + 1), SUB * plan.full
    across, within = swaps(tiles, True), swaps(tiles, False)

    near_shapes = (
        shape_of(nt, window, SUB, cols),
        shape_of(3, window, SUB, cols),
        shape_of(2, window, SUB, cols),
        shape_of(4, blocks, SUB, cols),
        shape_of(3, blocks, SUB, cols),
        shape_of(3, blocks, SUB, cols),
    )
    h_scratch = (pltpu.VMEM((nt, (window + 2) * SUB, cols), F32), pltpu.VMEM(((window + 2) * SUB, cols), F32))
    w_scratch = (pltpu.VMEM((4, (blocks + 2) * SUB, cols), F32), pltpu.VMEM(((blocks + 2) * SUB, cols), F32))
    kernel = lambda f, *more: functools.partial(f, plan, *more)

    p, q, pq, top_fields, chl = call(
        kernel(pack_kernel),
        (
            shape_of(p_rows, cols),
            shape_of(plan.q_rows[0], cols),
            shape_of(p_rows + plan.q_rows[0], cols),
            shape_of(4, top, cols),
            shape_of(lev, cols),
        ),
        tuple(
            pltpu.with_memory_space_constraint(v, pltpu.HBM) for v in (wet_levels.reshape(1, cols), fields, tracers)
        ),
        specs=[HBM] * 3,
        scratch=[
            pltpu.VMEM((1, cols), jnp.int32),
            pltpu.VMEM((nt, SUB, cols), F32),
            pltpu.VMEM((nf, top, cols), F32),
            pltpu.SemaphoreType.DMA((6,)),
        ],
    )
    cross_p = sent(p, across)
    lagged = sent(top_fields, over_comp((1,), tiles))
    core = sent(pq, within)
    cross_q = sent(q, across)
    n = -(-nt // 2) * 2 * SUB
    matrix, rates = call(
        matrix_kernel, (jax.ShapeDtypeStruct((2 * n, n), BF16), shape_of(nt, cols)), (reaction,)
    )

    near = call(
        kernel(near_kernel, False),
        near_shapes,
        (neighbours, fields, lagged, fields, pq, core, chl),
        cost=8_000_000,
    )
    p_one, edge = call(
        kernel(upper_kernel),
        (shape_of(p_rows, cols), shape_of(nt, SUB, cols)),
        (matrix, neighbours, pq, cross_p, *near[:3]),
        scratch=h_scratch,
        cost=8_000_000,
    )
    cross_p_one = sent(p_one, across)
    q_one, pq_one, ocean_one, over_one = call(
        kernel(lower_kernel),
        (
            shape_of(plan.q_rows[1], cols),
            shape_of(p_rows + plan.q_rows[1], cols),
            shape_of(nf, lev, cols),
            shape_of(4, lev - tall, cols),
        ),
        (matrix, neighbours, fields, pq, cross_p, cross_q, *near, p_one, edge),
        scratch=h_scratch + w_scratch,
        cost=8_000_000,
    )
    over = sent(over_one, over_comp((0, 1), tiles))
    core_one = sent(pq_one, within)
    cross_q_one = sent(q_one, across)
    rest = sent(ocean_one, over_comp((0,), tiles))

    *near, chl_one = call(
        kernel(near_kernel, True),
        near_shapes + (shape_of(lev, cols),),
        (neighbours, ocean_one, ocean_one, over, pq_one, core_one, p_one, over),
        cost=8_000_000,
    )
    upper = call(
        kernel(chl_kernel),
        shape_of(top, cols),
        (rates, neighbours, pq_one, cross_p_one, *near[:3]),
        scratch=h_scratch,
        cost=8_000_000,
    )
    upper = sent(upper, over_comp((0,), tiles))
    ocean_out, mine = call(
        kernel(second_kernel),
        (shape_of(nf, lev, cols), shape_of(lev - tall, cols)),
        (rates, neighbours, ocean_one, rest, pq_one, cross_p_one, cross_q_one, *near),
        scratch=h_scratch + w_scratch,
        cost=8_000_000,
    )
    chl_out = call(kernel(merge_kernel), shape_of(lev, cols), (chl_one, mine, upper))
    return (ocean_out[None], chl_out[None])


def solution(mesh):
    return jax.shard_map(
        per_device,
        mesh=mesh,
        in_specs=(
            P("comp", None, None, "tile"),
            P(None, None, "tile"),
            P(),
            P("tile"),
            P(None, "tile"),
        ),
        out_specs=(P("comp", None, None, "tile"), P("comp", None, "tile")),
        check_vma=False,
    )
```

```python
import functools
import math

import jax
import jax.numpy as jnp
from jax import lax
from jax.experimental import pallas as pl
from jax.experimental.pallas import tpu as pltpu
from jax.sharding import PartitionSpec as P


ROTATE_COS = math.cos(0.3)
ROTATE_SIN = math.sin(0.3)
SUB = 8
AXES = ("comp", "tile")
ANGLES = [2.0 * math.pi * k / 3.0 for k in range(3)]
F32 = jnp.float32
BF16 = jnp.bfloat16
GRANT = 8 << 20


VMEM = pl.BlockSpec(memory_space=pltpu.VMEM)
SMEM = pl.BlockSpec(memory_space=pltpu.SMEM)
HBM = pl.BlockSpec(memory_space=pltpu.HBM)


class Plan:
    def __init__(self, nt, lev):
        self.nt, self.lev = nt, lev
        self.blocks = lev // SUB
        self.full = self.blocks // 2 - 1
        self.window = self.full + 2
        self.half = SUB // 2
        self.halves = SUB * nt * self.full
        self.wet = self.halves + self.half * nt
        self.p_rows = -(-(self.wet + self.half) // SUB) * SUB
        self.q_rows = (
            max(4 * lev, -(-(SUB + self.half) * nt // SUB) * SUB),
            max(4 * lev, 2 * SUB * nt),
        )

    def rs(self, comp):
        return list(range(1 - comp, self.window))

    def level(self, comp, r):
        return SUB * (r - 1) if comp == 0 else SUB * (self.full + r)

    def rest(self, i):
        tall = SUB * self.full
        return (0, self.lev, 2 * self.lev, 2 * self.lev + tall, 2 * self.lev + 2 * tall, 2 * self.lev + 3 * tall)[i]

    def block(self, comp, second, p, q, j, r):
        if comp == 0:
            return p(SUB * (self.full * j + r - 1)) if r <= self.full else p(self.halves + self.half * j)
        if r < self.full:
            return p(SUB * (self.full * j + r))
        if second:
            return q(SUB * (2 * j + r - self.full))
        if r > self.full:
            return q(SUB * j)
        upper = p(self.halves + self.half * j)
        lower = q(SUB * self.nt + self.half * (j - 1))
        sub = lax.broadcasted_iota(jnp.int32, upper.shape, 0)
        return jnp.where(sub < self.half, upper, lower)


def rows_at(ref, base=0):
    return lambda offset: ref[base + offset : base + offset + SUB, :]


def edge_weights(eastward, northward):
    return [
        0.05 + 0.25 * jax.nn.sigmoid(eastward * math.cos(a) + northward * math.sin(a)) for a in ANGLES
    ]


def take_lanes(block, index):
    return jnp.take_along_axis(block, index, axis=1, mode="promise_in_bounds")


def shape_of(*dims):
    return jax.ShapeDtypeStruct(dims, F32)


def neighbours_of(nb_ref, odd):
    cols = nb_ref.shape[-1]
    core_side = jnp.where(odd == 1, 0, 2)
    index, in_core, in_cross = [], [], []
    for k in range(3):
        nb = jnp.broadcast_to(nb_ref[k : k + 1, :], (SUB, cols))
        side = nb // cols
        index.append(nb - side * cols)
        in_core.append(side == core_side)
        in_cross.append(side == 2 - core_side)
    return index, in_core, in_cross


def level_block(first, cols):
    return lax.broadcasted_iota(jnp.int32, (SUB, cols), 0).astype(F32) + float(first)


def link_weight(level, wet, mixing, last):
    nxt = level + 1.0
    return jnp.where((nxt < wet) & (nxt <= last), 0.02 + 0.13 * jax.nn.sigmoid(mixing), 0.0)


def growth_rate(temperature, salinity, light):
    return 0.5 * light * jax.nn.sigmoid(temperature + 0.5 * salinity)


def wet_of(plan, ref):
    return jnp.broadcast_to(ref[plan.wet : plan.wet + 1, :], (SUB, ref.shape[1]))


def on_side(comp):
    return pl.when(lax.axis_index("comp") == comp)


def pack_kernel(plan, wet_ref, f_ref, t_ref, p_ref, q_ref, pq_ref, top_ref, chl_ref, wet_buf, half_buf, top_buf, sems):
    nt, full, half, lev = plan.nt, plan.full, plan.half, plan.lev
    tall = SUB * full
    first = pl.multiple_of(lax.axis_index("comp") * tall, SUB)
    copies = [
        (t_ref.at[:, pl.ds(first, tall)], p_ref.at[pl.ds(0, plan.halves)].reshape(nt, tall, p_ref.shape[1])),
        (t_ref.at[:, pl.ds(pl.multiple_of(first + tall, SUB), SUB)], half_buf),
        (wet_ref, wet_buf),
        (f_ref.at[:, pl.ds(0, top_ref.shape[1])], top_buf),
        (t_ref.at[0], chl_ref),
    ]
    copies = [pltpu.make_async_copy(s, d, sems.at[i]) for i, (s, d) in enumerate(copies)]
    for c in copies:
        c.start()
    base = len(copies)
    slab = lambda n, rows: q_ref.at[pl.ds(0, n * rows)].reshape(n, rows, q_ref.shape[1])
    ocean = [pltpu.make_async_copy(f_ref.at[pl.ds(0, 4)], slab(4, lev), sems.at[base])]
    deep = [pltpu.make_async_copy(t_ref.at[:, pl.ds(lev - SUB, SUB)], slab(nt, SUB), sems.at[base])]

    @on_side(0)
    def _():
        for c in ocean:
            c.start()

    @on_side(1)
    def _():
        for c in deep:
            c.start()

    for c in copies:
        c.wait()
    p_ref[plan.wet : plan.wet + half, :] = jnp.broadcast_to(wet_buf[...].astype(F32), (half, wet_buf.shape[1]))
    for j in range(nt):
        p_ref[plan.halves + half * j : plan.halves + half * (j + 1), :] = half_buf[j, 0:half, :]

    @on_side(0)
    def _():
        for c in ocean:
            c.wait()

    @on_side(1)
    def _():
        for c in deep:
            c.wait()
        top_ref[0] = growth_rate(top_buf[0], top_buf[1], top_buf[5])
        top_ref[1:4] = top_buf[2:5]
        for j in range(nt):
            at = SUB * nt + half * j
            q_ref[at : at + half, :] = half_buf[j, half:SUB, :]

    pq_ref[0 : plan.p_rows, :] = p_ref[...]
    pq_ref[plan.p_rows :, :] = q_ref[...]


def matrix_kernel(r_ref, out_ref, first_ref):
    nt = r_ref.shape[0]
    rows, n = out_ref.shape
    p = lax.broadcasted_iota(jnp.int32, (n, nt), 0)
    spread = (p // SUB == lax.broadcasted_iota(jnp.int32, (n, nt), 1)).astype(F32)
    exact = functools.partial(
        lax.dot_general, precision=lax.Precision.HIGHEST, preferred_element_type=F32
    )
    tall = exact(spread, r_ref[...], (((1,), (0,)), ((), ())))
    full = exact(tall, spread, (((1,), (1,)), ((), ())))
    a = lax.broadcasted_iota(jnp.int32, (n, n), 0)
    b = lax.broadcasted_iota(jnp.int32, (n, n), 1)
    full = jnp.where(a % SUB == b % SUB, full, 0.0)
    high = full.astype(BF16)
    out_ref[0:n, :] = high
    out_ref[n:rows, :] = (full - high.astype(F32)).astype(BF16)
    ones = jnp.ones((1, first_ref.shape[1]), F32)
    first_ref[...] = exact(r_ref[0:1, :], ones, (((0,), (0,)), ((), ())))


def near_kernel(plan, second, nb_ref, f_ref, ga_ref, gb_ref, pq_ref, core_ref, chl_ref, *refs):
    if second:
        chl_low_ref, *refs = refs
    part_ref, far_ref, aux_ref, opart_ref, ofar_ref, oaux_ref = refs[:6]
    chl_out_ref = refs[6] if second else None
    odd = lax.axis_index("tile") % 2
    cols = nb_ref.shape[-1]
    nt, p_rows = plan.nt, plan.p_rows
    index, in_core, in_cross = neighbours_of(nb_ref, odd)
    wet, wet_core = wet_of(plan, pq_ref), wet_of(plan, core_ref)
    near_wet = []
    for k in range(3):
        found = jnp.where(in_core[k], take_lanes(wet_core, index[k]), take_lanes(wet, index[k]))
        near_wet.append(jnp.where(in_cross[k], 0.0, found))
    last = float(plan.lev - 1)

    def split(level, ws):
        active = level < wet
        near = [jnp.where(active & (level < near_wet[k]), ws[k], 0.0) for k in range(3)]
        far = [jnp.where(active & in_cross[k], ws[k], 0.0) for k in range(3)]
        return near, far

    def moves(own, core, near, rest):
        totals = [o * r for o, r in zip(own, rest)]
        for k in range(3):
            for j in range(len(own)):
                v = jnp.where(in_core[k], take_lanes(core[j], index[k]), take_lanes(own[j], index[k]))
                totals[j] = totals[j] + near[j][k] * v
        return totals

    def tracers(comp):
        for r in plan.rs(comp):
            first = plan.level(comp, r)
            level = level_block(first, cols)
            passed = comp == int(second)
            ref, at = (gb_ref if comp else ga_ref), first - SUB * plan.full * int(passed and comp)
            g = [ref[i, at : at + SUB, :] for i in range(4 if passed else 6)]
            if not passed:
                g = [growth_rate(g[0], g[1], g[5])] + g[2:5]
            near, far = split(level, edge_weights(g[1], g[2]))
            rest = 1.0 - (near[0] + near[1] + near[2])
            for k in range(3):
                far_ref[k, r] = far[k]
            aux_ref[0, r] = link_weight(level, wet, g[3], last)
            aux_ref[1, r] = g[0]
            own = [plan.block(comp, second, rows_at(pq_ref), rows_at(pq_ref, p_rows), j, r) for j in range(nt)]
            core = [plan.block(comp, second, rows_at(core_ref), rows_at(core_ref, p_rows), j, r) for j in range(nt)]
            for j, v in enumerate(moves(own, core, [near] * nt, [rest] * nt)):
                part_ref[j, r] = v

    @on_side(1)
    def _():
        tracers(1)

    @on_side(0)
    def _():
        tracers(0)
        top = f_ref[5, 0:1, :]
        cut = SUB * (plan.full + 1) - SUB + 2

        def chl_block(b):
            at = SUB * b
            if not second:
                return chl_ref[at : at + SUB, :]
            if b < plan.full:
                return chl_ref[at : at + SUB, :]
            v = chl_low_ref[0, at - SUB * plan.full : at - SUB * plan.full + SUB, :]
            if b > plan.full:
                return v
            return jnp.where(level_block(at, cols) < float(cut), chl_ref[plan.halves : plan.halves + SUB, :], v)

        run = jnp.zeros((1, cols), F32)
        for b in range(plan.blocks):
            x = chl_block(b)
            if second:
                chl_out_ref[SUB * b : SUB * (b + 1), :] = x
            absorbed = 0.01 + 0.3 * (jnp.maximum(x, 0.0) + jnp.log1p(jnp.exp(-jnp.abs(x))))
            level = level_block(SUB * b, cols)
            sub = lax.broadcasted_iota(jnp.int32, (SUB, cols), 0)
            cum = absorbed
            for d in (1, 2, 4):
                cum = cum + jnp.where(sub >= d, pltpu.roll(cum, d, 0), 0.0)
            depth = cum + run
            ceiling = jnp.exp(-(depth - absorbed))
            oaux_ref[1, b] = 4.0 * top * (ceiling - jnp.exp(-depth))
            oaux_ref[2, b] = jnp.where(level < wet, top * ceiling, 0.0)
            run = depth[SUB - 1 : SUB, :]

        for b in range(plan.blocks):
            at = SUB * b
            level = level_block(at, cols)
            f = [f_ref[i, at : at + SUB, :] for i in range(5)]
            near, far = split(level, edge_weights(f[2], f[3]))
            rest = 1.0 - (near[0] + near[1] + near[2])
            flat = [jnp.where(v > 0.0, 0.15, 0.0) for v in near]
            rest_flat = 1.0 - (flat[0] + flat[1] + flat[2])
            for k in range(3):
                ofar_ref[k, b] = far[k]
            oaux_ref[0, b] = link_weight(level, wet, f[4], last)
            core = [rows_at(core_ref, p_rows)(plan.lev * i + at) for i in range(4)]
            out = moves(f[:4], core, [near, near, flat, flat], [rest, rest, rest_flat, rest_flat])
            for i in range(4):
                opart_ref[i, b] = out[i]


def far_wet(index, in_cross, wet_cross):
    return [jnp.where(in_cross[k], take_lanes(wet_cross, index[k]), 0.0) for k in range(3)]


def far_moves(parts, own, cross, far, index):
    totals = [p - o * (f[0] + f[1] + f[2]) for p, o, f in zip(parts, own, far)]
    for k in range(3):
        for j in range(len(own)):
            totals[j] = totals[j] + far[j][k] * take_lanes(cross[j], index[k])
    return totals


class Far:
    def __init__(self, plan, comp, second, nb_ref, pq_ref, cross_p_ref, part_ref, far_ref, aux_ref, h_ref, l_ref):
        self.plan, self.comp, self.second = plan, comp, second
        self.cols = nb_ref.shape[-1]
        self.own_p, self.own_q = rows_at(pq_ref), rows_at(pq_ref, plan.p_rows)
        self.part, self.far, self.aux, self.h, self.l = part_ref, far_ref, aux_ref, h_ref, l_ref
        self.index, _, in_cross = neighbours_of(nb_ref, lax.axis_index("tile") % 2)
        self.wet = wet_of(plan, pq_ref)
        self.wets = far_wet(self.index, in_cross, wet_of(plan, cross_p_ref))

    def at(self, r):
        return SUB * (r + 1)

    def clear(self, before, after):
        zero = jnp.zeros((SUB, self.cols), F32)
        if before is not None:
            self.l[self.at(before) : self.at(before) + SUB, :] = zero
        for j in range(self.plan.nt):
            for r in (before, after):
                if r is not None:
                    self.h[j, self.at(r) : self.at(r) + SUB, :] = zero

    def move(self, r, p, q):
        plan, at = self.plan, self.at(r)
        level = level_block(plan.level(self.comp, r), self.cols)
        far = [jnp.where(level < self.wets[k], self.far[k, r], 0.0) for k in range(3)]
        self.l[at : at + SUB, :] = self.aux[0, r]
        js = range(plan.nt)
        parts = [self.part[j, r] for j in js]
        own = [plan.block(self.comp, self.second, self.own_p, self.own_q, j, r) for j in js]
        cross = [plan.block(self.comp, self.second, p, q, j, r) for j in js]
        for j, v in enumerate(far_moves(parts, own, cross, [far] * plan.nt, self.index)):
            self.h[j, at : at + SUB, :] = v

    def react(self, r, react_ref, put):
        plan, at = self.plan, self.at(r)
        active = (level_block(plan.level(self.comp, r), self.cols) < self.wet).astype(F32)
        down, up = self.l[at : at + SUB, :], self.l[at - 1 : at - 1 + SUB, :]
        ys, ts = [], []
        for j in range(plan.nt):
            v = self.h[j, at : at + SUB, :]
            y = v + down * (self.h[j, at + 1 : at + 1 + SUB, :] - v) - up * (v - self.h[j, at - 1 : at - 1 + SUB, :])
            ys.append(y)
            ts.append(jnp.tanh(y))
        growth = self.aux[1, r]
        if self.second:
            total = react_ref[0:1, :] * ts[0]
            for j in range(1, plan.nt):
                total = total + react_ref[j : j + 1, :] * ts[j]
            put(0, r, (ys[0] + growth * total) * active)
            return
        n = react_ref.shape[1]
        ts += [jnp.zeros_like(ts[0])] * (n // SUB - plan.nt)
        stack = jnp.concatenate(ts, axis=0)
        high = stack.astype(BF16)
        rest = (stack - high.astype(F32)).astype(BF16)
        both = jnp.dot(react_ref[...], high, preferred_element_type=F32)
        total = both[:n] + both[n:] + jnp.dot(react_ref[0:n, :], rest, preferred_element_type=F32)
        for i in range(plan.nt):
            put(i, r, (ys[i] + growth * total[i * SUB : (i + 1) * SUB]) * active)


def nothing(offset):
    raise ValueError("not there")


def upper_kernel(plan, react_ref, nb_ref, pq_ref, p_ref, part_ref, far_ref, aux_ref, out_ref, edge_ref, h_ref, l_ref):
    out_ref[plan.wet : plan.wet + plan.half, :] = pq_ref[plan.wet : plan.wet + plan.half, :]
    refs = (nb_ref, pq_ref, p_ref, part_ref, far_ref, aux_ref, h_ref, l_ref)
    p = rows_at(p_ref)

    @on_side(0)
    def _():
        work = Far(plan, 0, False, *refs)
        work.clear(0, plan.window)
        for r in plan.rs(0):
            work.move(r, p, nothing)

        def put(i, r, value):
            if r <= plan.full:
                at = SUB * (plan.full * i + r - 1)
                out_ref[at : at + SUB, :] = value
            else:
                at = plan.halves + plan.half * i
                out_ref[at : at + plan.half, :] = value[0 : plan.half]

        for r in plan.rs(0):
            work.react(r, react_ref, put)

    @on_side(1)
    def _():
        work = Far(plan, 1, False, *refs)
        work.clear(-1, None)
        lower = lambda offset: jnp.zeros((SUB, work.cols), F32)
        for r in range(plan.full + 1):
            work.move(r, p, lower)
        at = work.at(plan.full - 1)
        for j in range(plan.nt):
            edge_ref[j] = h_ref[j, at : at + SUB, :]

        def put(i, r, value):
            at = SUB * (plan.full * i + r)
            out_ref[at : at + SUB, :] = value

        for r in range(plan.full):
            work.react(r, react_ref, put)


def ocean_far(plan, nb_ref, f_ref, pq_ref, p_ref, q_ref, opart_ref, ofar_ref, oaux_ref, w_ref, l_ref, put):
    cols = nb_ref.shape[-1]
    index, _, in_cross = neighbours_of(nb_ref, lax.axis_index("tile") % 2)
    wet = wet_of(plan, pq_ref)
    wets = far_wet(index, in_cross, wet_of(plan, p_ref))
    zero = jnp.zeros((SUB, cols), F32)
    end = SUB * (plan.blocks + 1)
    l_ref[0:SUB, :] = zero
    for i in range(4):
        w_ref[i, 0:SUB, :] = zero
        w_ref[i, end : end + SUB, :] = zero
    for b in range(plan.blocks):
        at = SUB * b
        level = level_block(at, cols)
        far = [jnp.where(level < wets[k], ofar_ref[k, b], 0.0) for k in range(3)]
        flat = [jnp.where(v > 0.0, 0.15, 0.0) for v in far]
        there = slice(at + SUB, at + 2 * SUB)
        l_ref[there, :] = oaux_ref[0, b]
        parts = [opart_ref[i, b] for i in range(4)]
        own = [f_ref[i, at : at + SUB, :] for i in range(4)]
        cross = [rows_at(q_ref)(plan.lev * i + at) for i in range(4)]
        q = far_moves(parts, own, cross, [far, far, flat, flat], index)
        w_ref[0, there, :] = q[0]
        w_ref[1, there, :] = q[1]
        w_ref[2, there, :] = ROTATE_COS * q[2] + ROTATE_SIN * q[3]
        w_ref[3, there, :] = -ROTATE_SIN * q[2] + ROTATE_COS * q[3]
    warm = [None] * plan.blocks
    for b in range(plan.blocks):
        at = SUB * (b + 1)
        active = (level_block(SUB * b, cols) < wet).astype(F32)
        down, up = l_ref[at : at + SUB, :], l_ref[at - 1 : at - 1 + SUB, :]
        for i in range(4):
            v = w_ref[i, at : at + SUB, :]
            y = v + down * (w_ref[i, at + 1 : at + 1 + SUB, :] - v) - up * (v - w_ref[i, at - 1 : at - 1 + SUB, :])
            if i == 0:
                warm[b] = y + oaux_ref[1, b]
                put(0, b, warm[b] * active)
            else:
                put(i, b, y * active)
        put(5, b, oaux_ref[2, b])
    sub = lax.broadcasted_iota(jnp.int32, (SUB, cols), 0)
    for b in range(plan.blocks):
        active = (level_block(SUB * b, cols) < wet).astype(F32)
        lower = pltpu.roll(warm[b], SUB - 1, 0)
        if b + 1 < plan.blocks:
            lower = jnp.where(sub == SUB - 1, pltpu.roll(warm[b + 1], SUB - 1, 0), lower)
        else:
            lower = jnp.where(sub == SUB - 1, warm[b], lower)
        put(4, b, (warm[b] - lower) * active)


def lower_kernel(
    plan, react_ref, nb_ref, f_ref, pq_ref, p_ref, q_ref, part_ref, far_ref, aux_ref, opart_ref, ofar_ref, oaux_ref,
    done_ref, edge_ref, out_ref, both_ref, ocean_ref, over_ref, rest_ref, h_ref, l_ref, w_ref, wl_ref,
):
    both_ref[0 : plan.p_rows, :] = done_ref[...]

    @on_side(0)
    def _():
        def put(i, b, value):
            at = SUB * b
            ocean_ref[i, at : at + SUB, :] = value
            if 2 <= i < 5 and b >= plan.full:
                over_ref[i - 1, at - SUB * plan.full : at - SUB * plan.full + SUB, :] = value
            else:
                rest_ref[plan.rest(i) + at : plan.rest(i) + at + SUB, :] = value
            if i < 4:
                for ref, base in ((out_ref, 0), (both_ref, plan.p_rows)):
                    ref[base + plan.lev * i + at : base + plan.lev * i + at + SUB, :] = value

        ocean_far(plan, nb_ref, f_ref, pq_ref, p_ref, q_ref, opart_ref, ofar_ref, oaux_ref, w_ref, wl_ref, put)
        tall = SUB * plan.full
        over_ref[0] = growth_rate(ocean_ref[0, tall:, :], ocean_ref[1, tall:, :], ocean_ref[5, tall:, :])

    @on_side(1)
    def _():
        work = Far(plan, 1, False, nb_ref, pq_ref, p_ref, part_ref, far_ref, aux_ref, h_ref, l_ref)
        work.clear(None, plan.window)
        before = work.at(plan.full - 1)
        l_ref[before : before + SUB, :] = aux_ref[0, plan.full - 1]
        for j in range(plan.nt):
            h_ref[j, before : before + SUB, :] = edge_ref[j]
        rs = (plan.full, plan.full + 1)
        for r in rs:
            work.move(r, rows_at(p_ref), rows_at(q_ref))

        def put(i, r, value):
            at = SUB * (2 * i + r - plan.full)
            out_ref[at : at + SUB, :] = value
            both_ref[plan.p_rows + at : plan.p_rows + at + SUB, :] = value
            if i == 0:
                over_ref[0, SUB * r : SUB * (r + 1), :] = value

        for r in rs:
            work.react(r, react_ref, put)
        for r in range(plan.full):
            over_ref[0, SUB * r : SUB * (r + 1), :] = done_ref[SUB * r : SUB * (r + 1), :]


def chl_kernel(plan, react_ref, nb_ref, pq_ref, p_ref, part_ref, far_ref, aux_ref, out_ref, h_ref, l_ref):
    @on_side(0)
    def _():
        work = Far(plan, 0, True, nb_ref, pq_ref, p_ref, part_ref, far_ref, aux_ref, h_ref, l_ref)
        work.clear(0, plan.window)
        for r in plan.rs(0):
            work.move(r, rows_at(p_ref), nothing)

        def put(i, r, value):
            out_ref[SUB * (r - 1) : SUB * r, :] = value

        for r in plan.rs(0):
            work.react(r, react_ref, put)


def second_kernel(
    plan, react_ref, nb_ref, f_ref, pq_ref, p_ref, q_ref, part_ref, far_ref, aux_ref, opart_ref,
    ofar_ref, oaux_ref, out_ref, mine_ref, h_ref, l_ref, w_ref, wl_ref,
):
    @on_side(0)
    def _():
        def put(i, b, value):
            out_ref[i, SUB * b : SUB * (b + 1), :] = value

        ocean_far(plan, nb_ref, f_ref, pq_ref, p_ref, q_ref, opart_ref, ofar_ref, oaux_ref, w_ref, wl_ref, put)

    @on_side(1)
    def _():
        work = Far(plan, 1, True, nb_ref, pq_ref, p_ref, part_ref, far_ref, aux_ref, h_ref, l_ref)
        work.clear(-1, plan.window)
        for r in plan.rs(1):
            work.move(r, rows_at(p_ref), rows_at(q_ref))

        def put(i, r, value):
            mine_ref[SUB * r : SUB * (r + 1), :] = value

        for r in plan.rs(1):
            work.react(r, react_ref, put)


def merge_kernel(plan, ocean_ref, over_ref, rest_ref, chl_ref, mine_ref, upper_ref, out_ref, chl_out_ref):
    tall = SUB * plan.full

    @on_side(0)
    def _():
        out_ref[...] = ocean_ref[...]
        chl_out_ref[...] = chl_ref[...]

    @on_side(1)
    def _():
        for i in range(6):
            at = plan.rest(i)
            if 2 <= i < 5:
                out_ref[i, 0:tall, :] = rest_ref[at : at + tall, :]
                out_ref[i, tall:, :] = over_ref[i - 1]
            else:
                out_ref[i] = rest_ref[at : at + plan.lev, :]
        sub = lax.broadcasted_iota(jnp.int32, (SUB, chl_out_ref.shape[1]), 0)
        chl_out_ref[0:tall, :] = upper_ref[0:tall, :]
        chl_out_ref[tall : tall + SUB, :] = jnp.where(sub < 2, upper_ref[tall : tall + SUB, :], mine_ref[0:SUB, :])
        chl_out_ref[tall + SUB :, :] = mine_ref[SUB:, :]


def call(kernel, outs, ins, specs=None, scratch=(), cost=1_000_000):
    return pl.pallas_call(
        kernel,
        out_shape=outs,
        in_specs=specs or [VMEM] * len(ins),
        out_specs=jax.tree.map(lambda _: VMEM, outs),
        scratch_shapes=list(scratch),
        compiler_params=pltpu.CompilerParams(vmem_limit_bytes=GRANT),
        cost_estimate=pl.CostEstimate(flops=cost, bytes_accessed=1_000_000, transcendentals=0),
    )(*ins)


def swaps(tiles, across):
    pairs = []
    for c in (0, 1):
        for t in range(tiles):
            other = (t + 1) % tiles if (t % 2 == 0) != across else (t - 1) % tiles
            pairs.append((c * tiles + t, c * tiles + other))
    return pairs


def over_comp(sources, tiles):
    return [(c * tiles + t, (1 - c) * tiles + t) for c in sources for t in range(tiles)]


def sent(v, pairs):
    return lax.ppermute(v, AXES, pairs)


def per_device(ocean_fields, tracers, reaction, wet_levels, neighbours):
    tiles = lax.axis_size("tile")
    nt, lev, cols = tracers.shape
    plan = Plan(nt, lev)
    blocks, window, p_rows = plan.blocks, plan.window, plan.p_rows
    fields = ocean_fields.reshape(-1, lev, cols)
    nf = fields.shape[0]
    top, tall = SUB * (plan.full + 1), SUB * plan.full
    across, within = swaps(tiles, True), swaps(tiles, False)

    near_shapes = (
        shape_of(nt, window, SUB, cols),
        shape_of(3, window, SUB, cols),
        shape_of(2, window, SUB, cols),
        shape_of(4, blocks, SUB, cols),
        shape_of(3, blocks, SUB, cols),
        shape_of(3, blocks, SUB, cols),
    )
    h_scratch = (pltpu.VMEM((nt, (window + 2) * SUB, cols), F32), pltpu.VMEM(((window + 2) * SUB, cols), F32))
    w_scratch = (pltpu.VMEM((4, (blocks + 2) * SUB, cols), F32), pltpu.VMEM(((blocks + 2) * SUB, cols), F32))
    kernel = lambda f, *more: functools.partial(f, plan, *more)

    p, q, pq, top_fields, chl = call(
        kernel(pack_kernel),
        (
            shape_of(p_rows, cols),
            shape_of(plan.q_rows[0], cols),
            shape_of(p_rows + plan.q_rows[0], cols),
            shape_of(4, top, cols),
            shape_of(lev, cols),
        ),
        tuple(
            pltpu.with_memory_space_constraint(v, pltpu.HBM) for v in (wet_levels.reshape(1, cols), fields, tracers)
        ),
        specs=[HBM] * 3,
        scratch=[
            pltpu.VMEM((1, cols), jnp.int32),
            pltpu.VMEM((nt, SUB, cols), F32),
            pltpu.VMEM((nf, top, cols), F32),
            pltpu.SemaphoreType.DMA((6,)),
        ],
    )
    cross_p = sent(p, across)
    lagged = sent(top_fields, over_comp((1,), tiles))
    core = sent(pq, within)
    cross_q = sent(q, across)
    n = -(-nt // 2) * 2 * SUB
    matrix, rates = call(
        matrix_kernel, (jax.ShapeDtypeStruct((2 * n, n), BF16), shape_of(nt, cols)), (reaction,)
    )

    near = call(
        kernel(near_kernel, False),
        near_shapes,
        (neighbours, fields, lagged, fields, pq, core, chl),
        cost=8_000_000,
    )
    p_one, edge = call(
        kernel(upper_kernel),
        (shape_of(p_rows, cols), shape_of(nt, SUB, cols)),
        (matrix, neighbours, pq, cross_p, *near[:3]),
        scratch=h_scratch,
        cost=8_000_000,
    )
    cross_p_one = sent(p_one, across)
    q_one, pq_one, ocean_one, over_one, rest_one = call(
        kernel(lower_kernel),
        (
            shape_of(plan.q_rows[1], cols),
            shape_of(p_rows + plan.q_rows[1], cols),
            shape_of(nf, lev, cols),
            shape_of(4, lev - tall, cols),
            shape_of(3 * (lev + tall), cols),
        ),
        (matrix, neighbours, fields, pq, cross_p, cross_q, *near, p_one, edge),
        scratch=h_scratch + w_scratch,
        cost=8_000_000,
    )
    over = sent(over_one, over_comp((0, 1), tiles))
    core_one = sent(pq_one, within)
    cross_q_one = sent(q_one, across)
    rest = sent(rest_one, over_comp((0,), tiles))

    *near, chl_one = call(
        kernel(near_kernel, True),
        near_shapes + (shape_of(lev, cols),),
        (neighbours, ocean_one, ocean_one, over, pq_one, core_one, p_one, over),
        cost=8_000_000,
    )
    upper = call(
        kernel(chl_kernel),
        shape_of(top, cols),
        (rates, neighbours, pq_one, cross_p_one, *near[:3]),
        scratch=h_scratch,
        cost=8_000_000,
    )
    upper = sent(upper, over_comp((0,), tiles))
    ocean_two, mine = call(
        kernel(second_kernel),
        (shape_of(nf, lev, cols), shape_of(lev - tall, cols)),
        (rates, neighbours, ocean_one, pq_one, cross_p_one, cross_q_one, *near),
        scratch=h_scratch + w_scratch,
        cost=8_000_000,
    )
    ocean_out, chl_out = call(
        kernel(merge_kernel),
        (shape_of(nf, lev, cols), shape_of(lev, cols)),
        (ocean_two, over, rest, chl_one, mine, upper),
    )
    return (ocean_out[None], chl_out[None])


def solution(mesh):
    return jax.shard_map(
        per_device,
        mesh=mesh,
        in_specs=(
            P("comp", None, None, "tile"),
            P(None, None, "tile"),
            P(),
            P("tile"),
            P(None, "tile"),
        ),
        out_specs=(P("comp", None, None, "tile"), P("comp", None, "tile")),
        check_vma=False,
    )
```

```python
import functools
import math

import jax
import jax.numpy as jnp
from jax import lax
from jax.experimental import pallas as pl
from jax.experimental.pallas import tpu as pltpu
from jax.sharding import PartitionSpec as P


ROTATE_COS = math.cos(0.3)
ROTATE_SIN = math.sin(0.3)
SUB = 8
AXES = ("comp", "tile")
ANGLES = [2.0 * math.pi * k / 3.0 for k in range(3)]
F32 = jnp.float32
BF16 = jnp.bfloat16
GRANT = 8 << 20


VMEM = pl.BlockSpec(memory_space=pltpu.VMEM)
SMEM = pl.BlockSpec(memory_space=pltpu.SMEM)
HBM = pl.BlockSpec(memory_space=pltpu.HBM)


class Plan:
    def __init__(self, nt, lev):
        self.nt, self.lev = nt, lev
        self.blocks = lev // SUB
        self.full = self.blocks // 2 - 1
        self.window = self.full + 2
        self.half = SUB // 2
        self.halves = SUB * nt * self.full
        self.wet = self.halves + self.half * nt
        self.p_rows = -(-(self.wet + self.half) // SUB) * SUB
        self.q_rows = (
            max(4 * lev, -(-(SUB + self.half) * nt // SUB) * SUB),
            max(4 * lev, 2 * SUB * nt),
        )

    def rs(self, comp):
        return list(range(1 - comp, self.window))

    def level(self, comp, r):
        return SUB * (r - 1) if comp == 0 else SUB * (self.full + r)

    def rest(self, i):
        tall = SUB * self.full
        return (0, self.lev, 2 * self.lev, 2 * self.lev + tall, 2 * self.lev + 2 * tall, 2 * self.lev + 3 * tall)[i]

    def block(self, comp, second, p, q, j, r):
        if comp == 0:
            return p(SUB * (self.full * j + r - 1)) if r <= self.full else p(self.halves + self.half * j)
        if r < self.full:
            return p(SUB * (self.full * j + r))
        if second:
            return q(SUB * (2 * j + r - self.full))
        if r > self.full:
            return q(SUB * j)
        upper = p(self.halves + self.half * j)
        lower = q(SUB * self.nt + self.half * (j - 1))
        sub = lax.broadcasted_iota(jnp.int32, upper.shape, 0)
        return jnp.where(sub < self.half, upper, lower)


def rows_at(ref, base=0):
    return lambda offset: ref[base + offset : base + offset + SUB, :]


def edge_weights(eastward, northward):
    return [
        0.05 + 0.25 * jax.nn.sigmoid(eastward * math.cos(a) + northward * math.sin(a)) for a in ANGLES
    ]


def take_lanes(block, index):
    return jnp.take_along_axis(block, index, axis=1, mode="promise_in_bounds")


def shape_of(*dims):
    return jax.ShapeDtypeStruct(dims, F32)


def neighbours_of(nb_ref, odd):
    cols = nb_ref.shape[-1]
    core_side = jnp.where(odd == 1, 0, 2)
    index, in_core, in_cross = [], [], []
    for k in range(3):
        nb = jnp.broadcast_to(nb_ref[k : k + 1, :], (SUB, cols))
        side = nb // cols
        index.append(nb - side * cols)
        in_core.append(side == core_side)
        in_cross.append(side == 2 - core_side)
    return index, in_core, in_cross


def level_block(first, cols):
    return lax.broadcasted_iota(jnp.int32, (SUB, cols), 0).astype(F32) + float(first)


def link_weight(level, wet, mixing, last):
    nxt = level + 1.0
    return jnp.where((nxt < wet) & (nxt <= last), 0.02 + 0.13 * jax.nn.sigmoid(mixing), 0.0)


def growth_rate(temperature, salinity, light):
    return 0.5 * light * jax.nn.sigmoid(temperature + 0.5 * salinity)


def wet_of(plan, ref):
    return jnp.broadcast_to(ref[plan.wet : plan.wet + 1, :], (SUB, ref.shape[1]))


def on_side(comp):
    return pl.when(lax.axis_index("comp") == comp)


def pack_kernel(plan, wet_ref, f_ref, t_ref, p_ref, q_ref, pq_ref, top_ref, chl_ref, wet_buf, half_buf, top_buf, sems):
    nt, full, half, lev = plan.nt, plan.full, plan.half, plan.lev
    tall = SUB * full
    first = pl.multiple_of(lax.axis_index("comp") * tall, SUB)
    copies = [
        (t_ref.at[:, pl.ds(first, tall)], p_ref.at[pl.ds(0, plan.halves)].reshape(nt, tall, p_ref.shape[1])),
        (t_ref.at[:, pl.ds(pl.multiple_of(first + tall, SUB), SUB)], half_buf),
        (wet_ref, wet_buf),
        (f_ref.at[:, pl.ds(0, top_ref.shape[1])], top_buf),
        (t_ref.at[0], chl_ref),
    ]
    copies = [pltpu.make_async_copy(s, d, sems.at[i]) for i, (s, d) in enumerate(copies)]
    for c in copies:
        c.start()
    base = len(copies)
    slab = lambda n, rows: q_ref.at[pl.ds(0, n * rows)].reshape(n, rows, q_ref.shape[1])
    ocean = [pltpu.make_async_copy(f_ref.at[pl.ds(0, 4)], slab(4, lev), sems.at[base])]
    deep = [pltpu.make_async_copy(t_ref.at[:, pl.ds(lev - SUB, SUB)], slab(nt, SUB), sems.at[base])]

    @on_side(0)
    def _():
        for c in ocean:
            c.start()

    @on_side(1)
    def _():
        for c in deep:
            c.start()

    for c in copies:
        c.wait()
    p_ref[plan.wet : plan.wet + half, :] = jnp.broadcast_to(wet_buf[...].astype(F32), (half, wet_buf.shape[1]))
    for j in range(nt):
        p_ref[plan.halves + half * j : plan.halves + half * (j + 1), :] = half_buf[j, 0:half, :]

    @on_side(0)
    def _():
        for c in ocean:
            c.wait()

    @on_side(1)
    def _():
        for c in deep:
            c.wait()
        top_ref[0] = growth_rate(top_buf[0], top_buf[1], top_buf[5])
        top_ref[1:4] = top_buf[2:5]
        for j in range(nt):
            at = SUB * nt + half * j
            q_ref[at : at + half, :] = half_buf[j, half:SUB, :]

    pq_ref[0 : plan.p_rows, :] = p_ref[...]
    pq_ref[plan.p_rows :, :] = q_ref[...]


def matrix_kernel(r_ref, out_ref, first_ref):
    nt = r_ref.shape[0]
    rows, n = out_ref.shape
    p = lax.broadcasted_iota(jnp.int32, (n, nt), 0)
    spread = (p // SUB == lax.broadcasted_iota(jnp.int32, (n, nt), 1)).astype(F32)
    exact = functools.partial(
        lax.dot_general, precision=lax.Precision.HIGHEST, preferred_element_type=F32
    )
    tall = exact(spread, r_ref[...], (((1,), (0,)), ((), ())))
    full = exact(tall, spread, (((1,), (1,)), ((), ())))
    a = lax.broadcasted_iota(jnp.int32, (n, n), 0)
    b = lax.broadcasted_iota(jnp.int32, (n, n), 1)
    full = jnp.where(a % SUB == b % SUB, full, 0.0)
    high = full.astype(BF16)
    out_ref[0:n, :] = high
    out_ref[n:rows, :] = (full - high.astype(F32)).astype(BF16)
    ones = jnp.ones((1, first_ref.shape[1]), F32)
    first_ref[...] = exact(r_ref[0:1, :], ones, (((0,), (0,)), ((), ())))


def near_kernel(plan, second, nb_ref, f_ref, ga_ref, gb_ref, pq_ref, core_ref, chl_ref, *refs):
    if second:
        chl_low_ref, *refs = refs
    part_ref, far_ref, aux_ref, opart_ref, ofar_ref, oaux_ref = refs[:6]
    chl_out_ref = refs[6] if second else None
    odd = lax.axis_index("tile") % 2
    cols = nb_ref.shape[-1]
    nt, p_rows = plan.nt, plan.p_rows
    index, in_core, in_cross = neighbours_of(nb_ref, odd)
    wet, wet_core = wet_of(plan, pq_ref), wet_of(plan, core_ref)
    near_wet = []
    for k in range(3):
        found = jnp.where(in_core[k], take_lanes(wet_core, index[k]), take_lanes(wet, index[k]))
        near_wet.append(jnp.where(in_cross[k], 0.0, found))
    last = float(plan.lev - 1)

    def split(level, ws):
        active = level < wet
        near = [jnp.where(active & (level < near_wet[k]), ws[k], 0.0) for k in range(3)]
        far = [jnp.where(active & in_cross[k], ws[k], 0.0) for k in range(3)]
        return near, far

    def moves(own, core, near, rest):
        totals = [o * r for o, r in zip(own, rest)]
        for k in range(3):
            for j in range(len(own)):
                v = jnp.where(in_core[k], take_lanes(core[j], index[k]), take_lanes(own[j], index[k]))
                totals[j] = totals[j] + near[j][k] * v
        return totals

    def tracers(comp):
        for r in plan.rs(comp):
            first = plan.level(comp, r)
            level = level_block(first, cols)
            passed = comp == int(second)
            ref, at = (gb_ref if comp else ga_ref), first - SUB * plan.full * int(passed and comp)
            g = [ref[i, at : at + SUB, :] for i in range(4 if passed else 6)]
            if not passed:
                g = [growth_rate(g[0], g[1], g[5])] + g[2:5]
            near, far = split(level, edge_weights(g[1], g[2]))
            rest = 1.0 - (near[0] + near[1] + near[2])
            for k in range(3):
                far_ref[k, r] = far[k]
            aux_ref[0, r] = link_weight(level, wet, g[3], last)
            aux_ref[1, r] = g[0]
            own = [plan.block(comp, second, rows_at(pq_ref), rows_at(pq_ref, p_rows), j, r) for j in range(nt)]
            core = [plan.block(comp, second, rows_at(core_ref), rows_at(core_ref, p_rows), j, r) for j in range(nt)]
            for j, v in enumerate(moves(own, core, [near] * nt, [rest] * nt)):
                part_ref[j, r] = v

    @on_side(1)
    def _():
        tracers(1)

    @on_side(0)
    def _():
        tracers(0)
        top = f_ref[5, 0:1, :]
        cut = SUB * (plan.full + 1) - SUB + 2

        def chl_block(b):
            at = SUB * b
            if not second:
                return chl_ref[at : at + SUB, :]
            if b < plan.full:
                return chl_ref[at : at + SUB, :]
            v = chl_low_ref[0, at - SUB * plan.full : at - SUB * plan.full + SUB, :]
            if b > plan.full:
                return v
            return jnp.where(level_block(at, cols) < float(cut), chl_ref[plan.halves : plan.halves + SUB, :], v)

        run = jnp.zeros((1, cols), F32)
        for b in range(plan.blocks):
            x = chl_block(b)
            if second:
                chl_out_ref[SUB * b : SUB * (b + 1), :] = x
            absorbed = 0.01 + 0.3 * (jnp.maximum(x, 0.0) + jnp.log1p(jnp.exp(-jnp.abs(x))))
            level = level_block(SUB * b, cols)
            sub = lax.broadcasted_iota(jnp.int32, (SUB, cols), 0)
            cum = absorbed
            for d in (1, 2, 4):
                cum = cum + jnp.where(sub >= d, pltpu.roll(cum, d, 0), 0.0)
            depth = cum + run
            ceiling = jnp.exp(-(depth - absorbed))
            oaux_ref[1, b] = 4.0 * top * (ceiling - jnp.exp(-depth))
            oaux_ref[2, b] = jnp.where(level < wet, top * ceiling, 0.0)
            run = depth[SUB - 1 : SUB, :]

        for b in range(plan.blocks):
            at = SUB * b
            level = level_block(at, cols)
            f = [f_ref[i, at : at + SUB, :] for i in range(5)]
            near, far = split(level, edge_weights(f[2], f[3]))
            rest = 1.0 - (near[0] + near[1] + near[2])
            flat = [jnp.where(v > 0.0, 0.15, 0.0) for v in near]
            rest_flat = 1.0 - (flat[0] + flat[1] + flat[2])
            for k in range(3):
                ofar_ref[k, b] = far[k]
            oaux_ref[0, b] = link_weight(level, wet, f[4], last)
            core = [rows_at(core_ref, p_rows)(plan.lev * i + at) for i in range(4)]
            out = moves(f[:4], core, [near, near, flat, flat], [rest, rest, rest_flat, rest_flat])
            for i in range(4):
                opart_ref[i, b] = out[i]


def far_wet(index, in_cross, wet_cross):
    return [jnp.where(in_cross[k], take_lanes(wet_cross, index[k]), 0.0) for k in range(3)]


def far_moves(parts, own, cross, far, index):
    totals = [p - o * (f[0] + f[1] + f[2]) for p, o, f in zip(parts, own, far)]
    for k in range(3):
        for j in range(len(own)):
            totals[j] = totals[j] + far[j][k] * take_lanes(cross[j], index[k])
    return totals


class Far:
    def __init__(self, plan, comp, second, nb_ref, pq_ref, cross_p_ref, part_ref, far_ref, aux_ref, h_ref, l_ref):
        self.plan, self.comp, self.second = plan, comp, second
        self.cols = nb_ref.shape[-1]
        self.own_p, self.own_q = rows_at(pq_ref), rows_at(pq_ref, plan.p_rows)
        self.part, self.far, self.aux, self.h, self.l = part_ref, far_ref, aux_ref, h_ref, l_ref
        self.index, _, in_cross = neighbours_of(nb_ref, lax.axis_index("tile") % 2)
        self.wet = wet_of(plan, pq_ref)
        self.wets = far_wet(self.index, in_cross, wet_of(plan, cross_p_ref))

    def at(self, r):
        return SUB * (r + 1)

    def clear(self, before, after):
        zero = jnp.zeros((SUB, self.cols), F32)
        if before is not None:
            self.l[self.at(before) : self.at(before) + SUB, :] = zero
        for j in range(self.plan.nt):
            for r in (before, after):
                if r is not None:
                    self.h[j, self.at(r) : self.at(r) + SUB, :] = zero

    def move(self, r, p, q):
        plan, at = self.plan, self.at(r)
        level = level_block(plan.level(self.comp, r), self.cols)
        far = [jnp.where(level < self.wets[k], self.far[k, r], 0.0) for k in range(3)]
        self.l[at : at + SUB, :] = self.aux[0, r]
        js = range(plan.nt)
        parts = [self.part[j, r] for j in js]
        own = [plan.block(self.comp, self.second, self.own_p, self.own_q, j, r) for j in js]
        cross = [plan.block(self.comp, self.second, p, q, j, r) for j in js]
        for j, v in enumerate(far_moves(parts, own, cross, [far] * plan.nt, self.index)):
            self.h[j, at : at + SUB, :] = v

    def react(self, r, react_ref, put):
        plan, at = self.plan, self.at(r)
        active = (level_block(plan.level(self.comp, r), self.cols) < self.wet).astype(F32)
        down, up = self.l[at : at + SUB, :], self.l[at - 1 : at - 1 + SUB, :]
        ys, ts = [], []
        for j in range(plan.nt):
            v = self.h[j, at : at + SUB, :]
            y = v + down * (self.h[j, at + 1 : at + 1 + SUB, :] - v) - up * (v - self.h[j, at - 1 : at - 1 + SUB, :])
            ys.append(y)
            ts.append(jnp.tanh(y))
        growth = self.aux[1, r]
        if self.second:
            total = react_ref[0:1, :] * ts[0]
            for j in range(1, plan.nt):
                total = total + react_ref[j : j + 1, :] * ts[j]
            put(0, r, (ys[0] + growth * total) * active)
            return
        n = react_ref.shape[1]
        ts += [jnp.zeros_like(ts[0])] * (n // SUB - plan.nt)
        stack = jnp.concatenate(ts, axis=0)
        high = stack.astype(BF16)
        rest = (stack - high.astype(F32)).astype(BF16)
        both = jnp.dot(react_ref[...], high, preferred_element_type=F32)
        total = both[:n] + both[n:] + jnp.dot(react_ref[0:n, :], rest, preferred_element_type=F32)
        for i in range(plan.nt):
            put(i, r, (ys[i] + growth * total[i * SUB : (i + 1) * SUB]) * active)


def nothing(offset):
    raise ValueError("not there")


def upper_kernel(plan, react_ref, nb_ref, pq_ref, p_ref, part_ref, far_ref, aux_ref, out_ref, edge_ref, h_ref, l_ref):
    out_ref[plan.wet : plan.wet + plan.half, :] = pq_ref[plan.wet : plan.wet + plan.half, :]
    refs = (nb_ref, pq_ref, p_ref, part_ref, far_ref, aux_ref, h_ref, l_ref)
    p = rows_at(p_ref)

    @on_side(0)
    def _():
        work = Far(plan, 0, False, *refs)
        work.clear(0, plan.window)
        for r in plan.rs(0):
            work.move(r, p, nothing)

        def put(i, r, value):
            if r <= plan.full:
                at = SUB * (plan.full * i + r - 1)
                out_ref[at : at + SUB, :] = value
            else:
                at = plan.halves + plan.half * i
                out_ref[at : at + plan.half, :] = value[0 : plan.half]

        for r in plan.rs(0):
            work.react(r, react_ref, put)

    @on_side(1)
    def _():
        work = Far(plan, 1, False, *refs)
        work.clear(-1, None)
        lower = lambda offset: jnp.zeros((SUB, work.cols), F32)
        for r in range(plan.full + 1):
            work.move(r, p, lower)
        at = work.at(plan.full - 1)
        for j in range(plan.nt):
            edge_ref[j] = h_ref[j, at : at + SUB, :]

        def put(i, r, value):
            at = SUB * (plan.full * i + r)
            out_ref[at : at + SUB, :] = value

        for r in range(plan.full):
            work.react(r, react_ref, put)


def ocean_far(plan, nb_ref, f_ref, pq_ref, p_ref, q_ref, opart_ref, ofar_ref, oaux_ref, w_ref, l_ref, put):
    cols = nb_ref.shape[-1]
    index, _, in_cross = neighbours_of(nb_ref, lax.axis_index("tile") % 2)
    wet = wet_of(plan, pq_ref)
    wets = far_wet(index, in_cross, wet_of(plan, p_ref))
    zero = jnp.zeros((SUB, cols), F32)
    end = SUB * (plan.blocks + 1)
    l_ref[0:SUB, :] = zero
    for i in range(4):
        w_ref[i, 0:SUB, :] = zero
        w_ref[i, end : end + SUB, :] = zero
    for b in range(plan.blocks):
        at = SUB * b
        level = level_block(at, cols)
        far = [jnp.where(level < wets[k], ofar_ref[k, b], 0.0) for k in range(3)]
        flat = [jnp.where(v > 0.0, 0.15, 0.0) for v in far]
        there = slice(at + SUB, at + 2 * SUB)
        l_ref[there, :] = oaux_ref[0, b]
        parts = [opart_ref[i, b] for i in range(4)]
        own = [f_ref[i, at : at + SUB, :] for i in range(4)]
        cross = [rows_at(q_ref)(plan.lev * i + at) for i in range(4)]
        q = far_moves(parts, own, cross, [far, far, flat, flat], index)
        w_ref[0, there, :] = q[0]
        w_ref[1, there, :] = q[1]
        w_ref[2, there, :] = ROTATE_COS * q[2] + ROTATE_SIN * q[3]
        w_ref[3, there, :] = -ROTATE_SIN * q[2] + ROTATE_COS * q[3]
    warm = [None] * plan.blocks
    for b in range(plan.blocks):
        at = SUB * (b + 1)
        active = (level_block(SUB * b, cols) < wet).astype(F32)
        down, up = l_ref[at : at + SUB, :], l_ref[at - 1 : at - 1 + SUB, :]
        for i in range(4):
            v = w_ref[i, at : at + SUB, :]
            y = v + down * (w_ref[i, at + 1 : at + 1 + SUB, :] - v) - up * (v - w_ref[i, at - 1 : at - 1 + SUB, :])
            if i == 0:
                warm[b] = y + oaux_ref[1, b]
                put(0, b, warm[b] * active)
            else:
                put(i, b, y * active)
        put(5, b, oaux_ref[2, b])
    sub = lax.broadcasted_iota(jnp.int32, (SUB, cols), 0)
    for b in range(plan.blocks):
        active = (level_block(SUB * b, cols) < wet).astype(F32)
        lower = pltpu.roll(warm[b], SUB - 1, 0)
        if b + 1 < plan.blocks:
            lower = jnp.where(sub == SUB - 1, pltpu.roll(warm[b + 1], SUB - 1, 0), lower)
        else:
            lower = jnp.where(sub == SUB - 1, warm[b], lower)
        put(4, b, (warm[b] - lower) * active)


def lower_kernel(
    plan, react_ref, nb_ref, f_ref, pq_ref, p_ref, q_ref, part_ref, far_ref, aux_ref, opart_ref, ofar_ref, oaux_ref,
    done_ref, edge_ref, out_ref, both_ref, ocean_ref, over_ref, rest_ref, h_ref, l_ref, w_ref, wl_ref,
):
    both_ref[0 : plan.p_rows, :] = done_ref[...]

    @on_side(0)
    def _():
        def put(i, b, value):
            at = SUB * b
            ocean_ref[i, at : at + SUB, :] = value
            if 2 <= i < 5 and b >= plan.full:
                over_ref[i - 1, at - SUB * plan.full : at - SUB * plan.full + SUB, :] = value
            else:
                rest_ref[plan.rest(i) + at : plan.rest(i) + at + SUB, :] = value
            if i < 4:
                for ref, base in ((out_ref, 0), (both_ref, plan.p_rows)):
                    ref[base + plan.lev * i + at : base + plan.lev * i + at + SUB, :] = value

        ocean_far(plan, nb_ref, f_ref, pq_ref, p_ref, q_ref, opart_ref, ofar_ref, oaux_ref, w_ref, wl_ref, put)
        tall = SUB * plan.full
        over_ref[0] = growth_rate(ocean_ref[0, tall:, :], ocean_ref[1, tall:, :], ocean_ref[5, tall:, :])

    @on_side(1)
    def _():
        work = Far(plan, 1, False, nb_ref, pq_ref, p_ref, part_ref, far_ref, aux_ref, h_ref, l_ref)
        work.clear(None, plan.window)
        before = work.at(plan.full - 1)
        l_ref[before : before + SUB, :] = aux_ref[0, plan.full - 1]
        for j in range(plan.nt):
            h_ref[j, before : before + SUB, :] = edge_ref[j]
        rs = (plan.full, plan.full + 1)
        for r in rs:
            work.move(r, rows_at(p_ref), rows_at(q_ref))

        def put(i, r, value):
            at = SUB * (2 * i + r - plan.full)
            out_ref[at : at + SUB, :] = value
            both_ref[plan.p_rows + at : plan.p_rows + at + SUB, :] = value
            if i == 0:
                over_ref[0, SUB * r : SUB * (r + 1), :] = value

        for r in rs:
            work.react(r, react_ref, put)
        for r in range(plan.full):
            over_ref[0, SUB * r : SUB * (r + 1), :] = done_ref[SUB * r : SUB * (r + 1), :]


def chl_kernel(plan, react_ref, nb_ref, pq_ref, p_ref, part_ref, far_ref, aux_ref, out_ref, h_ref, l_ref):
    @on_side(0)
    def _():
        work = Far(plan, 0, True, nb_ref, pq_ref, p_ref, part_ref, far_ref, aux_ref, h_ref, l_ref)
        work.clear(0, plan.window)
        for r in plan.rs(0):
            work.move(r, rows_at(p_ref), nothing)

        def put(i, r, value):
            out_ref[SUB * (r - 1) : SUB * r, :] = value

        for r in plan.rs(0):
            work.react(r, react_ref, put)


def second_kernel(
    plan, react_ref, nb_ref, f_ref, pq_ref, p_ref, q_ref, part_ref, far_ref, aux_ref, opart_ref,
    ofar_ref, oaux_ref, out_ref, mine_ref, h_ref, l_ref, w_ref, wl_ref,
):
    @on_side(0)
    def _():
        def put(i, b, value):
            out_ref[i, SUB * b : SUB * (b + 1), :] = value

        ocean_far(plan, nb_ref, f_ref, pq_ref, p_ref, q_ref, opart_ref, ofar_ref, oaux_ref, w_ref, wl_ref, put)

    @on_side(1)
    def _():
        work = Far(plan, 1, True, nb_ref, pq_ref, p_ref, part_ref, far_ref, aux_ref, h_ref, l_ref)
        work.clear(-1, plan.window)
        for r in plan.rs(1):
            work.move(r, rows_at(p_ref), rows_at(q_ref))

        def put(i, r, value):
            mine_ref[SUB * r : SUB * (r + 1), :] = value

        for r in plan.rs(1):
            work.react(r, react_ref, put)


def merge_kernel(plan, ocean_ref, over_ref, rest_ref, chl_ref, mine_ref, upper_ref, out_ref, chl_out_ref):
    tall = SUB * plan.full

    @on_side(0)
    def _():
        out_ref[...] = ocean_ref[...]
        chl_out_ref[...] = chl_ref[...]

    @on_side(1)
    def _():
        for i in range(6):
            at = plan.rest(i)
            if 2 <= i < 5:
                out_ref[i, 0:tall, :] = rest_ref[at : at + tall, :]
                out_ref[i, tall:, :] = over_ref[i - 1]
            else:
                out_ref[i] = rest_ref[at : at + plan.lev, :]
        sub = lax.broadcasted_iota(jnp.int32, (SUB, chl_out_ref.shape[1]), 0)
        chl_out_ref[0:tall, :] = upper_ref[0:tall, :]
        chl_out_ref[tall : tall + SUB, :] = jnp.where(sub < 2, upper_ref[tall : tall + SUB, :], mine_ref[0:SUB, :])
        chl_out_ref[tall + SUB :, :] = mine_ref[SUB:, :]


def call(kernel, outs, ins, specs=None, scratch=(), cost=1_000_000):
    return pl.pallas_call(
        kernel,
        out_shape=outs,
        in_specs=specs or [VMEM] * len(ins),
        out_specs=jax.tree.map(lambda _: VMEM, outs),
        scratch_shapes=list(scratch),
        compiler_params=pltpu.CompilerParams(vmem_limit_bytes=GRANT),
        cost_estimate=pl.CostEstimate(flops=cost, bytes_accessed=1_000_000, transcendentals=0),
    )(*ins)


def swaps(tiles, across):
    pairs = []
    for c in (0, 1):
        for t in range(tiles):
            other = (t + 1) % tiles if (t % 2 == 0) != across else (t - 1) % tiles
            pairs.append((c * tiles + t, c * tiles + other))
    return pairs


def over_comp(tiles):
    return [(c * tiles + t, (1 - c) * tiles + t) for c in (0, 1) for t in range(tiles)]


def sent(v, pairs):
    return lax.ppermute(v, AXES, pairs)


def per_device(ocean_fields, tracers, reaction, wet_levels, neighbours):
    tiles = lax.axis_size("tile")
    nt, lev, cols = tracers.shape
    plan = Plan(nt, lev)
    blocks, window, p_rows = plan.blocks, plan.window, plan.p_rows
    fields = ocean_fields.reshape(-1, lev, cols)
    nf = fields.shape[0]
    top, tall = SUB * (plan.full + 1), SUB * plan.full
    across, within = swaps(tiles, True), swaps(tiles, False)

    near_shapes = (
        shape_of(nt, window, SUB, cols),
        shape_of(3, window, SUB, cols),
        shape_of(2, window, SUB, cols),
        shape_of(4, blocks, SUB, cols),
        shape_of(3, blocks, SUB, cols),
        shape_of(3, blocks, SUB, cols),
    )
    h_scratch = (pltpu.VMEM((nt, (window + 2) * SUB, cols), F32), pltpu.VMEM(((window + 2) * SUB, cols), F32))
    w_scratch = (pltpu.VMEM((4, (blocks + 2) * SUB, cols), F32), pltpu.VMEM(((blocks + 2) * SUB, cols), F32))
    kernel = lambda f, *more: functools.partial(f, plan, *more)

    p, q, pq, top_fields, chl = call(
        kernel(pack_kernel),
        (
            shape_of(p_rows, cols),
            shape_of(plan.q_rows[0], cols),
            shape_of(p_rows + plan.q_rows[0], cols),
            shape_of(4, top, cols),
            shape_of(lev, cols),
        ),
        tuple(
            pltpu.with_memory_space_constraint(v, pltpu.HBM) for v in (wet_levels.reshape(1, cols), fields, tracers)
        ),
        specs=[HBM] * 3,
        scratch=[
            pltpu.VMEM((1, cols), jnp.int32),
            pltpu.VMEM((nt, SUB, cols), F32),
            pltpu.VMEM((nf, top, cols), F32),
            pltpu.SemaphoreType.DMA((6,)),
        ],
    )
    cross_p = sent(p, across)
    lagged = sent(top_fields, over_comp(tiles))
    core = sent(pq, within)
    cross_q = sent(q, across)
    n = -(-nt // 2) * 2 * SUB
    matrix, rates = call(
        matrix_kernel, (jax.ShapeDtypeStruct((2 * n, n), BF16), shape_of(nt, cols)), (reaction,)
    )

    near = call(
        kernel(near_kernel, False),
        near_shapes,
        (neighbours, fields, lagged, fields, pq, core, chl),
        cost=8_000_000,
    )
    p_one, edge = call(
        kernel(upper_kernel),
        (shape_of(p_rows, cols), shape_of(nt, SUB, cols)),
        (matrix, neighbours, pq, cross_p, *near[:3]),
        scratch=h_scratch,
        cost=8_000_000,
    )
    cross_p_one = sent(p_one, across)
    q_one, pq_one, ocean_one, over_one, rest_one = call(
        kernel(lower_kernel),
        (
            shape_of(plan.q_rows[1], cols),
            shape_of(p_rows + plan.q_rows[1], cols),
            shape_of(nf, lev, cols),
            shape_of(4, lev - tall, cols),
            shape_of(3 * (lev + tall), cols),
        ),
        (matrix, neighbours, fields, pq, cross_p, cross_q, *near, p_one, edge),
        scratch=h_scratch + w_scratch,
        cost=8_000_000,
    )
    over = sent(over_one, over_comp(tiles))
    core_one = sent(pq_one, within)
    cross_q_one = sent(q_one, across)
    rest = sent(rest_one, over_comp(tiles))

    *near, chl_one = call(
        kernel(near_kernel, True),
        near_shapes + (shape_of(lev, cols),),
        (neighbours, ocean_one, ocean_one, over, pq_one, core_one, p_one, over),
        cost=8_000_000,
    )
    upper = call(
        kernel(chl_kernel),
        shape_of(top, cols),
        (rates, neighbours, pq_one, cross_p_one, *near[:3]),
        scratch=h_scratch,
        cost=8_000_000,
    )
    upper = sent(upper, over_comp(tiles))
    ocean_two, mine = call(
        kernel(second_kernel),
        (shape_of(nf, lev, cols), shape_of(lev - tall, cols)),
        (rates, neighbours, ocean_one, pq_one, cross_p_one, cross_q_one, *near),
        scratch=h_scratch + w_scratch,
        cost=8_000_000,
    )
    ocean_out, chl_out = call(
        kernel(merge_kernel),
        (shape_of(nf, lev, cols), shape_of(lev, cols)),
        (ocean_two, over, rest, chl_one, mine, upper),
    )
    return (ocean_out[None], chl_out[None])


def solution(mesh):
    return jax.shard_map(
        per_device,
        mesh=mesh,
        in_specs=(
            P("comp", None, None, "tile"),
            P(None, None, "tile"),
            P(),
            P("tile"),
            P(None, "tile"),
        ),
        out_specs=(P("comp", None, None, "tile"), P("comp", None, "tile")),
        check_vma=False,
    )
```

```python
import functools
import math

import jax
import jax.numpy as jnp
from jax import lax
from jax.experimental import pallas as pl
from jax.experimental.pallas import tpu as pltpu
from jax.sharding import PartitionSpec as P


ROTATE_COS = math.cos(0.3)
ROTATE_SIN = math.sin(0.3)
SUB = 8
AXES = ("comp", "tile")
ANGLES = [2.0 * math.pi * k / 3.0 for k in range(3)]
F32 = jnp.float32
BF16 = jnp.bfloat16
GRANT = 8 << 20


VMEM = pl.BlockSpec(memory_space=pltpu.VMEM)
SMEM = pl.BlockSpec(memory_space=pltpu.SMEM)
HBM = pl.BlockSpec(memory_space=pltpu.HBM)


class Plan:
    def __init__(self, nt, lev):
        self.nt, self.lev = nt, lev
        self.blocks = lev // SUB
        self.full = self.blocks // 2 - 1
        self.window = self.full + 2
        self.half = SUB // 2
        self.halves = SUB * nt * self.full
        self.wet = self.halves + self.half * nt
        self.p_rows = -(-(self.wet + self.half) // SUB) * SUB
        self.edges = (SUB + self.half) * nt
        self.q_rows = max(4 * lev, -(-(self.edges + nt + SUB) // SUB) * SUB)

    def rs(self, comp):
        return list(range(1 - comp, self.window))

    def level(self, comp, r):
        return SUB * (r - 1) if comp == 0 else SUB * (self.full + r)

    def rest(self, i):
        tall = SUB * self.full
        return (0, self.lev, 2 * self.lev, 2 * self.lev + tall, 2 * self.lev + 2 * tall, 2 * self.lev + 3 * tall)[i]

    def block(self, comp, second, p, q, j, r):
        if comp == 0:
            return p(SUB * (self.full * j + r - 1)) if r <= self.full else p(self.halves + self.half * j)
        if r < self.full:
            return p(SUB * (self.full * j + r))
        if r > self.full:
            return q(SUB * j)
        upper = p(self.halves + self.half * j)
        lower = q(SUB * self.nt + self.half * (j - 1))
        sub = lax.broadcasted_iota(jnp.int32, upper.shape, 0)
        if second:
            edge = self.half - 1
            lower = jnp.where(sub == edge, q(self.edges + j - edge), lower)
            return jnp.where(sub < edge, upper, lower)
        return jnp.where(sub < self.half, upper, lower)


def rows_at(ref, base=0):
    return lambda offset: ref[base + offset : base + offset + SUB, :]


def edge_weights(eastward, northward):
    return [
        0.05 + 0.25 * jax.nn.sigmoid(eastward * math.cos(a) + northward * math.sin(a)) for a in ANGLES
    ]


def take_lanes(block, index):
    return jnp.take_along_axis(block, index, axis=1, mode="promise_in_bounds")


def shape_of(*dims):
    return jax.ShapeDtypeStruct(dims, F32)


def neighbours_of(nb_ref, odd):
    cols = nb_ref.shape[-1]
    core_side = jnp.where(odd == 1, 0, 2)
    index, in_core, in_cross = [], [], []
    for k in range(3):
        nb = jnp.broadcast_to(nb_ref[k : k + 1, :], (SUB, cols))
        side = nb // cols
        index.append(nb - side * cols)
        in_core.append(side == core_side)
        in_cross.append(side == 2 - core_side)
    return index, in_core, in_cross


def level_block(first, cols):
    return lax.broadcasted_iota(jnp.int32, (SUB, cols), 0).astype(F32) + float(first)


def link_weight(level, wet, mixing, last):
    nxt = level + 1.0
    return jnp.where((nxt < wet) & (nxt <= last), 0.02 + 0.13 * jax.nn.sigmoid(mixing), 0.0)


def growth_rate(temperature, salinity, light):
    return 0.5 * light * jax.nn.sigmoid(temperature + 0.5 * salinity)


def wet_of(plan, ref):
    return jnp.broadcast_to(ref[plan.wet : plan.wet + 1, :], (SUB, ref.shape[1]))


def on_side(comp):
    return pl.when(lax.axis_index("comp") == comp)


def pack_kernel(plan, wet_ref, f_ref, t_ref, p_ref, q_ref, pq_ref, top_ref, chl_ref, wet_buf, half_buf, top_buf, sems):
    nt, full, half, lev = plan.nt, plan.full, plan.half, plan.lev
    tall = SUB * full
    first = pl.multiple_of(lax.axis_index("comp") * tall, SUB)
    copies = [
        (t_ref.at[:, pl.ds(first, tall)], p_ref.at[pl.ds(0, plan.halves)].reshape(nt, tall, p_ref.shape[1])),
        (t_ref.at[:, pl.ds(pl.multiple_of(first + tall, SUB), SUB)], half_buf),
        (wet_ref, wet_buf),
        (f_ref.at[:, pl.ds(0, top_ref.shape[1])], top_buf),
        (t_ref.at[0], chl_ref),
    ]
    copies = [pltpu.make_async_copy(s, d, sems.at[i]) for i, (s, d) in enumerate(copies)]
    for c in copies:
        c.start()
    base = len(copies)
    slab = lambda n, rows: q_ref.at[pl.ds(0, n * rows)].reshape(n, rows, q_ref.shape[1])
    ocean = [pltpu.make_async_copy(f_ref.at[pl.ds(0, 4)], slab(4, lev), sems.at[base])]
    deep = [pltpu.make_async_copy(t_ref.at[:, pl.ds(lev - SUB, SUB)], slab(nt, SUB), sems.at[base])]

    @on_side(0)
    def _():
        for c in ocean:
            c.start()

    @on_side(1)
    def _():
        for c in deep:
            c.start()

    for c in copies:
        c.wait()
    p_ref[plan.wet : plan.wet + half, :] = jnp.broadcast_to(wet_buf[...].astype(F32), (half, wet_buf.shape[1]))
    for j in range(nt):
        p_ref[plan.halves + half * j : plan.halves + half * (j + 1), :] = half_buf[j, 0:half, :]

    @on_side(0)
    def _():
        for c in ocean:
            c.wait()

    @on_side(1)
    def _():
        for c in deep:
            c.wait()
        top_ref[0] = growth_rate(top_buf[0], top_buf[1], top_buf[5])
        top_ref[1:4] = top_buf[2:5]
        for j in range(nt):
            at = SUB * nt + half * j
            q_ref[at : at + half, :] = half_buf[j, half:SUB, :]

    pq_ref[0 : plan.p_rows, :] = p_ref[...]
    pq_ref[plan.p_rows :, :] = q_ref[...]


def matrix_kernel(r_ref, out_ref, first_ref):
    nt = r_ref.shape[0]
    rows, n = out_ref.shape
    p = lax.broadcasted_iota(jnp.int32, (n, nt), 0)
    spread = (p // SUB == lax.broadcasted_iota(jnp.int32, (n, nt), 1)).astype(F32)
    exact = functools.partial(
        lax.dot_general, precision=lax.Precision.HIGHEST, preferred_element_type=F32
    )
    tall = exact(spread, r_ref[...], (((1,), (0,)), ((), ())))
    full = exact(tall, spread, (((1,), (1,)), ((), ())))
    a = lax.broadcasted_iota(jnp.int32, (n, n), 0)
    b = lax.broadcasted_iota(jnp.int32, (n, n), 1)
    full = jnp.where(a % SUB == b % SUB, full, 0.0)
    high = full.astype(BF16)
    out_ref[0:n, :] = high
    out_ref[n:rows, :] = (full - high.astype(F32)).astype(BF16)
    ones = jnp.ones((1, first_ref.shape[1]), F32)
    first_ref[...] = exact(r_ref[0:1, :], ones, (((0,), (0,)), ((), ())))


def near_kernel(plan, second, nb_ref, f_ref, ga_ref, gb_ref, pq_ref, core_ref, chl_ref, *refs):
    if second:
        chl_low_ref, *refs = refs
    part_ref, far_ref, aux_ref, opart_ref, ofar_ref, oaux_ref = refs[:6]
    chl_out_ref = refs[6] if second else None
    odd = lax.axis_index("tile") % 2
    cols = nb_ref.shape[-1]
    nt, p_rows = plan.nt, plan.p_rows
    index, in_core, in_cross = neighbours_of(nb_ref, odd)
    wet, wet_core = wet_of(plan, pq_ref), wet_of(plan, core_ref)
    near_wet = []
    for k in range(3):
        found = jnp.where(in_core[k], take_lanes(wet_core, index[k]), take_lanes(wet, index[k]))
        near_wet.append(jnp.where(in_cross[k], 0.0, found))
    last = float(plan.lev - 1)

    def split(level, ws):
        active = level < wet
        near = [jnp.where(active & (level < near_wet[k]), ws[k], 0.0) for k in range(3)]
        far = [jnp.where(active & in_cross[k], ws[k], 0.0) for k in range(3)]
        return near, far

    def moves(own, core, near, rest):
        totals = [o * r for o, r in zip(own, rest)]
        for k in range(3):
            for j in range(len(own)):
                v = jnp.where(in_core[k], take_lanes(core[j], index[k]), take_lanes(own[j], index[k]))
                totals[j] = totals[j] + near[j][k] * v
        return totals

    def tracers(comp):
        for r in plan.rs(comp):
            first = plan.level(comp, r)
            level = level_block(first, cols)
            passed = comp == int(second)
            ref, at = (gb_ref if comp else ga_ref), first - SUB * plan.full * int(passed and comp)
            g = [ref[i, at : at + SUB, :] for i in range(4 if passed else 6)]
            if not passed:
                g = [growth_rate(g[0], g[1], g[5])] + g[2:5]
            near, far = split(level, edge_weights(g[1], g[2]))
            rest = 1.0 - (near[0] + near[1] + near[2])
            for k in range(3):
                far_ref[k, r] = far[k]
            aux_ref[0, r] = link_weight(level, wet, g[3], last)
            aux_ref[1, r] = g[0]
            own = [plan.block(comp, second, rows_at(pq_ref), rows_at(pq_ref, p_rows), j, r) for j in range(nt)]
            core = [plan.block(comp, second, rows_at(core_ref), rows_at(core_ref, p_rows), j, r) for j in range(nt)]
            for j, v in enumerate(moves(own, core, [near] * nt, [rest] * nt)):
                part_ref[j, r] = v

    @on_side(1)
    def _():
        tracers(1)

    @on_side(0)
    def _():
        tracers(0)
        top = f_ref[5, 0:1, :]
        cut = SUB * (plan.full + 1) - SUB + 2

        def chl_block(b):
            at = SUB * b
            if not second:
                return chl_ref[at : at + SUB, :]
            if b < plan.full:
                return chl_ref[at : at + SUB, :]
            v = chl_low_ref[0, at - SUB * plan.full : at - SUB * plan.full + SUB, :]
            if b > plan.full:
                return v
            return jnp.where(level_block(at, cols) < float(cut), chl_ref[plan.halves : plan.halves + SUB, :], v)

        run = jnp.zeros((1, cols), F32)
        for b in range(plan.blocks):
            x = chl_block(b)
            if second:
                chl_out_ref[SUB * b : SUB * (b + 1), :] = x
            absorbed = 0.01 + 0.3 * (jnp.maximum(x, 0.0) + jnp.log1p(jnp.exp(-jnp.abs(x))))
            level = level_block(SUB * b, cols)
            sub = lax.broadcasted_iota(jnp.int32, (SUB, cols), 0)
            cum = absorbed
            for d in (1, 2, 4):
                cum = cum + jnp.where(sub >= d, pltpu.roll(cum, d, 0), 0.0)
            depth = cum + run
            ceiling = jnp.exp(-(depth - absorbed))
            oaux_ref[1, b] = 4.0 * top * (ceiling - jnp.exp(-depth))
            oaux_ref[2, b] = jnp.where(level < wet, top * ceiling, 0.0)
            run = depth[SUB - 1 : SUB, :]

        for b in range(plan.blocks):
            at = SUB * b
            level = level_block(at, cols)
            f = [f_ref[i, at : at + SUB, :] for i in range(5)]
            near, far = split(level, edge_weights(f[2], f[3]))
            rest = 1.0 - (near[0] + near[1] + near[2])
            flat = [jnp.where(v > 0.0, 0.15, 0.0) for v in near]
            rest_flat = 1.0 - (flat[0] + flat[1] + flat[2])
            for k in range(3):
                ofar_ref[k, b] = far[k]
            oaux_ref[0, b] = link_weight(level, wet, f[4], last)
            core = [rows_at(core_ref, p_rows)(plan.lev * i + at) for i in range(4)]
            out = moves(f[:4], core, [near, near, flat, flat], [rest, rest, rest_flat, rest_flat])
            for i in range(4):
                opart_ref[i, b] = out[i]


def far_wet(index, in_cross, wet_cross):
    return [jnp.where(in_cross[k], take_lanes(wet_cross, index[k]), 0.0) for k in range(3)]


def far_moves(parts, own, cross, far, index):
    totals = [p - o * (f[0] + f[1] + f[2]) for p, o, f in zip(parts, own, far)]
    for k in range(3):
        for j in range(len(own)):
            totals[j] = totals[j] + far[j][k] * take_lanes(cross[j], index[k])
    return totals


class Far:
    def __init__(self, plan, comp, second, nb_ref, pq_ref, cross_p_ref, part_ref, far_ref, aux_ref, h_ref, l_ref):
        self.plan, self.comp, self.second = plan, comp, second
        self.cols = nb_ref.shape[-1]
        self.own_p, self.own_q = rows_at(pq_ref), rows_at(pq_ref, plan.p_rows)
        self.part, self.far, self.aux, self.h, self.l = part_ref, far_ref, aux_ref, h_ref, l_ref
        self.index, _, in_cross = neighbours_of(nb_ref, lax.axis_index("tile") % 2)
        self.wet = wet_of(plan, pq_ref)
        self.wets = far_wet(self.index, in_cross, wet_of(plan, cross_p_ref))

    def at(self, r):
        return SUB * (r + 1)

    def clear(self, before, after):
        zero = jnp.zeros((SUB, self.cols), F32)
        if before is not None:
            self.l[self.at(before) : self.at(before) + SUB, :] = zero
        for j in range(self.plan.nt):
            for r in (before, after):
                if r is not None:
                    self.h[j, self.at(r) : self.at(r) + SUB, :] = zero

    def move(self, r, p, q):
        plan, at = self.plan, self.at(r)
        level = level_block(plan.level(self.comp, r), self.cols)
        far = [jnp.where(level < self.wets[k], self.far[k, r], 0.0) for k in range(3)]
        self.l[at : at + SUB, :] = self.aux[0, r]
        js = range(plan.nt)
        parts = [self.part[j, r] for j in js]
        own = [plan.block(self.comp, self.second, self.own_p, self.own_q, j, r) for j in js]
        cross = [plan.block(self.comp, self.second, p, q, j, r) for j in js]
        for j, v in enumerate(far_moves(parts, own, cross, [far] * plan.nt, self.index)):
            self.h[j, at : at + SUB, :] = v

    def react(self, r, react_ref, put):
        plan, at = self.plan, self.at(r)
        active = (level_block(plan.level(self.comp, r), self.cols) < self.wet).astype(F32)
        down, up = self.l[at : at + SUB, :], self.l[at - 1 : at - 1 + SUB, :]
        ys, ts = [], []
        for j in range(plan.nt):
            v = self.h[j, at : at + SUB, :]
            y = v + down * (self.h[j, at + 1 : at + 1 + SUB, :] - v) - up * (v - self.h[j, at - 1 : at - 1 + SUB, :])
            ys.append(y)
            ts.append(jnp.tanh(y))
        growth = self.aux[1, r]
        if self.second:
            total = react_ref[0:1, :] * ts[0]
            for j in range(1, plan.nt):
                total = total + react_ref[j : j + 1, :] * ts[j]
            put(0, r, (ys[0] + growth * total) * active)
            return
        n = react_ref.shape[1]
        ts += [jnp.zeros_like(ts[0])] * (n // SUB - plan.nt)
        stack = jnp.concatenate(ts, axis=0)
        high = stack.astype(BF16)
        rest = (stack - high.astype(F32)).astype(BF16)
        both = jnp.dot(react_ref[...], high, preferred_element_type=F32)
        total = both[:n] + both[n:] + jnp.dot(react_ref[0:n, :], rest, preferred_element_type=F32)
        for i in range(plan.nt):
            put(i, r, (ys[i] + growth * total[i * SUB : (i + 1) * SUB]) * active)


def nothing(offset):
    raise ValueError("not there")


def upper_kernel(plan, react_ref, nb_ref, pq_ref, p_ref, part_ref, far_ref, aux_ref, out_ref, edge_ref, h_ref, l_ref):
    out_ref[plan.wet : plan.wet + plan.half, :] = pq_ref[plan.wet : plan.wet + plan.half, :]
    refs = (nb_ref, pq_ref, p_ref, part_ref, far_ref, aux_ref, h_ref, l_ref)
    p = rows_at(p_ref)

    @on_side(0)
    def _():
        work = Far(plan, 0, False, *refs)
        work.clear(0, plan.window)
        for r in plan.rs(0):
            work.move(r, p, nothing)

        def put(i, r, value):
            if r <= plan.full:
                at = SUB * (plan.full * i + r - 1)
                out_ref[at : at + SUB, :] = value
            else:
                at = plan.halves + plan.half * i
                out_ref[at : at + plan.half, :] = value[0 : plan.half]

        for r in plan.rs(0):
            work.react(r, react_ref, put)

    @on_side(1)
    def _():
        work = Far(plan, 1, False, *refs)
        work.clear(-1, plan.full + 1)
        lower = lambda offset: jnp.zeros((SUB, work.cols), F32)
        for r in range(plan.full + 1):
            work.move(r, p, lower)
        at = work.at(plan.full - 1)
        for j in range(plan.nt):
            edge_ref[j] = h_ref[j, at : at + SUB, :]

        def put(i, r, value):
            if r < plan.full:
                at = SUB * (plan.full * i + r)
                out_ref[at : at + SUB, :] = value
            else:
                at = plan.halves + plan.half * i
                out_ref[at : at + plan.half, :] = value[0 : plan.half]

        for r in range(plan.full + 1):
            work.react(r, react_ref, put)


def ocean_far(plan, nb_ref, f_ref, pq_ref, p_ref, q_ref, opart_ref, ofar_ref, oaux_ref, w_ref, l_ref, put):
    cols = nb_ref.shape[-1]
    index, _, in_cross = neighbours_of(nb_ref, lax.axis_index("tile") % 2)
    wet = wet_of(plan, pq_ref)
    wets = far_wet(index, in_cross, wet_of(plan, p_ref))
    zero = jnp.zeros((SUB, cols), F32)
    end = SUB * (plan.blocks + 1)
    l_ref[0:SUB, :] = zero
    for i in range(4):
        w_ref[i, 0:SUB, :] = zero
        w_ref[i, end : end + SUB, :] = zero
    for b in range(plan.blocks):
        at = SUB * b
        level = level_block(at, cols)
        far = [jnp.where(level < wets[k], ofar_ref[k, b], 0.0) for k in range(3)]
        flat = [jnp.where(v > 0.0, 0.15, 0.0) for v in far]
        there = slice(at + SUB, at + 2 * SUB)
        l_ref[there, :] = oaux_ref[0, b]
        parts = [opart_ref[i, b] for i in range(4)]
        own = [f_ref[i, at : at + SUB, :] for i in range(4)]
        cross = [rows_at(q_ref)(plan.lev * i + at) for i in range(4)]
        q = far_moves(parts, own, cross, [far, far, flat, flat], index)
        w_ref[0, there, :] = q[0]
        w_ref[1, there, :] = q[1]
        w_ref[2, there, :] = ROTATE_COS * q[2] + ROTATE_SIN * q[3]
        w_ref[3, there, :] = -ROTATE_SIN * q[2] + ROTATE_COS * q[3]
    warm = [None] * plan.blocks
    for b in range(plan.blocks):
        at = SUB * (b + 1)
        active = (level_block(SUB * b, cols) < wet).astype(F32)
        down, up = l_ref[at : at + SUB, :], l_ref[at - 1 : at - 1 + SUB, :]
        for i in range(4):
            v = w_ref[i, at : at + SUB, :]
            y = v + down * (w_ref[i, at + 1 : at + 1 + SUB, :] - v) - up * (v - w_ref[i, at - 1 : at - 1 + SUB, :])
            if i == 0:
                warm[b] = y + oaux_ref[1, b]
                put(0, b, warm[b] * active)
            else:
                put(i, b, y * active)
        put(5, b, oaux_ref[2, b])
    sub = lax.broadcasted_iota(jnp.int32, (SUB, cols), 0)
    for b in range(plan.blocks):
        active = (level_block(SUB * b, cols) < wet).astype(F32)
        lower = pltpu.roll(warm[b], SUB - 1, 0)
        if b + 1 < plan.blocks:
            lower = jnp.where(sub == SUB - 1, pltpu.roll(warm[b + 1], SUB - 1, 0), lower)
        else:
            lower = jnp.where(sub == SUB - 1, warm[b], lower)
        put(4, b, (warm[b] - lower) * active)


def lower_kernel(
    plan, react_ref, nb_ref, f_ref, pq_ref, p_ref, q_ref, part_ref, far_ref, aux_ref, opart_ref, ofar_ref, oaux_ref,
    done_ref, edge_ref, out_ref, both_ref, ocean_ref, over_ref, rest_ref, h_ref, l_ref, w_ref, wl_ref,
):
    both_ref[0 : plan.p_rows, :] = done_ref[...]

    @on_side(0)
    def _():
        def put(i, b, value):
            at = SUB * b
            ocean_ref[i, at : at + SUB, :] = value
            if 2 <= i < 5 and b >= plan.full:
                over_ref[i - 1, at - SUB * plan.full : at - SUB * plan.full + SUB, :] = value
            else:
                rest_ref[plan.rest(i) + at : plan.rest(i) + at + SUB, :] = value
            if i < 4:
                for ref, base in ((out_ref, 0), (both_ref, plan.p_rows)):
                    ref[base + plan.lev * i + at : base + plan.lev * i + at + SUB, :] = value

        ocean_far(plan, nb_ref, f_ref, pq_ref, p_ref, q_ref, opart_ref, ofar_ref, oaux_ref, w_ref, wl_ref, put)
        tall = SUB * plan.full
        over_ref[0] = growth_rate(ocean_ref[0, tall:, :], ocean_ref[1, tall:, :], ocean_ref[5, tall:, :])

    @on_side(1)
    def _():
        work = Far(plan, 1, False, nb_ref, pq_ref, p_ref, part_ref, far_ref, aux_ref, h_ref, l_ref)
        work.clear(None, plan.window)
        before = work.at(plan.full - 1)
        l_ref[before : before + SUB, :] = aux_ref[0, plan.full - 1]
        for j in range(plan.nt):
            h_ref[j, before : before + SUB, :] = edge_ref[j]
        rs = (plan.full, plan.full + 1)
        for r in rs:
            work.move(r, rows_at(p_ref), rows_at(q_ref))

        def put(i, r, value):
            for ref, base in ((out_ref, 0), (both_ref, plan.p_rows)):
                if r > plan.full:
                    ref[base + SUB * i : base + SUB * (i + 1), :] = value
                else:
                    at = base + SUB * plan.nt + plan.half * i
                    ref[at : at + plan.half, :] = value[plan.half :]
                    at = base + plan.edges + i
                    ref[at : at + 1, :] = value[plan.half - 1 : plan.half]
            if i == 0:
                over_ref[0, SUB * r : SUB * (r + 1), :] = value

        for r in rs:
            work.react(r, react_ref, put)
        for r in range(plan.full):
            over_ref[0, SUB * r : SUB * (r + 1), :] = done_ref[SUB * r : SUB * (r + 1), :]


def chl_kernel(plan, react_ref, nb_ref, pq_ref, p_ref, part_ref, far_ref, aux_ref, out_ref, h_ref, l_ref):
    @on_side(0)
    def _():
        work = Far(plan, 0, True, nb_ref, pq_ref, p_ref, part_ref, far_ref, aux_ref, h_ref, l_ref)
        work.clear(0, plan.window)
        for r in plan.rs(0):
            work.move(r, rows_at(p_ref), nothing)

        def put(i, r, value):
            out_ref[SUB * (r - 1) : SUB * r, :] = value

        for r in plan.rs(0):
            work.react(r, react_ref, put)


def second_kernel(
    plan, react_ref, nb_ref, f_ref, pq_ref, p_ref, q_ref, part_ref, far_ref, aux_ref, opart_ref,
    ofar_ref, oaux_ref, out_ref, mine_ref, h_ref, l_ref, w_ref, wl_ref,
):
    @on_side(0)
    def _():
        def put(i, b, value):
            out_ref[i, SUB * b : SUB * (b + 1), :] = value

        ocean_far(plan, nb_ref, f_ref, pq_ref, p_ref, q_ref, opart_ref, ofar_ref, oaux_ref, w_ref, wl_ref, put)

    @on_side(1)
    def _():
        work = Far(plan, 1, True, nb_ref, pq_ref, p_ref, part_ref, far_ref, aux_ref, h_ref, l_ref)
        work.clear(-1, plan.window)
        for r in plan.rs(1):
            work.move(r, rows_at(p_ref), rows_at(q_ref))

        def put(i, r, value):
            mine_ref[SUB * r : SUB * (r + 1), :] = value

        for r in plan.rs(1):
            work.react(r, react_ref, put)


def merge_kernel(plan, ocean_ref, over_ref, rest_ref, chl_ref, mine_ref, upper_ref, out_ref, chl_out_ref):
    tall = SUB * plan.full

    @on_side(0)
    def _():
        out_ref[...] = ocean_ref[...]
        chl_out_ref[...] = chl_ref[...]

    @on_side(1)
    def _():
        for i in range(6):
            at = plan.rest(i)
            if 2 <= i < 5:
                out_ref[i, 0:tall, :] = rest_ref[at : at + tall, :]
                out_ref[i, tall:, :] = over_ref[i - 1]
            else:
                out_ref[i] = rest_ref[at : at + plan.lev, :]
        sub = lax.broadcasted_iota(jnp.int32, (SUB, chl_out_ref.shape[1]), 0)
        chl_out_ref[0:tall, :] = upper_ref[0:tall, :]
        chl_out_ref[tall : tall + SUB, :] = jnp.where(sub < 2, upper_ref[tall : tall + SUB, :], mine_ref[0:SUB, :])
        chl_out_ref[tall + SUB :, :] = mine_ref[SUB:, :]


def call(kernel, outs, ins, specs=None, scratch=(), cost=1_000_000):
    return pl.pallas_call(
        kernel,
        out_shape=outs,
        in_specs=specs or [VMEM] * len(ins),
        out_specs=jax.tree.map(lambda _: VMEM, outs),
        scratch_shapes=list(scratch),
        compiler_params=pltpu.CompilerParams(vmem_limit_bytes=GRANT),
        cost_estimate=pl.CostEstimate(flops=cost, bytes_accessed=1_000_000, transcendentals=0),
    )(*ins)


def swaps(tiles, across):
    pairs = []
    for c in (0, 1):
        for t in range(tiles):
            other = (t + 1) % tiles if (t % 2 == 0) != across else (t - 1) % tiles
            pairs.append((c * tiles + t, c * tiles + other))
    return pairs


def over_comp(tiles):
    return [(c * tiles + t, (1 - c) * tiles + t) for c in (0, 1) for t in range(tiles)]


def sent(v, pairs):
    return lax.ppermute(v, AXES, pairs)


def per_device(ocean_fields, tracers, reaction, wet_levels, neighbours):
    tiles = lax.axis_size("tile")
    nt, lev, cols = tracers.shape
    plan = Plan(nt, lev)
    blocks, window, p_rows = plan.blocks, plan.window, plan.p_rows
    fields = ocean_fields.reshape(-1, lev, cols)
    nf = fields.shape[0]
    top, tall = SUB * (plan.full + 1), SUB * plan.full
    across, within = swaps(tiles, True), swaps(tiles, False)

    near_shapes = (
        shape_of(nt, window, SUB, cols),
        shape_of(3, window, SUB, cols),
        shape_of(2, window, SUB, cols),
        shape_of(4, blocks, SUB, cols),
        shape_of(3, blocks, SUB, cols),
        shape_of(3, blocks, SUB, cols),
    )
    h_scratch = (pltpu.VMEM((nt, (window + 2) * SUB, cols), F32), pltpu.VMEM(((window + 2) * SUB, cols), F32))
    w_scratch = (pltpu.VMEM((4, (blocks + 2) * SUB, cols), F32), pltpu.VMEM(((blocks + 2) * SUB, cols), F32))
    kernel = lambda f, *more: functools.partial(f, plan, *more)

    p, q, pq, top_fields, chl = call(
        kernel(pack_kernel),
        (
            shape_of(p_rows, cols),
            shape_of(plan.q_rows, cols),
            shape_of(p_rows + plan.q_rows, cols),
            shape_of(4, top, cols),
            shape_of(lev, cols),
        ),
        tuple(
            pltpu.with_memory_space_constraint(v, pltpu.HBM) for v in (wet_levels.reshape(1, cols), fields, tracers)
        ),
        specs=[HBM] * 3,
        scratch=[
            pltpu.VMEM((1, cols), jnp.int32),
            pltpu.VMEM((nt, SUB, cols), F32),
            pltpu.VMEM((nf, top, cols), F32),
            pltpu.SemaphoreType.DMA((6,)),
        ],
    )
    cross_p = sent(p, across)
    lagged = sent(top_fields, over_comp(tiles))
    core = sent(pq, within)
    cross_q = sent(q, across)
    n = -(-nt // 2) * 2 * SUB
    matrix, rates = call(
        matrix_kernel, (jax.ShapeDtypeStruct((2 * n, n), BF16), shape_of(nt, cols)), (reaction,)
    )

    near = call(
        kernel(near_kernel, False),
        near_shapes,
        (neighbours, fields, lagged, fields, pq, core, chl),
        cost=8_000_000,
    )
    p_one, edge = call(
        kernel(upper_kernel),
        (shape_of(p_rows, cols), shape_of(nt, SUB, cols)),
        (matrix, neighbours, pq, cross_p, *near[:3]),
        scratch=h_scratch,
        cost=8_000_000,
    )
    cross_p_one = sent(p_one, across)
    q_one, pq_one, ocean_one, over_one, rest_one = call(
        kernel(lower_kernel),
        (
            shape_of(plan.q_rows, cols),
            shape_of(p_rows + plan.q_rows, cols),
            shape_of(nf, lev, cols),
            shape_of(4, lev - tall, cols),
            shape_of(3 * (lev + tall), cols),
        ),
        (matrix, neighbours, fields, pq, cross_p, cross_q, *near, p_one, edge),
        scratch=h_scratch + w_scratch,
        cost=8_000_000,
    )
    over = sent(over_one, over_comp(tiles))
    core_one = sent(pq_one, within)
    cross_q_one = sent(q_one, across)
    rest = sent(rest_one, over_comp(tiles))

    *near, chl_one = call(
        kernel(near_kernel, True),
        near_shapes + (shape_of(lev, cols),),
        (neighbours, ocean_one, ocean_one, over, pq_one, core_one, p_one, over),
        cost=8_000_000,
    )
    upper = call(
        kernel(chl_kernel),
        shape_of(top, cols),
        (rates, neighbours, pq_one, cross_p_one, *near[:3]),
        scratch=h_scratch,
        cost=8_000_000,
    )
    upper = sent(upper, over_comp(tiles))
    ocean_two, mine = call(
        kernel(second_kernel),
        (shape_of(nf, lev, cols), shape_of(lev - tall, cols)),
        (rates, neighbours, ocean_one, pq_one, cross_p_one, cross_q_one, *near),
        scratch=h_scratch + w_scratch,
        cost=8_000_000,
    )
    ocean_out, chl_out = call(
        kernel(merge_kernel),
        (shape_of(nf, lev, cols), shape_of(lev, cols)),
        (ocean_two, over, rest, chl_one, mine, upper),
    )
    return (ocean_out[None], chl_out[None])


def solution(mesh):
    return jax.shard_map(
        per_device,
        mesh=mesh,
        in_specs=(
            P("comp", None, None, "tile"),
            P(None, None, "tile"),
            P(),
            P("tile"),
            P(None, "tile"),
        ),
        out_specs=(P("comp", None, None, "tile"), P("comp", None, "tile")),
        check_vma=False,
    )
```

```python
import functools
import math

import jax
import jax.numpy as jnp
from jax import lax
from jax.experimental import pallas as pl
from jax.experimental.pallas import tpu as pltpu
from jax.sharding import PartitionSpec as P


ROTATE_COS = math.cos(0.3)
ROTATE_SIN = math.sin(0.3)
SUB = 8
AXES = ("comp", "tile")
ANGLES = [2.0 * math.pi * k / 3.0 for k in range(3)]
F32 = jnp.float32
BF16 = jnp.bfloat16
GRANT = 8 << 20
WIDTH = 2


VMEM = pl.BlockSpec(memory_space=pltpu.VMEM)
SMEM = pl.BlockSpec(memory_space=pltpu.SMEM)
HBM = pl.BlockSpec(memory_space=pltpu.HBM)


class Plan:
    def __init__(self, nt, lev):
        self.nt, self.lev = nt, lev
        self.blocks = lev // SUB
        self.full = self.blocks // 2 - 1
        self.window = self.full + 2
        self.half = SUB // 2
        self.halves = SUB * nt * self.full
        self.wet = self.halves + self.half * nt
        self.p_rows = -(-(self.wet + self.half) // SUB) * SUB
        self.edges = (SUB + self.half) * nt
        self.q_rows = max(4 * lev, -(-(self.edges + nt + SUB) // SUB) * SUB)

    def rs(self, comp):
        return list(range(1 - comp, self.window))

    def level(self, comp, r):
        return SUB * (r - 1) if comp == 0 else SUB * (self.full + r)

    def rest(self, i):
        tall = SUB * self.full
        return (0, self.lev, 2 * self.lev, 2 * self.lev + tall, 2 * self.lev + 2 * tall, 2 * self.lev + 3 * tall)[i]

    def block(self, comp, second, p, q, j, r):
        if comp == 0:
            return p(SUB * (self.full * j + r - 1)) if r <= self.full else p(self.halves + self.half * j)
        if r < self.full:
            return p(SUB * (self.full * j + r))
        if r > self.full:
            return q(SUB * j)
        upper = p(self.halves + self.half * j)
        lower = q(SUB * self.nt + self.half * (j - 1))
        sub = lax.broadcasted_iota(jnp.int32, upper.shape, 0)
        if second:
            edge = self.half - 1
            lower = jnp.where(sub == edge, q(self.edges + j - edge), lower)
            return jnp.where(sub < edge, upper, lower)
        return jnp.where(sub < self.half, upper, lower)


def rows_at(ref, base=0):
    return lambda offset: ref[base + offset : base + offset + SUB, :]


def edge_weights(eastward, northward):
    return [
        0.05 + 0.25 * jax.nn.sigmoid(eastward * math.cos(a) + northward * math.sin(a)) for a in ANGLES
    ]


def take_lanes(block, index):
    return jnp.take_along_axis(block, index, axis=1, mode="promise_in_bounds")


def shape_of(*dims):
    return jax.ShapeDtypeStruct(dims, F32)


def neighbours_of(nb_ref, odd):
    cols = nb_ref.shape[-1]
    core_side = jnp.where(odd == 1, 0, 2)
    index, in_core, in_cross = [], [], []
    for k in range(3):
        nb = jnp.broadcast_to(nb_ref[k : k + 1, :], (SUB, cols))
        side = nb // cols
        index.append(nb - side * cols)
        in_core.append(side == core_side)
        in_cross.append(side == 2 - core_side)
    return index, in_core, in_cross


def level_block(first, cols):
    return lax.broadcasted_iota(jnp.int32, (SUB, cols), 0).astype(F32) + float(first)


def link_weight(level, wet, mixing, last):
    nxt = level + 1.0
    return jnp.where((nxt < wet) & (nxt <= last), 0.02 + 0.13 * jax.nn.sigmoid(mixing), 0.0)


def growth_rate(temperature, salinity, light):
    return 0.5 * light * jax.nn.sigmoid(temperature + 0.5 * salinity)


def wet_of(plan, ref):
    return jnp.broadcast_to(ref[plan.wet : plan.wet + 1, :], (SUB, ref.shape[1]))


def on_side(comp):
    return pl.when(lax.axis_index("comp") == comp)


def pack_kernel(plan, wet_ref, f_ref, t_ref, p_ref, q_ref, pq_ref, top_ref, chl_ref, wet_buf, half_buf, top_buf, sems):
    nt, full, half, lev = plan.nt, plan.full, plan.half, plan.lev
    tall = SUB * full
    first = pl.multiple_of(lax.axis_index("comp") * tall, SUB)
    copies = [
        (t_ref.at[:, pl.ds(first, tall)], p_ref.at[pl.ds(0, plan.halves)].reshape(nt, tall, p_ref.shape[1])),
        (t_ref.at[:, pl.ds(pl.multiple_of(first + tall, SUB), SUB)], half_buf),
        (wet_ref, wet_buf),
        (f_ref.at[:, pl.ds(0, top_ref.shape[1])], top_buf),
        (t_ref.at[0], chl_ref),
    ]
    copies = [pltpu.make_async_copy(s, d, sems.at[i]) for i, (s, d) in enumerate(copies)]
    for c in copies:
        c.start()
    base = len(copies)
    slab = lambda n, rows: q_ref.at[pl.ds(0, n * rows)].reshape(n, rows, q_ref.shape[1])
    ocean = [pltpu.make_async_copy(f_ref.at[pl.ds(0, 4)], slab(4, lev), sems.at[base])]
    deep = [pltpu.make_async_copy(t_ref.at[:, pl.ds(lev - SUB, SUB)], slab(nt, SUB), sems.at[base])]

    @on_side(0)
    def _():
        for c in ocean:
            c.start()

    @on_side(1)
    def _():
        for c in deep:
            c.start()

    for c in copies:
        c.wait()
    p_ref[plan.wet : plan.wet + half, :] = jnp.broadcast_to(wet_buf[...].astype(F32), (half, wet_buf.shape[1]))
    for j in range(nt):
        p_ref[plan.halves + half * j : plan.halves + half * (j + 1), :] = half_buf[j, 0:half, :]

    @on_side(0)
    def _():
        for c in ocean:
            c.wait()

    @on_side(1)
    def _():
        for c in deep:
            c.wait()
        top_ref[0] = growth_rate(top_buf[0], top_buf[1], top_buf[5])
        top_ref[1:4] = top_buf[2:5]
        for j in range(nt):
            at = SUB * nt + half * j
            q_ref[at : at + half, :] = half_buf[j, half:SUB, :]

    pq_ref[0 : plan.p_rows, :] = p_ref[...]
    pq_ref[plan.p_rows :, :] = q_ref[...]


def matrix_kernel(r_ref, out_ref, first_ref):
    nt = r_ref.shape[0]
    rows, n = out_ref.shape
    p = lax.broadcasted_iota(jnp.int32, (n, nt), 0)
    spread = (p // SUB == lax.broadcasted_iota(jnp.int32, (n, nt), 1)).astype(F32)
    exact = functools.partial(
        lax.dot_general, precision=lax.Precision.HIGHEST, preferred_element_type=F32
    )
    tall = exact(spread, r_ref[...], (((1,), (0,)), ((), ())))
    full = exact(tall, spread, (((1,), (1,)), ((), ())))
    a = lax.broadcasted_iota(jnp.int32, (n, n), 0)
    b = lax.broadcasted_iota(jnp.int32, (n, n), 1)
    full = jnp.where(a % SUB == b % SUB, full, 0.0)
    high = full.astype(BF16)
    out_ref[0:n, :] = high
    out_ref[n:rows, :] = (full - high.astype(F32)).astype(BF16)
    ones = jnp.ones((1, first_ref.shape[1]), F32)
    first_ref[...] = exact(r_ref[0:1, :], ones, (((0,), (0,)), ((), ())))


def near_kernel(plan, second, nb_ref, f_ref, ga_ref, gb_ref, pq_ref, core_ref, chl_ref, *refs):
    if second:
        chl_low_ref, *refs = refs
    part_ref, far_ref, aux_ref, opart_ref, ofar_ref, oaux_ref = refs[:6]
    chl_out_ref = refs[6] if second else None
    odd = lax.axis_index("tile") % 2
    cols = nb_ref.shape[-1]
    nt, p_rows = plan.nt, plan.p_rows
    index, in_core, in_cross = neighbours_of(nb_ref, odd)
    wet, wet_core = wet_of(plan, pq_ref), wet_of(plan, core_ref)
    near_wet = []
    for k in range(3):
        found = jnp.where(in_core[k], take_lanes(wet_core, index[k]), take_lanes(wet, index[k]))
        near_wet.append(jnp.where(in_cross[k], 0.0, found))
    last = float(plan.lev - 1)

    def split(level, ws):
        active = level < wet
        near = [jnp.where(active & (level < near_wet[k]), ws[k], 0.0) for k in range(3)]
        far = [jnp.where(active & in_cross[k], ws[k], 0.0) for k in range(3)]
        return near, far

    def moves(own, core, near, rest):
        totals = [o * r for o, r in zip(own, rest)]
        for k in range(3):
            for j in range(len(own)):
                v = jnp.where(in_core[k], take_lanes(core[j], index[k]), take_lanes(own[j], index[k]))
                totals[j] = totals[j] + near[j][k] * v
        return totals

    def tracers(comp):
        for r in plan.rs(comp):
            first = plan.level(comp, r)
            level = level_block(first, cols)
            passed = comp == int(second)
            ref, at = (gb_ref if comp else ga_ref), first - SUB * plan.full * int(passed and comp)
            g = [ref[i, at : at + SUB, :] for i in range(4 if passed else 6)]
            if not passed:
                g = [growth_rate(g[0], g[1], g[5])] + g[2:5]
            near, far = split(level, edge_weights(g[1], g[2]))
            rest = 1.0 - (near[0] + near[1] + near[2])
            for k in range(3):
                far_ref[k, r] = far[k]
            aux_ref[0, r] = link_weight(level, wet, g[3], last)
            aux_ref[1, r] = g[0]
            own = [plan.block(comp, second, rows_at(pq_ref), rows_at(pq_ref, p_rows), j, r) for j in range(nt)]
            core = [plan.block(comp, second, rows_at(core_ref), rows_at(core_ref, p_rows), j, r) for j in range(nt)]
            for j, v in enumerate(moves(own, core, [near] * nt, [rest] * nt)):
                part_ref[j, r] = v

    @on_side(1)
    def _():
        tracers(1)

    @on_side(0)
    def _():
        tracers(0)
        top = f_ref[5, 0:1, :]
        cut = SUB * (plan.full + 1) - SUB + 2

        def chl_block(b):
            at = SUB * b
            if not second:
                return chl_ref[at : at + SUB, :]
            if b < plan.full:
                return chl_ref[at : at + SUB, :]
            v = chl_low_ref[0, at - SUB * plan.full : at - SUB * plan.full + SUB, :]
            if b > plan.full:
                return v
            return jnp.where(level_block(at, cols) < float(cut), chl_ref[plan.halves : plan.halves + SUB, :], v)

        run = jnp.zeros((1, cols), F32)
        for b in range(plan.blocks):
            x = chl_block(b)
            if second:
                chl_out_ref[SUB * b : SUB * (b + 1), :] = x
            absorbed = 0.01 + 0.3 * (jnp.maximum(x, 0.0) + jnp.log1p(jnp.exp(-jnp.abs(x))))
            level = level_block(SUB * b, cols)
            sub = lax.broadcasted_iota(jnp.int32, (SUB, cols), 0)
            cum = absorbed
            for d in (1, 2, 4):
                cum = cum + jnp.where(sub >= d, pltpu.roll(cum, d, 0), 0.0)
            depth = cum + run
            ceiling = jnp.exp(-(depth - absorbed))
            oaux_ref[1, b] = 4.0 * top * (ceiling - jnp.exp(-depth))
            oaux_ref[2, b] = jnp.where(level < wet, top * ceiling, 0.0)
            run = depth[SUB - 1 : SUB, :]

        for b in range(plan.blocks):
            at = SUB * b
            level = level_block(at, cols)
            f = [f_ref[i, at : at + SUB, :] for i in range(5)]
            near, far = split(level, edge_weights(f[2], f[3]))
            rest = 1.0 - (near[0] + near[1] + near[2])
            flat = [jnp.where(v > 0.0, 0.15, 0.0) for v in near]
            rest_flat = 1.0 - (flat[0] + flat[1] + flat[2])
            for k in range(3):
                ofar_ref[k, b] = far[k]
            oaux_ref[0, b] = link_weight(level, wet, f[4], last)
            core = [rows_at(core_ref, p_rows)(plan.lev * i + at) for i in range(4)]
            out = moves(f[:4], core, [near, near, flat, flat], [rest, rest, rest_flat, rest_flat])
            for i in range(4):
                opart_ref[i, b] = out[i]


def far_wet(index, in_cross, wet_cross):
    return [jnp.where(in_cross[k], take_lanes(wet_cross, index[k]), 0.0) for k in range(3)]


def far_moves(parts, own, cross, far, index):
    totals = [p - o * (f[0] + f[1] + f[2]) for p, o, f in zip(parts, own, far)]
    for k in range(3):
        for j in range(len(own)):
            totals[j] = totals[j] + far[j][k] * take_lanes(cross[j], index[k])
    return totals


class Far:
    def __init__(self, plan, comp, second, nb_ref, pq_ref, cross_p_ref, part_ref, far_ref, aux_ref, h_ref, l_ref):
        self.plan, self.comp, self.second = plan, comp, second
        self.cols = nb_ref.shape[-1]
        self.own_p, self.own_q = rows_at(pq_ref), rows_at(pq_ref, plan.p_rows)
        self.part, self.far, self.aux, self.h, self.l = part_ref, far_ref, aux_ref, h_ref, l_ref
        self.index, _, in_cross = neighbours_of(nb_ref, lax.axis_index("tile") % 2)
        self.wet = wet_of(plan, pq_ref)
        self.wets = far_wet(self.index, in_cross, wet_of(plan, cross_p_ref))

    def at(self, r):
        return SUB * (r + 1)

    def clear(self, before, after):
        zero = jnp.zeros((SUB, self.cols), F32)
        if before is not None:
            self.l[self.at(before) : self.at(before) + SUB, :] = zero
        for j in range(self.plan.nt):
            for r in (before, after):
                if r is not None:
                    self.h[j, self.at(r) : self.at(r) + SUB, :] = zero

    def move(self, r, p, q):
        plan, at = self.plan, self.at(r)
        level = level_block(plan.level(self.comp, r), self.cols)
        far = [jnp.where(level < self.wets[k], self.far[k, r], 0.0) for k in range(3)]
        self.l[at : at + SUB, :] = self.aux[0, r]
        js = range(plan.nt)
        parts = [self.part[j, r] for j in js]
        own = [plan.block(self.comp, self.second, self.own_p, self.own_q, j, r) for j in js]
        cross = [plan.block(self.comp, self.second, p, q, j, r) for j in js]
        for j, v in enumerate(far_moves(parts, own, cross, [far] * plan.nt, self.index)):
            self.h[j, at : at + SUB, :] = v

    def mix(self, r):
        plan, at = self.plan, self.at(r)
        down, up = self.l[at : at + SUB, :], self.l[at - 1 : at - 1 + SUB, :]
        ys = []
        for j in range(plan.nt):
            v = self.h[j, at : at + SUB, :]
            ys.append(
                v + down * (self.h[j, at + 1 : at + 1 + SUB, :] - v) - up * (v - self.h[j, at - 1 : at - 1 + SUB, :])
            )
        return ys

    def react(self, rs, react_ref, put):
        plan = self.plan
        ys = [self.mix(r) for r in rs]
        ts = [[jnp.tanh(y) for y in block] for block in ys]
        if not self.second:
            n = react_ref.shape[1]
            pad = [jnp.zeros_like(ts[0][0])] * (n // SUB - plan.nt)
            stack = jnp.concatenate([jnp.concatenate(t + pad, axis=0) for t in ts], axis=1)
            high = stack.astype(BF16)
            rest = (stack - high.astype(F32)).astype(BF16)
            both = jnp.dot(react_ref[...], high, preferred_element_type=F32)
            total = both[:n] + both[n:] + jnp.dot(react_ref[0:n, :], rest, preferred_element_type=F32)
        for b, r in enumerate(rs):
            active = (level_block(plan.level(self.comp, r), self.cols) < self.wet).astype(F32)
            growth = self.aux[1, r]
            if self.second:
                sums = [react_ref[0:1, :] * ts[b][0]]
                for j in range(1, plan.nt):
                    sums[0] = sums[0] + react_ref[j : j + 1, :] * ts[b][j]
            else:
                sums = [total[i * SUB : (i + 1) * SUB, b * self.cols : (b + 1) * self.cols] for i in range(plan.nt)]
            for i, v in enumerate(sums):
                put(i, r, (ys[b][i] + growth * v) * active)

    def react_all(self, rs, react_ref, put, width=WIDTH):
        for i in range(0, len(rs), width):
            self.react(rs[i : i + width], react_ref, put)


def nothing(offset):
    raise ValueError("not there")


def upper_kernel(plan, react_ref, nb_ref, pq_ref, p_ref, part_ref, far_ref, aux_ref, out_ref, edge_ref, h_ref, l_ref):
    out_ref[plan.wet : plan.wet + plan.half, :] = pq_ref[plan.wet : plan.wet + plan.half, :]
    refs = (nb_ref, pq_ref, p_ref, part_ref, far_ref, aux_ref, h_ref, l_ref)
    p = rows_at(p_ref)

    @on_side(0)
    def _():
        work = Far(plan, 0, False, *refs)
        work.clear(0, plan.window)
        for r in plan.rs(0):
            work.move(r, p, nothing)

        def put(i, r, value):
            if r <= plan.full:
                at = SUB * (plan.full * i + r - 1)
                out_ref[at : at + SUB, :] = value
            else:
                at = plan.halves + plan.half * i
                out_ref[at : at + plan.half, :] = value[0 : plan.half]

        work.react_all(plan.rs(0), react_ref, put)

    @on_side(1)
    def _():
        work = Far(plan, 1, False, *refs)
        work.clear(-1, plan.full + 1)
        lower = lambda offset: jnp.zeros((SUB, work.cols), F32)
        for r in range(plan.full + 1):
            work.move(r, p, lower)
        at = work.at(plan.full - 1)
        for j in range(plan.nt):
            edge_ref[j] = h_ref[j, at : at + SUB, :]

        def put(i, r, value):
            if r < plan.full:
                at = SUB * (plan.full * i + r)
                out_ref[at : at + SUB, :] = value
            else:
                at = plan.halves + plan.half * i
                out_ref[at : at + plan.half, :] = value[0 : plan.half]

        work.react_all(list(range(plan.full + 1)), react_ref, put)


def ocean_far(plan, nb_ref, f_ref, pq_ref, p_ref, q_ref, opart_ref, ofar_ref, oaux_ref, w_ref, l_ref, put):
    cols = nb_ref.shape[-1]
    index, _, in_cross = neighbours_of(nb_ref, lax.axis_index("tile") % 2)
    wet = wet_of(plan, pq_ref)
    wets = far_wet(index, in_cross, wet_of(plan, p_ref))
    zero = jnp.zeros((SUB, cols), F32)
    end = SUB * (plan.blocks + 1)
    l_ref[0:SUB, :] = zero
    for i in range(4):
        w_ref[i, 0:SUB, :] = zero
        w_ref[i, end : end + SUB, :] = zero
    for b in range(plan.blocks):
        at = SUB * b
        level = level_block(at, cols)
        far = [jnp.where(level < wets[k], ofar_ref[k, b], 0.0) for k in range(3)]
        flat = [jnp.where(v > 0.0, 0.15, 0.0) for v in far]
        there = slice(at + SUB, at + 2 * SUB)
        l_ref[there, :] = oaux_ref[0, b]
        parts = [opart_ref[i, b] for i in range(4)]
        own = [f_ref[i, at : at + SUB, :] for i in range(4)]
        cross = [rows_at(q_ref)(plan.lev * i + at) for i in range(4)]
        q = far_moves(parts, own, cross, [far, far, flat, flat], index)
        w_ref[0, there, :] = q[0]
        w_ref[1, there, :] = q[1]
        w_ref[2, there, :] = ROTATE_COS * q[2] + ROTATE_SIN * q[3]
        w_ref[3, there, :] = -ROTATE_SIN * q[2] + ROTATE_COS * q[3]
    warm = [None] * plan.blocks
    for b in range(plan.blocks):
        at = SUB * (b + 1)
        active = (level_block(SUB * b, cols) < wet).astype(F32)
        down, up = l_ref[at : at + SUB, :], l_ref[at - 1 : at - 1 + SUB, :]
        for i in range(4):
            v = w_ref[i, at : at + SUB, :]
            y = v + down * (w_ref[i, at + 1 : at + 1 + SUB, :] - v) - up * (v - w_ref[i, at - 1 : at - 1 + SUB, :])
            if i == 0:
                warm[b] = y + oaux_ref[1, b]
                put(0, b, warm[b] * active)
            else:
                put(i, b, y * active)
        put(5, b, oaux_ref[2, b])
    sub = lax.broadcasted_iota(jnp.int32, (SUB, cols), 0)
    for b in range(plan.blocks):
        active = (level_block(SUB * b, cols) < wet).astype(F32)
        lower = pltpu.roll(warm[b], SUB - 1, 0)
        if b + 1 < plan.blocks:
            lower = jnp.where(sub == SUB - 1, pltpu.roll(warm[b + 1], SUB - 1, 0), lower)
        else:
            lower = jnp.where(sub == SUB - 1, warm[b], lower)
        put(4, b, (warm[b] - lower) * active)


def lower_kernel(
    plan, react_ref, nb_ref, f_ref, pq_ref, p_ref, q_ref, part_ref, far_ref, aux_ref, opart_ref, ofar_ref, oaux_ref,
    done_ref, edge_ref, out_ref, both_ref, ocean_ref, over_ref, rest_ref, h_ref, l_ref, w_ref, wl_ref,
):
    both_ref[0 : plan.p_rows, :] = done_ref[...]

    @on_side(0)
    def _():
        def put(i, b, value):
            at = SUB * b
            ocean_ref[i, at : at + SUB, :] = value
            if 2 <= i < 5 and b >= plan.full:
                over_ref[i - 1, at - SUB * plan.full : at - SUB * plan.full + SUB, :] = value
            else:
                rest_ref[plan.rest(i) + at : plan.rest(i) + at + SUB, :] = value
            if i < 4:
                for ref, base in ((out_ref, 0), (both_ref, plan.p_rows)):
                    ref[base + plan.lev * i + at : base + plan.lev * i + at + SUB, :] = value

        ocean_far(plan, nb_ref, f_ref, pq_ref, p_ref, q_ref, opart_ref, ofar_ref, oaux_ref, w_ref, wl_ref, put)
        tall = SUB * plan.full
        over_ref[0] = growth_rate(ocean_ref[0, tall:, :], ocean_ref[1, tall:, :], ocean_ref[5, tall:, :])

    @on_side(1)
    def _():
        work = Far(plan, 1, False, nb_ref, pq_ref, p_ref, part_ref, far_ref, aux_ref, h_ref, l_ref)
        work.clear(None, plan.window)
        before = work.at(plan.full - 1)
        l_ref[before : before + SUB, :] = aux_ref[0, plan.full - 1]
        for j in range(plan.nt):
            h_ref[j, before : before + SUB, :] = edge_ref[j]
        rs = (plan.full, plan.full + 1)
        for r in rs:
            work.move(r, rows_at(p_ref), rows_at(q_ref))

        def put(i, r, value):
            for ref, base in ((out_ref, 0), (both_ref, plan.p_rows)):
                if r > plan.full:
                    ref[base + SUB * i : base + SUB * (i + 1), :] = value
                else:
                    at = base + SUB * plan.nt + plan.half * i
                    ref[at : at + plan.half, :] = value[plan.half :]
                    at = base + plan.edges + i
                    ref[at : at + 1, :] = value[plan.half - 1 : plan.half]
            if i == 0:
                over_ref[0, SUB * r : SUB * (r + 1), :] = value

        work.react_all(rs, react_ref, put)
        for r in range(plan.full):
            over_ref[0, SUB * r : SUB * (r + 1), :] = done_ref[SUB * r : SUB * (r + 1), :]


def chl_kernel(plan, react_ref, nb_ref, pq_ref, p_ref, part_ref, far_ref, aux_ref, out_ref, h_ref, l_ref):
    @on_side(0)
    def _():
        work = Far(plan, 0, True, nb_ref, pq_ref, p_ref, part_ref, far_ref, aux_ref, h_ref, l_ref)
        work.clear(0, plan.window)
        for r in plan.rs(0):
            work.move(r, rows_at(p_ref), nothing)

        def put(i, r, value):
            out_ref[SUB * (r - 1) : SUB * r, :] = value

        work.react_all(plan.rs(0), react_ref, put, 1)


def second_kernel(
    plan, react_ref, nb_ref, f_ref, pq_ref, p_ref, q_ref, part_ref, far_ref, aux_ref, opart_ref,
    ofar_ref, oaux_ref, out_ref, mine_ref, h_ref, l_ref, w_ref, wl_ref,
):
    @on_side(0)
    def _():
        def put(i, b, value):
            out_ref[i, SUB * b : SUB * (b + 1), :] = value

        ocean_far(plan, nb_ref, f_ref, pq_ref, p_ref, q_ref, opart_ref, ofar_ref, oaux_ref, w_ref, wl_ref, put)

    @on_side(1)
    def _():
        work = Far(plan, 1, True, nb_ref, pq_ref, p_ref, part_ref, far_ref, aux_ref, h_ref, l_ref)
        work.clear(-1, plan.window)
        for r in plan.rs(1):
            work.move(r, rows_at(p_ref), rows_at(q_ref))

        def put(i, r, value):
            mine_ref[SUB * r : SUB * (r + 1), :] = value

        work.react_all(plan.rs(1), react_ref, put, 1)


def merge_kernel(plan, ocean_ref, over_ref, rest_ref, chl_ref, mine_ref, upper_ref, out_ref, chl_out_ref):
    tall = SUB * plan.full

    @on_side(0)
    def _():
        out_ref[...] = ocean_ref[...]
        chl_out_ref[...] = chl_ref[...]

    @on_side(1)
    def _():
        for i in range(6):
            at = plan.rest(i)
            if 2 <= i < 5:
                out_ref[i, 0:tall, :] = rest_ref[at : at + tall, :]
                out_ref[i, tall:, :] = over_ref[i - 1]
            else:
                out_ref[i] = rest_ref[at : at + plan.lev, :]
        sub = lax.broadcasted_iota(jnp.int32, (SUB, chl_out_ref.shape[1]), 0)
        chl_out_ref[0:tall, :] = upper_ref[0:tall, :]
        chl_out_ref[tall : tall + SUB, :] = jnp.where(sub < 2, upper_ref[tall : tall + SUB, :], mine_ref[0:SUB, :])
        chl_out_ref[tall + SUB :, :] = mine_ref[SUB:, :]


def call(kernel, outs, ins, specs=None, scratch=(), cost=1_000_000):
    return pl.pallas_call(
        kernel,
        out_shape=outs,
        in_specs=specs or [VMEM] * len(ins),
        out_specs=jax.tree.map(lambda _: VMEM, outs),
        scratch_shapes=list(scratch),
        compiler_params=pltpu.CompilerParams(vmem_limit_bytes=GRANT),
        cost_estimate=pl.CostEstimate(flops=cost, bytes_accessed=1_000_000, transcendentals=0),
    )(*ins)


def swaps(tiles, across):
    pairs = []
    for c in (0, 1):
        for t in range(tiles):
            other = (t + 1) % tiles if (t % 2 == 0) != across else (t - 1) % tiles
            pairs.append((c * tiles + t, c * tiles + other))
    return pairs


def over_comp(tiles):
    return [(c * tiles + t, (1 - c) * tiles + t) for c in (0, 1) for t in range(tiles)]


def sent(v, pairs):
    return lax.ppermute(v, AXES, pairs)


def per_device(ocean_fields, tracers, reaction, wet_levels, neighbours):
    tiles = lax.axis_size("tile")
    nt, lev, cols = tracers.shape
    plan = Plan(nt, lev)
    blocks, window, p_rows = plan.blocks, plan.window, plan.p_rows
    fields = ocean_fields.reshape(-1, lev, cols)
    nf = fields.shape[0]
    top, tall = SUB * (plan.full + 1), SUB * plan.full
    across, within = swaps(tiles, True), swaps(tiles, False)

    near_shapes = (
        shape_of(nt, window, SUB, cols),
        shape_of(3, window, SUB, cols),
        shape_of(2, window, SUB, cols),
        shape_of(4, blocks, SUB, cols),
        shape_of(3, blocks, SUB, cols),
        shape_of(3, blocks, SUB, cols),
    )
    h_scratch = (pltpu.VMEM((nt, (window + 2) * SUB, cols), F32), pltpu.VMEM(((window + 2) * SUB, cols), F32))
    w_scratch = (pltpu.VMEM((4, (blocks + 2) * SUB, cols), F32), pltpu.VMEM(((blocks + 2) * SUB, cols), F32))
    kernel = lambda f, *more: functools.partial(f, plan, *more)

    p, q, pq, top_fields, chl = call(
        kernel(pack_kernel),
        (
            shape_of(p_rows, cols),
            shape_of(plan.q_rows, cols),
            shape_of(p_rows + plan.q_rows, cols),
            shape_of(4, top, cols),
            shape_of(lev, cols),
        ),
        tuple(
            pltpu.with_memory_space_constraint(v, pltpu.HBM) for v in (wet_levels.reshape(1, cols), fields, tracers)
        ),
        specs=[HBM] * 3,
        scratch=[
            pltpu.VMEM((1, cols), jnp.int32),
            pltpu.VMEM((nt, SUB, cols), F32),
            pltpu.VMEM((nf, top, cols), F32),
            pltpu.SemaphoreType.DMA((6,)),
        ],
    )
    cross_p = sent(p, across)
    lagged = sent(top_fields, over_comp(tiles))
    core = sent(pq, within)
    cross_q = sent(q, across)
    n = -(-nt // 2) * 2 * SUB
    matrix, rates = call(
        matrix_kernel, (jax.ShapeDtypeStruct((2 * n, n), BF16), shape_of(nt, cols)), (reaction,)
    )

    near = call(
        kernel(near_kernel, False),
        near_shapes,
        (neighbours, fields, lagged, fields, pq, core, chl),
        cost=8_000_000,
    )
    p_one, edge = call(
        kernel(upper_kernel),
        (shape_of(p_rows, cols), shape_of(nt, SUB, cols)),
        (matrix, neighbours, pq, cross_p, *near[:3]),
        scratch=h_scratch,
        cost=8_000_000,
    )
    cross_p_one = sent(p_one, across)
    q_one, pq_one, ocean_one, over_one, rest_one = call(
        kernel(lower_kernel),
        (
            shape_of(plan.q_rows, cols),
            shape_of(p_rows + plan.q_rows, cols),
            shape_of(nf, lev, cols),
            shape_of(4, lev - tall, cols),
            shape_of(3 * (lev + tall), cols),
        ),
        (matrix, neighbours, fields, pq, cross_p, cross_q, *near, p_one, edge),
        scratch=h_scratch + w_scratch,
        cost=8_000_000,
    )
    over = sent(over_one, over_comp(tiles))
    core_one = sent(pq_one, within)
    cross_q_one = sent(q_one, across)
    rest = sent(rest_one, over_comp(tiles))

    *near, chl_one = call(
        kernel(near_kernel, True),
        near_shapes + (shape_of(lev, cols),),
        (neighbours, ocean_one, ocean_one, over, pq_one, core_one, p_one, over),
        cost=8_000_000,
    )
    upper = call(
        kernel(chl_kernel),
        shape_of(top, cols),
        (rates, neighbours, pq_one, cross_p_one, *near[:3]),
        scratch=h_scratch,
        cost=8_000_000,
    )
    upper = sent(upper, over_comp(tiles))
    ocean_two, mine = call(
        kernel(second_kernel),
        (shape_of(nf, lev, cols), shape_of(lev - tall, cols)),
        (rates, neighbours, ocean_one, pq_one, cross_p_one, cross_q_one, *near),
        scratch=h_scratch + w_scratch,
        cost=8_000_000,
    )
    ocean_out, chl_out = call(
        kernel(merge_kernel),
        (shape_of(nf, lev, cols), shape_of(lev, cols)),
        (ocean_two, over, rest, chl_one, mine, upper),
    )
    return (ocean_out[None], chl_out[None])


def solution(mesh):
    return jax.shard_map(
        per_device,
        mesh=mesh,
        in_specs=(
            P("comp", None, None, "tile"),
            P(None, None, "tile"),
            P(),
            P("tile"),
            P(None, "tile"),
        ),
        out_specs=(P("comp", None, None, "tile"), P("comp", None, "tile")),
        check_vma=False,
    )
```

```python
import functools
import math

import jax
import jax.numpy as jnp
from jax import lax
from jax.experimental import pallas as pl
from jax.experimental.pallas import tpu as pltpu
from jax.sharding import PartitionSpec as P


ROTATE_COS = math.cos(0.3)
ROTATE_SIN = math.sin(0.3)
SUB = 8
AXES = ("comp", "tile")
ANGLES = [2.0 * math.pi * k / 3.0 for k in range(3)]
F32 = jnp.float32
BF16 = jnp.bfloat16
GRANT = 8 << 20
WIDTH = 4


VMEM = pl.BlockSpec(memory_space=pltpu.VMEM)
SMEM = pl.BlockSpec(memory_space=pltpu.SMEM)
HBM = pl.BlockSpec(memory_space=pltpu.HBM)


class Plan:
    def __init__(self, nt, lev):
        self.nt, self.lev = nt, lev
        self.blocks = lev // SUB
        self.full = self.blocks // 2 - 1
        self.window = self.full + 2
        self.half = SUB // 2
        self.halves = SUB * nt * self.full
        self.wet = self.halves + self.half * nt
        self.p_rows = -(-(self.wet + self.half) // SUB) * SUB
        self.edges = (SUB + self.half) * nt
        self.q_rows = max(4 * lev, -(-(self.edges + nt + SUB) // SUB) * SUB)

    def rs(self, comp):
        return list(range(1 - comp, self.window))

    def level(self, comp, r):
        return SUB * (r - 1) if comp == 0 else SUB * (self.full + r)

    def rest(self, i):
        tall = SUB * self.full
        return (0, self.lev, 2 * self.lev, 2 * self.lev + tall, 2 * self.lev + 2 * tall, 2 * self.lev + 3 * tall)[i]

    def block(self, comp, second, p, q, j, r):
        if comp == 0:
            return p(SUB * (self.full * j + r - 1)) if r <= self.full else p(self.halves + self.half * j)
        if r < self.full:
            return p(SUB * (self.full * j + r))
        if r > self.full:
            return q(SUB * j)
        upper = p(self.halves + self.half * j)
        lower = q(SUB * self.nt + self.half * (j - 1))
        sub = lax.broadcasted_iota(jnp.int32, upper.shape, 0)
        if second:
            edge = self.half - 1
            lower = jnp.where(sub == edge, q(self.edges + j - edge), lower)
            return jnp.where(sub < edge, upper, lower)
        return jnp.where(sub < self.half, upper, lower)


def rows_at(ref, base=0):
    return lambda offset: ref[base + offset : base + offset + SUB, :]


def edge_weights(eastward, northward):
    return [
        0.05 + 0.25 * jax.nn.sigmoid(eastward * math.cos(a) + northward * math.sin(a)) for a in ANGLES
    ]


def take_lanes(block, index):
    return jnp.take_along_axis(block, index, axis=1, mode="promise_in_bounds")


def shape_of(*dims):
    return jax.ShapeDtypeStruct(dims, F32)


def neighbours_of(nb_ref, odd):
    cols = nb_ref.shape[-1]
    core_side = jnp.where(odd == 1, 0, 2)
    index, in_core, in_cross = [], [], []
    for k in range(3):
        nb = jnp.broadcast_to(nb_ref[k : k + 1, :], (SUB, cols))
        side = nb // cols
        index.append(nb - side * cols)
        in_core.append(side == core_side)
        in_cross.append(side == 2 - core_side)
    return index, in_core, in_cross


def level_block(first, cols):
    return lax.broadcasted_iota(jnp.int32, (SUB, cols), 0).astype(F32) + float(first)


def link_weight(level, wet, mixing, last):
    nxt = level + 1.0
    return jnp.where((nxt < wet) & (nxt <= last), 0.02 + 0.13 * jax.nn.sigmoid(mixing), 0.0)


def growth_rate(temperature, salinity, light):
    return 0.5 * light * jax.nn.sigmoid(temperature + 0.5 * salinity)


def wet_of(plan, ref):
    return jnp.broadcast_to(ref[plan.wet : plan.wet + 1, :], (SUB, ref.shape[1]))


def on_side(comp):
    return pl.when(lax.axis_index("comp") == comp)


def pack_kernel(plan, wet_ref, f_ref, t_ref, p_ref, q_ref, pq_ref, top_ref, chl_ref, wet_buf, half_buf, top_buf, sems):
    nt, full, half, lev = plan.nt, plan.full, plan.half, plan.lev
    tall = SUB * full
    first = pl.multiple_of(lax.axis_index("comp") * tall, SUB)
    copies = [
        (t_ref.at[:, pl.ds(first, tall)], p_ref.at[pl.ds(0, plan.halves)].reshape(nt, tall, p_ref.shape[1])),
        (t_ref.at[:, pl.ds(pl.multiple_of(first + tall, SUB), SUB)], half_buf),
        (wet_ref, wet_buf),
    ]
    copies = [pltpu.make_async_copy(s, d, sems.at[i]) for i, (s, d) in enumerate(copies)]
    for c in copies:
        c.start()
    base = len(copies)
    slab = lambda n, rows: q_ref.at[pl.ds(0, n * rows)].reshape(n, rows, q_ref.shape[1])
    ocean = [
        pltpu.make_async_copy(f_ref.at[pl.ds(0, 4)], slab(4, lev), sems.at[base]),
        pltpu.make_async_copy(t_ref.at[0], chl_ref, sems.at[base + 1]),
    ]
    deep = [
        pltpu.make_async_copy(t_ref.at[:, pl.ds(lev - SUB, SUB)], slab(nt, SUB), sems.at[base]),
        pltpu.make_async_copy(f_ref.at[:, pl.ds(0, top_ref.shape[1])], top_buf, sems.at[base + 1]),
    ]

    @on_side(0)
    def _():
        for c in ocean:
            c.start()

    @on_side(1)
    def _():
        for c in deep:
            c.start()

    for c in copies:
        c.wait()
    p_ref[plan.wet : plan.wet + half, :] = jnp.broadcast_to(wet_buf[...].astype(F32), (half, wet_buf.shape[1]))
    for j in range(nt):
        p_ref[plan.halves + half * j : plan.halves + half * (j + 1), :] = half_buf[j, 0:half, :]

    @on_side(0)
    def _():
        for c in ocean:
            c.wait()

    @on_side(1)
    def _():
        for c in deep:
            c.wait()
        top_ref[0] = growth_rate(top_buf[0], top_buf[1], top_buf[5])
        top_ref[1:4] = top_buf[2:5]
        for j in range(nt):
            at = SUB * nt + half * j
            q_ref[at : at + half, :] = half_buf[j, half:SUB, :]

    pq_ref[0 : plan.p_rows, :] = p_ref[...]
    pq_ref[plan.p_rows :, :] = q_ref[...]


def matrix_kernel(r_ref, out_ref, first_ref):
    nt = r_ref.shape[0]
    rows, n = out_ref.shape
    p = lax.broadcasted_iota(jnp.int32, (n, nt), 0)
    spread = (p // SUB == lax.broadcasted_iota(jnp.int32, (n, nt), 1)).astype(F32)
    exact = functools.partial(
        lax.dot_general, precision=lax.Precision.HIGHEST, preferred_element_type=F32
    )
    tall = exact(spread, r_ref[...], (((1,), (0,)), ((), ())))
    full = exact(tall, spread, (((1,), (1,)), ((), ())))
    a = lax.broadcasted_iota(jnp.int32, (n, n), 0)
    b = lax.broadcasted_iota(jnp.int32, (n, n), 1)
    full = jnp.where(a % SUB == b % SUB, full, 0.0)
    high = full.astype(BF16)
    out_ref[0:n, :] = high
    out_ref[n:rows, :] = (full - high.astype(F32)).astype(BF16)
    ones = jnp.ones((1, first_ref.shape[1]), F32)
    first_ref[...] = exact(r_ref[0:1, :], ones, (((0,), (0,)), ((), ())))


def near_kernel(plan, second, nb_ref, f_ref, ga_ref, gb_ref, pq_ref, core_ref, chl_ref, *refs):
    if second:
        chl_low_ref, *refs = refs
    part_ref, far_ref, aux_ref, opart_ref, ofar_ref, oaux_ref = refs[:6]
    chl_out_ref = refs[6] if second else None
    odd = lax.axis_index("tile") % 2
    cols = nb_ref.shape[-1]
    nt, p_rows = plan.nt, plan.p_rows
    index, in_core, in_cross = neighbours_of(nb_ref, odd)
    wet, wet_core = wet_of(plan, pq_ref), wet_of(plan, core_ref)
    near_wet = []
    for k in range(3):
        found = jnp.where(in_core[k], take_lanes(wet_core, index[k]), take_lanes(wet, index[k]))
        near_wet.append(jnp.where(in_cross[k], 0.0, found))
    last = float(plan.lev - 1)

    def split(level, ws):
        active = level < wet
        near = [jnp.where(active & (level < near_wet[k]), ws[k], 0.0) for k in range(3)]
        far = [jnp.where(active & in_cross[k], ws[k], 0.0) for k in range(3)]
        return near, far

    def moves(own, core, near, rest):
        totals = [o * r for o, r in zip(own, rest)]
        for k in range(3):
            for j in range(len(own)):
                v = jnp.where(in_core[k], take_lanes(core[j], index[k]), take_lanes(own[j], index[k]))
                totals[j] = totals[j] + near[j][k] * v
        return totals

    def tracers(comp):
        for r in plan.rs(comp):
            first = plan.level(comp, r)
            level = level_block(first, cols)
            passed = comp == int(second)
            ref, at = (gb_ref if comp else ga_ref), first - SUB * plan.full * int(passed and comp)
            g = [ref[i, at : at + SUB, :] for i in range(4 if passed else 6)]
            if not passed:
                g = [growth_rate(g[0], g[1], g[5])] + g[2:5]
            near, far = split(level, edge_weights(g[1], g[2]))
            rest = 1.0 - (near[0] + near[1] + near[2])
            for k in range(3):
                far_ref[k, r] = far[k]
            aux_ref[0, r] = link_weight(level, wet, g[3], last)
            aux_ref[1, r] = g[0]
            own = [plan.block(comp, second, rows_at(pq_ref), rows_at(pq_ref, p_rows), j, r) for j in range(nt)]
            core = [plan.block(comp, second, rows_at(core_ref), rows_at(core_ref, p_rows), j, r) for j in range(nt)]
            for j, v in enumerate(moves(own, core, [near] * nt, [rest] * nt)):
                part_ref[j, r] = v

    @on_side(1)
    def _():
        tracers(1)

    @on_side(0)
    def _():
        tracers(0)
        top = f_ref[5, 0:1, :]
        cut = SUB * (plan.full + 1) - SUB + 2

        def chl_block(b):
            at = SUB * b
            if not second:
                return chl_ref[at : at + SUB, :]
            if b < plan.full:
                return chl_ref[at : at + SUB, :]
            v = chl_low_ref[0, at - SUB * plan.full : at - SUB * plan.full + SUB, :]
            if b > plan.full:
                return v
            return jnp.where(level_block(at, cols) < float(cut), chl_ref[plan.halves : plan.halves + SUB, :], v)

        run = jnp.zeros((1, cols), F32)
        for b in range(plan.blocks):
            x = chl_block(b)
            if second:
                chl_out_ref[SUB * b : SUB * (b + 1), :] = x
            absorbed = 0.01 + 0.3 * (jnp.maximum(x, 0.0) + jnp.log1p(jnp.exp(-jnp.abs(x))))
            level = level_block(SUB * b, cols)
            sub = lax.broadcasted_iota(jnp.int32, (SUB, cols), 0)
            cum = absorbed
            for d in (1, 2, 4):
                cum = cum + jnp.where(sub >= d, pltpu.roll(cum, d, 0), 0.0)
            depth = cum + run
            ceiling = jnp.exp(-(depth - absorbed))
            oaux_ref[1, b] = 4.0 * top * (ceiling - jnp.exp(-depth))
            oaux_ref[2, b] = jnp.where(level < wet, top * ceiling, 0.0)
            run = depth[SUB - 1 : SUB, :]

        for b in range(plan.blocks):
            at = SUB * b
            level = level_block(at, cols)
            f = [f_ref[i, at : at + SUB, :] for i in range(5)]
            near, far = split(level, edge_weights(f[2], f[3]))
            rest = 1.0 - (near[0] + near[1] + near[2])
            flat = [jnp.where(v > 0.0, 0.15, 0.0) for v in near]
            rest_flat = 1.0 - (flat[0] + flat[1] + flat[2])
            for k in range(3):
                ofar_ref[k, b] = far[k]
            oaux_ref[0, b] = link_weight(level, wet, f[4], last)
            core = [rows_at(core_ref, p_rows)(plan.lev * i + at) for i in range(4)]
            out = moves(f[:4], core, [near, near, flat, flat], [rest, rest, rest_flat, rest_flat])
            for i in range(4):
                opart_ref[i, b] = out[i]


def far_wet(index, in_cross, wet_cross):
    return [jnp.where(in_cross[k], take_lanes(wet_cross, index[k]), 0.0) for k in range(3)]


def far_moves(parts, own, cross, far, index):
    totals = [p - o * (f[0] + f[1] + f[2]) for p, o, f in zip(parts, own, far)]
    for k in range(3):
        for j in range(len(own)):
            totals[j] = totals[j] + far[j][k] * take_lanes(cross[j], index[k])
    return totals


class Far:
    def __init__(self, plan, comp, second, nb_ref, pq_ref, cross_p_ref, part_ref, far_ref, aux_ref, h_ref, l_ref):
        self.plan, self.comp, self.second = plan, comp, second
        self.cols = nb_ref.shape[-1]
        self.own_p, self.own_q = rows_at(pq_ref), rows_at(pq_ref, plan.p_rows)
        self.part, self.far, self.aux, self.h, self.l = part_ref, far_ref, aux_ref, h_ref, l_ref
        self.index, _, in_cross = neighbours_of(nb_ref, lax.axis_index("tile") % 2)
        self.wet = wet_of(plan, pq_ref)
        self.wets = far_wet(self.index, in_cross, wet_of(plan, cross_p_ref))

    def at(self, r):
        return SUB * (r + 1)

    def clear(self, before, after):
        zero = jnp.zeros((SUB, self.cols), F32)
        if before is not None:
            self.l[self.at(before) : self.at(before) + SUB, :] = zero
        for j in range(self.plan.nt):
            for r in (before, after):
                if r is not None:
                    self.h[j, self.at(r) : self.at(r) + SUB, :] = zero

    def move(self, r, p, q):
        plan, at = self.plan, self.at(r)
        level = level_block(plan.level(self.comp, r), self.cols)
        far = [jnp.where(level < self.wets[k], self.far[k, r], 0.0) for k in range(3)]
        self.l[at : at + SUB, :] = self.aux[0, r]
        js = range(plan.nt)
        parts = [self.part[j, r] for j in js]
        own = [plan.block(self.comp, self.second, self.own_p, self.own_q, j, r) for j in js]
        cross = [plan.block(self.comp, self.second, p, q, j, r) for j in js]
        for j, v in enumerate(far_moves(parts, own, cross, [far] * plan.nt, self.index)):
            self.h[j, at : at + SUB, :] = v

    def mix(self, r):
        plan, at = self.plan, self.at(r)
        down, up = self.l[at : at + SUB, :], self.l[at - 1 : at - 1 + SUB, :]
        ys = []
        for j in range(plan.nt):
            v = self.h[j, at : at + SUB, :]
            ys.append(
                v + down * (self.h[j, at + 1 : at + 1 + SUB, :] - v) - up * (v - self.h[j, at - 1 : at - 1 + SUB, :])
            )
        return ys

    def react(self, rs, react_ref, put):
        plan = self.plan
        ys = [self.mix(r) for r in rs]
        ts = [[jnp.tanh(y) for y in block] for block in ys]
        if not self.second:
            n = react_ref.shape[1]
            pad = [jnp.zeros_like(ts[0][0])] * (n // SUB - plan.nt)
            stack = jnp.concatenate([jnp.concatenate(t + pad, axis=0) for t in ts], axis=1)
            high = stack.astype(BF16)
            rest = (stack - high.astype(F32)).astype(BF16)
            both = jnp.dot(react_ref[...], high, preferred_element_type=F32)
            total = both[:n] + both[n:] + jnp.dot(react_ref[0:n, :], rest, preferred_element_type=F32)
        for b, r in enumerate(rs):
            active = (level_block(plan.level(self.comp, r), self.cols) < self.wet).astype(F32)
            growth = self.aux[1, r]
            if self.second:
                sums = [react_ref[0:1, :] * ts[b][0]]
                for j in range(1, plan.nt):
                    sums[0] = sums[0] + react_ref[j : j + 1, :] * ts[b][j]
            else:
                sums = [total[i * SUB : (i + 1) * SUB, b * self.cols : (b + 1) * self.cols] for i in range(plan.nt)]
            for i, v in enumerate(sums):
                put(i, r, (ys[b][i] + growth * v) * active)

    def react_all(self, rs, react_ref, put, width=WIDTH):
        for i in range(0, len(rs), width):
            self.react(rs[i : i + width], react_ref, put)


def nothing(offset):
    raise ValueError("not there")


def upper_kernel(plan, react_ref, nb_ref, pq_ref, p_ref, part_ref, far_ref, aux_ref, out_ref, edge_ref, h_ref, l_ref):
    out_ref[plan.wet : plan.wet + plan.half, :] = pq_ref[plan.wet : plan.wet + plan.half, :]
    refs = (nb_ref, pq_ref, p_ref, part_ref, far_ref, aux_ref, h_ref, l_ref)
    p = rows_at(p_ref)

    @on_side(0)
    def _():
        work = Far(plan, 0, False, *refs)
        work.clear(0, plan.window)
        for r in plan.rs(0):
            work.move(r, p, nothing)

        def put(i, r, value):
            if r <= plan.full:
                at = SUB * (plan.full * i + r - 1)
                out_ref[at : at + SUB, :] = value
            else:
                at = plan.halves + plan.half * i
                out_ref[at : at + plan.half, :] = value[0 : plan.half]

        work.react_all(plan.rs(0), react_ref, put)

    @on_side(1)
    def _():
        work = Far(plan, 1, False, *refs)
        work.clear(-1, plan.full + 1)
        lower = lambda offset: jnp.zeros((SUB, work.cols), F32)
        for r in range(plan.full + 1):
            work.move(r, p, lower)
        at = work.at(plan.full - 1)
        for j in range(plan.nt):
            edge_ref[j] = h_ref[j, at : at + SUB, :]

        def put(i, r, value):
            if r < plan.full:
                at = SUB * (plan.full * i + r)
                out_ref[at : at + SUB, :] = value
            else:
                at = plan.halves + plan.half * i
                out_ref[at : at + plan.half, :] = value[0 : plan.half]

        work.react_all(list(range(plan.full + 1)), react_ref, put)


def ocean_far(plan, nb_ref, f_ref, pq_ref, p_ref, q_ref, opart_ref, ofar_ref, oaux_ref, w_ref, l_ref, put):
    cols = nb_ref.shape[-1]
    index, _, in_cross = neighbours_of(nb_ref, lax.axis_index("tile") % 2)
    wet = wet_of(plan, pq_ref)
    wets = far_wet(index, in_cross, wet_of(plan, p_ref))
    zero = jnp.zeros((SUB, cols), F32)
    end = SUB * (plan.blocks + 1)
    l_ref[0:SUB, :] = zero
    for i in range(4):
        w_ref[i, 0:SUB, :] = zero
        w_ref[i, end : end + SUB, :] = zero
    for b in range(plan.blocks):
        at = SUB * b
        level = level_block(at, cols)
        far = [jnp.where(level < wets[k], ofar_ref[k, b], 0.0) for k in range(3)]
        flat = [jnp.where(v > 0.0, 0.15, 0.0) for v in far]
        there = slice(at + SUB, at + 2 * SUB)
        l_ref[there, :] = oaux_ref[0, b]
        parts = [opart_ref[i, b] for i in range(4)]
        own = [f_ref[i, at : at + SUB, :] for i in range(4)]
        cross = [rows_at(q_ref)(plan.lev * i + at) for i in range(4)]
        q = far_moves(parts, own, cross, [far, far, flat, flat], index)
        w_ref[0, there, :] = q[0]
        w_ref[1, there, :] = q[1]
        w_ref[2, there, :] = ROTATE_COS * q[2] + ROTATE_SIN * q[3]
        w_ref[3, there, :] = -ROTATE_SIN * q[2] + ROTATE_COS * q[3]
    warm = [None] * plan.blocks
    for b in range(plan.blocks):
        at = SUB * (b + 1)
        active = (level_block(SUB * b, cols) < wet).astype(F32)
        down, up = l_ref[at : at + SUB, :], l_ref[at - 1 : at - 1 + SUB, :]
        for i in range(4):
            v = w_ref[i, at : at + SUB, :]
            y = v + down * (w_ref[i, at + 1 : at + 1 + SUB, :] - v) - up * (v - w_ref[i, at - 1 : at - 1 + SUB, :])
            if i == 0:
                warm[b] = y + oaux_ref[1, b]
                put(0, b, warm[b] * active)
            else:
                put(i, b, y * active)
        put(5, b, oaux_ref[2, b])
    sub = lax.broadcasted_iota(jnp.int32, (SUB, cols), 0)
    for b in range(plan.blocks):
        active = (level_block(SUB * b, cols) < wet).astype(F32)
        lower = pltpu.roll(warm[b], SUB - 1, 0)
        if b + 1 < plan.blocks:
            lower = jnp.where(sub == SUB - 1, pltpu.roll(warm[b + 1], SUB - 1, 0), lower)
        else:
            lower = jnp.where(sub == SUB - 1, warm[b], lower)
        put(4, b, (warm[b] - lower) * active)


def lower_kernel(
    plan, react_ref, nb_ref, f_ref, pq_ref, p_ref, q_ref, part_ref, far_ref, aux_ref, opart_ref, ofar_ref, oaux_ref,
    done_ref, edge_ref, out_ref, both_ref, ocean_ref, over_ref, rest_ref, h_ref, l_ref, w_ref, wl_ref,
):
    both_ref[0 : plan.p_rows, :] = done_ref[...]

    @on_side(0)
    def _():
        def put(i, b, value):
            at = SUB * b
            ocean_ref[i, at : at + SUB, :] = value
            if 2 <= i < 5 and b >= plan.full:
                over_ref[i - 1, at - SUB * plan.full : at - SUB * plan.full + SUB, :] = value
            else:
                rest_ref[plan.rest(i) + at : plan.rest(i) + at + SUB, :] = value
            if i < 4:
                for ref, base in ((out_ref, 0), (both_ref, plan.p_rows)):
                    ref[base + plan.lev * i + at : base + plan.lev * i + at + SUB, :] = value

        ocean_far(plan, nb_ref, f_ref, pq_ref, p_ref, q_ref, opart_ref, ofar_ref, oaux_ref, w_ref, wl_ref, put)
        tall = SUB * plan.full
        over_ref[0] = growth_rate(ocean_ref[0, tall:, :], ocean_ref[1, tall:, :], ocean_ref[5, tall:, :])

    @on_side(1)
    def _():
        work = Far(plan, 1, False, nb_ref, pq_ref, p_ref, part_ref, far_ref, aux_ref, h_ref, l_ref)
        work.clear(None, plan.window)
        before = work.at(plan.full - 1)
        l_ref[before : before + SUB, :] = aux_ref[0, plan.full - 1]
        for j in range(plan.nt):
            h_ref[j, before : before + SUB, :] = edge_ref[j]
        rs = (plan.full, plan.full + 1)
        for r in rs:
            work.move(r, rows_at(p_ref), rows_at(q_ref))

        def put(i, r, value):
            for ref, base in ((out_ref, 0), (both_ref, plan.p_rows)):
                if r > plan.full:
                    ref[base + SUB * i : base + SUB * (i + 1), :] = value
                else:
                    at = base + SUB * plan.nt + plan.half * i
                    ref[at : at + plan.half, :] = value[plan.half :]
                    at = base + plan.edges + i
                    ref[at : at + 1, :] = value[plan.half - 1 : plan.half]
            if i == 0:
                over_ref[0, SUB * r : SUB * (r + 1), :] = value

        work.react_all(rs, react_ref, put)
        for r in range(plan.full):
            over_ref[0, SUB * r : SUB * (r + 1), :] = done_ref[SUB * r : SUB * (r + 1), :]


def chl_kernel(plan, react_ref, nb_ref, pq_ref, p_ref, part_ref, far_ref, aux_ref, out_ref, h_ref, l_ref):
    @on_side(0)
    def _():
        work = Far(plan, 0, True, nb_ref, pq_ref, p_ref, part_ref, far_ref, aux_ref, h_ref, l_ref)
        work.clear(0, plan.window)
        for r in plan.rs(0):
            work.move(r, rows_at(p_ref), nothing)

        def put(i, r, value):
            out_ref[SUB * (r - 1) : SUB * r, :] = value

        work.react_all(plan.rs(0), react_ref, put, 1)


def second_kernel(
    plan, react_ref, nb_ref, f_ref, pq_ref, p_ref, q_ref, part_ref, far_ref, aux_ref, opart_ref,
    ofar_ref, oaux_ref, out_ref, mine_ref, h_ref, l_ref, w_ref, wl_ref,
):
    @on_side(0)
    def _():
        def put(i, b, value):
            out_ref[i, SUB * b : SUB * (b + 1), :] = value

        ocean_far(plan, nb_ref, f_ref, pq_ref, p_ref, q_ref, opart_ref, ofar_ref, oaux_ref, w_ref, wl_ref, put)

    @on_side(1)
    def _():
        work = Far(plan, 1, True, nb_ref, pq_ref, p_ref, part_ref, far_ref, aux_ref, h_ref, l_ref)
        work.clear(-1, plan.window)
        for r in plan.rs(1):
            work.move(r, rows_at(p_ref), rows_at(q_ref))

        def put(i, r, value):
            mine_ref[SUB * r : SUB * (r + 1), :] = value

        work.react_all(plan.rs(1), react_ref, put, 1)


def merge_kernel(plan, ocean_ref, over_ref, rest_ref, chl_ref, mine_ref, upper_ref, out_ref, chl_out_ref):
    tall = SUB * plan.full

    @on_side(0)
    def _():
        out_ref[...] = ocean_ref[...]
        chl_out_ref[...] = chl_ref[...]

    @on_side(1)
    def _():
        for i in range(6):
            at = plan.rest(i)
            if 2 <= i < 5:
                out_ref[i, 0:tall, :] = rest_ref[at : at + tall, :]
                out_ref[i, tall:, :] = over_ref[i - 1]
            else:
                out_ref[i] = rest_ref[at : at + plan.lev, :]
        sub = lax.broadcasted_iota(jnp.int32, (SUB, chl_out_ref.shape[1]), 0)
        chl_out_ref[0:tall, :] = upper_ref[0:tall, :]
        chl_out_ref[tall : tall + SUB, :] = jnp.where(sub < 2, upper_ref[tall : tall + SUB, :], mine_ref[0:SUB, :])
        chl_out_ref[tall + SUB :, :] = mine_ref[SUB:, :]


def call(kernel, outs, ins, specs=None, scratch=(), cost=1_000_000):
    return pl.pallas_call(
        kernel,
        out_shape=outs,
        in_specs=specs or [VMEM] * len(ins),
        out_specs=jax.tree.map(lambda _: VMEM, outs),
        scratch_shapes=list(scratch),
        compiler_params=pltpu.CompilerParams(vmem_limit_bytes=GRANT),
        cost_estimate=pl.CostEstimate(flops=cost, bytes_accessed=1_000_000, transcendentals=0),
    )(*ins)


def swaps(tiles, across):
    pairs = []
    for c in (0, 1):
        for t in range(tiles):
            other = (t + 1) % tiles if (t % 2 == 0) != across else (t - 1) % tiles
            pairs.append((c * tiles + t, c * tiles + other))
    return pairs


def over_comp(tiles):
    return [(c * tiles + t, (1 - c) * tiles + t) for c in (0, 1) for t in range(tiles)]


def sent(v, pairs):
    return lax.ppermute(v, AXES, pairs)


def per_device(ocean_fields, tracers, reaction, wet_levels, neighbours):
    tiles = lax.axis_size("tile")
    nt, lev, cols = tracers.shape
    plan = Plan(nt, lev)
    blocks, window, p_rows = plan.blocks, plan.window, plan.p_rows
    fields = ocean_fields.reshape(-1, lev, cols)
    nf = fields.shape[0]
    top, tall = SUB * (plan.full + 1), SUB * plan.full
    across, within = swaps(tiles, True), swaps(tiles, False)

    near_shapes = (
        shape_of(nt, window, SUB, cols),
        shape_of(3, window, SUB, cols),
        shape_of(2, window, SUB, cols),
        shape_of(4, blocks, SUB, cols),
        shape_of(3, blocks, SUB, cols),
        shape_of(3, blocks, SUB, cols),
    )
    h_scratch = (pltpu.VMEM((nt, (window + 2) * SUB, cols), F32), pltpu.VMEM(((window + 2) * SUB, cols), F32))
    w_scratch = (pltpu.VMEM((4, (blocks + 2) * SUB, cols), F32), pltpu.VMEM(((blocks + 2) * SUB, cols), F32))
    kernel = lambda f, *more: functools.partial(f, plan, *more)

    p, q, pq, top_fields, chl = call(
        kernel(pack_kernel),
        (
            shape_of(p_rows, cols),
            shape_of(plan.q_rows, cols),
            shape_of(p_rows + plan.q_rows, cols),
            shape_of(4, top, cols),
            shape_of(lev, cols),
        ),
        tuple(
            pltpu.with_memory_space_constraint(v, pltpu.HBM) for v in (wet_levels.reshape(1, cols), fields, tracers)
        ),
        specs=[HBM] * 3,
        scratch=[
            pltpu.VMEM((1, cols), jnp.int32),
            pltpu.VMEM((nt, SUB, cols), F32),
            pltpu.VMEM((nf, top, cols), F32),
            pltpu.SemaphoreType.DMA((6,)),
        ],
    )
    cross_p = sent(p, across)
    lagged = sent(top_fields, over_comp(tiles))
    core = sent(pq, within)
    cross_q = sent(q, across)
    n = -(-nt // 2) * 2 * SUB
    matrix, rates = call(
        matrix_kernel, (jax.ShapeDtypeStruct((2 * n, n), BF16), shape_of(nt, cols)), (reaction,)
    )

    near = call(
        kernel(near_kernel, False),
        near_shapes,
        (neighbours, fields, lagged, fields, pq, core, chl),
        cost=8_000_000,
    )
    p_one, edge = call(
        kernel(upper_kernel),
        (shape_of(p_rows, cols), shape_of(nt, SUB, cols)),
        (matrix, neighbours, pq, cross_p, *near[:3]),
        scratch=h_scratch,
        cost=8_000_000,
    )
    cross_p_one = sent(p_one, across)
    q_one, pq_one, ocean_one, over_one, rest_one = call(
        kernel(lower_kernel),
        (
            shape_of(plan.q_rows, cols),
            shape_of(p_rows + plan.q_rows, cols),
            shape_of(nf, lev, cols),
            shape_of(4, lev - tall, cols),
            shape_of(3 * (lev + tall), cols),
        ),
        (matrix, neighbours, fields, pq, cross_p, cross_q, *near, p_one, edge),
        scratch=h_scratch + w_scratch,
        cost=8_000_000,
    )
    over = sent(over_one, over_comp(tiles))
    core_one = sent(pq_one, within)
    cross_q_one = sent(q_one, across)
    rest = sent(rest_one, over_comp(tiles))

    *near, chl_one = call(
        kernel(near_kernel, True),
        near_shapes + (shape_of(lev, cols),),
        (neighbours, ocean_one, ocean_one, over, pq_one, core_one, p_one, over),
        cost=8_000_000,
    )
    upper = call(
        kernel(chl_kernel),
        shape_of(top, cols),
        (rates, neighbours, pq_one, cross_p_one, *near[:3]),
        scratch=h_scratch,
        cost=8_000_000,
    )
    upper = sent(upper, over_comp(tiles))
    ocean_two, mine = call(
        kernel(second_kernel),
        (shape_of(nf, lev, cols), shape_of(lev - tall, cols)),
        (rates, neighbours, ocean_one, pq_one, cross_p_one, cross_q_one, *near),
        scratch=h_scratch + w_scratch,
        cost=8_000_000,
    )
    ocean_out, chl_out = call(
        kernel(merge_kernel),
        (shape_of(nf, lev, cols), shape_of(lev, cols)),
        (ocean_two, over, rest, chl_one, mine, upper),
    )
    return (ocean_out[None], chl_out[None])


def solution(mesh):
    return jax.shard_map(
        per_device,
        mesh=mesh,
        in_specs=(
            P("comp", None, None, "tile"),
            P(None, None, "tile"),
            P(),
            P("tile"),
            P(None, "tile"),
        ),
        out_specs=(P("comp", None, None, "tile"), P("comp", None, "tile")),
        check_vma=False,
    )
```
